32 devices in a mesh: grp: 2 (over y), ex: 4 (over z), proj: 4 (over x, core).
Axes of the slice: x: 2, y: 2, z: 4, core: 2. Of those that a mesh axis runs over, the one named last changes fastest.
Arguments:
- inputs: bfloat16 [32, 144, 5120], P(('grp', 'ex'), None, 'proj'), parts along dimension 0, may hold values from -6 to 6
- cotangents: bfloat16 [32, 144, 5120], P(('grp', 'ex'), None, 'proj'), parts along dimension 0, may hold values from -6 to 6
- lengths: int32 [32], P(('grp', 'ex')), parts along dimension 0, may hold values from 1 to 144, 1152 in all
- adapter_down_matrix: bfloat16 [128, 5120], P(None, 'proj'), may hold values from -0.078125 to 0.078125
- adapter_up_matrix: bfloat16 [5120, 128], P('proj'), may hold values from -0.078125 to 0.078125
- width_side_sketch: bfloat16 [5120, 512], P('proj'), may hold values from -0.078125 to 0.078125
- rank_side_sketch: bfloat16 [2, 128, 8], replicated, may hold values from -0.5 to 0.5
- heldout_gradient_rows: bfloat16 [256, 8192], P(('grp', 'ex'), 'proj'), parts along dimension 0, may hold values from -20 to 20
Outputs:
- train_proj: bfloat16 [32, 8192], P(('grp', 'ex'), 'proj'), parts along dimension 0
- scores: float32 [32, 128], P(('grp', 'ex'), 'proj'), parts along dimension 0
The draws below stay inside these ranges and needn't reach their ends.
There are 2 independent parts, one for each index of `grp`. The reference program is written for one: setup_inputs(seed, part) draws one part's arguments, and reference() takes and returns one part's arrays. A program takes and returns all parts, laid end to end along the dimension named above; an argument that names none is the same for every part. Nothing has to cross between parts.
Inputs may be any that keep to these rules, and one draw needn't show every extreme that they name: The lengths of each part along grp sum to 1152.
All inputs are finite; a program needn't handle non-finite values. No bound on the sum of `lengths` on one device may be relied on, other than what follows from the above.
Results may differ from the reference program's by a relative error of at most 0.01.
Values may be sent and summed in bfloat16 or wider, within the bound.
A program may use at most 64 MiB of HBM per device.

```python
import math
import jax
import jax.numpy as jnp
import numpy as np
from jax import lax

MODEL_WIDTH = 5120
ADAPTER_RANK = 128
K1 = 512
K2 = 8
PDIM = 8192
SEQ = 144
EXAMPLES = 16
NVAL = 128


def draw_heldout_gradient_rows(key, part):
    key_base, key_rows, key_cols = jax.random.split(key, 3)
    values = jax.random.normal(key_base, (NVAL, PDIM), jnp.float32)
    values = jnp.clip(values, -4.0, 4.0)
    row_scale = jnp.exp(jax.random.uniform(key_rows, (NVAL, 1), jnp.float32, jnp.log(0.1), 0.0))
    col_scale = jnp.exp(jax.random.uniform(key_cols, (1, PDIM), jnp.float32, jnp.log(0.5), jnp.log(5.0)))
    return (values * row_scale * col_scale).astype(jnp.bfloat16)


def steps_of(rng, dims, pieces, smallest, largest):
    factor_of = 1.0
    for axis_at, parts in pieces:
        heights = jax.random.uniform(jax.random.fold_in(jax.random.fold_in(rng, 6), axis_at), (parts,), jnp.float32, smallest / len(pieces), largest / len(pieces))
        factor_of = factor_of * jnp.repeat(jnp.exp(heights), dims[axis_at] // parts).reshape((-1,) + (1,) * (len(dims) - 1 - axis_at))
    return factor_of


def split_up(number_of, total, most, skew):
    weights = [(1 << 20) // math.isqrt(rank ** skew) + 1 for rank in range(2, number_of + 1)]
    rest, holding = total - most - (number_of - 1), [1] * (number_of - 1)
    while rest > 0:
        candidates = [i for i in range(number_of - 1) if holding[i] < most]
        pool, remaining = sum([weights[i] for i in candidates]), rest
        for i in candidates:
            addition = min(most - holding[i], max(1, remaining * weights[i] // pool), rest)
            holding[i] = holding[i] + addition
            rest = rest - addition
    return np.array([most] + holding)


def uneven(rng, amount, total, bound, lean):
    if amount == 2:
        one = jax.random.randint(rng, (), max(1, total - bound), min(bound, total - 1) + 1)
        return jnp.stack([one, total - one])
    tallies = jnp.asarray(split_up(amount, total, bound, lean), jnp.int32)
    couples = (amount - 1) // 2
    giver, taker = tallies[1:1 + 2 * couples:2], tallies[2:2 + 2 * couples:2]
    room = jnp.minimum(giver - 1, bound - taker)
    passed = jax.random.randint(jax.random.fold_in(rng, 1), (couples,), 0, 1 << 20) % (room + 1)
    tallies = tallies.at[1:1 + 2 * couples:2].set(giver - passed).at[2:2 + 2 * couples:2].set(taker + passed)
    return tallies[jax.random.permutation(jax.random.fold_in(rng, 2), amount)]


def centred(stream_key, extent, width, bound, pieces=(), kind=jnp.bfloat16):
    factor_of = steps_of(stream_key, extent, pieces, -0.22, 0.18) if pieces else 1.0
    array = jax.random.normal(stream_key, extent, jnp.float32) * width * factor_of
    return jnp.minimum(jnp.maximum(array, -bound), bound).astype(kind)


def setup_inputs(seed: int = 0, part: int = 0) -> dict:
    keys = jax.random.split(jax.random.key(seed), 9)
    part_keys = jax.random.split(jax.random.fold_in(keys[8], part), 9)
    return {
        "inputs": centred(part_keys[0], (EXAMPLES, SEQ, MODEL_WIDTH), 1.0, 6.0, ((0, 4), (2, 4))),
        "cotangents": centred(part_keys[1], (EXAMPLES, SEQ, MODEL_WIDTH), 1.0, 6.0, ((0, 4), (2, 4))),
        "lengths": uneven(part_keys[2], EXAMPLES, EXAMPLES * SEQ // 2, SEQ, 2).astype(jnp.int32),
        "adapter_down_matrix": centred(keys[3], (ADAPTER_RANK, MODEL_WIDTH), MODEL_WIDTH ** -0.5, 0.078125, ((1, 4),)),
        "adapter_up_matrix": centred(keys[4], (MODEL_WIDTH, ADAPTER_RANK), MODEL_WIDTH ** -0.5, 0.078125, ((0, 4),)),
        "width_side_sketch": centred(keys[5], (MODEL_WIDTH, K1), MODEL_WIDTH ** -0.5, 0.078125, ((0, 4),)),
        "rank_side_sketch": centred(keys[6], (2, ADAPTER_RANK, K2), ADAPTER_RANK ** -0.5, 0.5),
        "heldout_gradient_rows": draw_heldout_gradient_rows(jax.random.fold_in(jax.random.fold_in(keys[8], part), 71), part),
    }


epsilon = 1e-06

def math_scale():
    return jnp.sqrt(jnp.float32(PDIM))

def reference(inputs, cotangents, lengths, adapter_down_matrix, adapter_up_matrix, width_side_sketch, rank_side_sketch, heldout_gradient_rows):
    row_count = EXAMPLES * SEQ
    flattened_input = inputs.reshape(row_count, MODEL_WIDTH)
    flattened_output = cotangents.reshape(row_count, MODEL_WIDTH)
    rank_side_input = lax.dot_general(flattened_input, adapter_down_matrix, (((1,), (1,)), ((), ())), preferred_element_type=jnp.float32).astype(jnp.bfloat16)
    rank_side_output = jnp.dot(flattened_output, adapter_up_matrix, preferred_element_type=jnp.float32).astype(jnp.bfloat16)
    left_out = jnp.dot(flattened_output, width_side_sketch, preferred_element_type=jnp.float32)
    left_in = jnp.dot(flattened_input, width_side_sketch, preferred_element_type=jnp.float32)
    right_out = jnp.dot(rank_side_input, rank_side_sketch[0], preferred_element_type=jnp.float32).astype(jnp.bfloat16)
    right_in = jnp.dot(rank_side_output, rank_side_sketch[1], preferred_element_type=jnp.float32).astype(jnp.bfloat16)
    left_rows = jnp.stack([left_out, left_in], axis=1).reshape(EXAMPLES, SEQ, 2, K1)
    right_rows = jnp.stack([right_out, right_in], axis=1).reshape(EXAMPLES, SEQ, 2, K2)
    positions = jnp.arange(SEQ, dtype=jnp.int32)
    live_mask = positions[None, :] < lengths[:, None]
    right_rows = jnp.where(live_mask[:, :, None, None], right_rows, jnp.zeros_like(right_rows))
    summed = jnp.einsum('etpk,etpq->ekpq', left_rows.astype(jnp.float32), right_rows.astype(jnp.float32))
    summed = summed / lengths.astype(jnp.float32)[:, None, None, None]
    train_proj = summed.reshape(EXAMPLES, PDIM).astype(jnp.bfloat16)
    train_f32 = train_proj.astype(jnp.float32)
    val_f32 = heldout_gradient_rows.astype(jnp.float32)
    train_sq = lax.optimization_barrier(jnp.sum(train_f32 * train_f32, axis=1))
    val_sq = lax.optimization_barrier(jnp.sum(val_f32 * val_f32, axis=1))
    dot_sums = lax.dot_general(train_proj, heldout_gradient_rows, (((1,), (1,)), ((), ())), preferred_element_type=jnp.float32)
    scores = math_scale() * dot_sums * lax.rsqrt(train_sq + epsilon)[:, None] * lax.rsqrt(val_sq + epsilon)[None, :]
    return (train_proj, scores)
```

```python
import functools
import math

import jax
import jax.numpy as jnp
from jax import lax
from jax.experimental import pallas as pl
from jax.experimental.pallas import tpu as pltpu
from jax.sharding import PartitionSpec as P

epsilon = 1e-06
MESH = pl.DeviceIdType.MESH
F32 = jnp.float32
BF16 = jnp.bfloat16
NT = (((1,), (1,)), ((), ()))


def dot(a, b, dims=(((1,), (0,)), ((), ()))):
    return lax.dot_general(a, b, dims, preferred_element_type=F32)


def kernel(
    sizes,
    len_ref, x_ref, c_ref, a_ref, b_ref, w_ref, r_ref, v_ref,
    tp_ref, sc_ref,
    xb, cb, ab, bb, wb, rows, left, gath,
    right_own, right_in, t_own, t_in, shuf, flat, sums, msg, msg_in,
    load_sem, rs_sem, rr_sem, ts_sem, tr_sem, ms_sem, mr_sem,
    gs_sem, gr_sem, own_sem,
):
    n_ex, n_proj, ex_dev, seq, pdim = sizes
    grp, me_ex, me = lax.axis_index("grp"), lax.axis_index("ex"), lax.axis_index("proj")
    k2 = r_ref.shape[1]
    pd = 2 * k2
    k1 = wb.shape[1]
    kc = k1 // n_proj
    reps = 128 // pd
    blocks = kc * pd // 128

    loads = []
    for i, (src, dst) in enumerate(
        ((a_ref, ab), (x_ref, xb), (b_ref, bb), (c_ref, cb), (w_ref, wb))
    ):
        copy = pltpu.make_async_copy(src, dst, load_sem.at[i])
        copy.start()
        loads.append(copy)
    own = pltpu.make_async_copy(v_ref, gath.at[me_ex], own_sem)
    own.start()

    def peer(k):
        return lax.rem(me + k, n_proj)

    barrier = pltpu.get_barrier_semaphore()
    for k in range(1, n_proj):
        pl.semaphore_signal(barrier, inc=1, device_id=(grp, me_ex, peer(k)), device_id_type=MESH)

    @pl.when(me_ex > 0)
    def _():
        pl.semaphore_signal(barrier, inc=1, device_id=(grp, me_ex - 1, me), device_id_type=MESH)

    @pl.when(me_ex < n_ex - 1)
    def _():
        pl.semaphore_signal(barrier, inc=1, device_id=(grp, me_ex + 1, me), device_id_type=MESH)

    sides = jnp.minimum(me_ex, 1) + jnp.minimum(n_ex - 1 - me_ex, 1)
    pl.semaphore_wait(barrier, n_proj - 1 + sides)

    chunks = gs_sem.shape[2]
    v_rows = gath.shape[1]
    part_rows = v_rows // chunks

    def hop(way, s, c, src=None):
        if way == 0:
            at, to = jnp.maximum(me_ex - s, 0), jnp.minimum(me_ex + 1, n_ex - 1)
        else:
            at, to = jnp.minimum(me_ex + s, n_ex - 1), jnp.maximum(me_ex - 1, 0)
        span = pl.ds(c * part_rows, part_rows)
        here = gath.at[at, span]
        return pltpu.make_async_remote_copy(
            src_ref=here if src is None else src.at[span],
            dst_ref=here,
            send_sem=gs_sem.at[way, s, c],
            recv_sem=gr_sem.at[way, s, c],
            device_id=(grp, to, me),
            device_id_type=MESH,
        )

    def sends(way, s):
        if way == 0:
            return (me_ex - s >= 0) & (me_ex < n_ex - 1)
        return (me_ex + s <= n_ex - 1) & (me_ex > 0)

    def receives(way, s):
        return (me_ex - 1 - s >= 0) if way == 0 else (me_ex + 1 + s <= n_ex - 1)

    def send_own():
        for way in range(2):
            @pl.when(sends(way, 0))
            def _():
                for c in range(chunks):
                    hop(way, 0, c, v_ref).start()

    def squares(at, first, count):
        held = gath[at, pl.ds(first, count)].astype(F32)
        held = held * held
        acc = held[:, :128]
        for c in range(1, gath.shape[2] // 128):
            acc = acc + held[:, c * 128:(c + 1) * 128]
        sums[pl.ds(pl.multiple_of(at * v_rows + first, part_rows), count), :] = acc

    def relay(s, c, forward=True):
        for way in range(2):
            @pl.when(receives(way, s))
            def _():
                hop(way, s, c).wait_recv()

            if forward:
                @pl.when(sends(way, s + 1))
                def _():
                    hop(way, s + 1, c).start()

            @pl.when(receives(way, s))
            def _():
                squares(me_ex - 1 - s if way == 0 else me_ex + 1 + s, c * part_rows, part_rows)

    def end_step(s):
        for way in range(2):
            @pl.when(sends(way, s))
            def _():
                for c in range(chunks):
                    hop(way, s, c).wait_send()

    send_own()

    def swap(k, src, dst, s_sem, r_sem):
        return pltpu.make_async_remote_copy(
            src_ref=src, dst_ref=dst.at[k - 1], send_sem=s_sem.at[k - 1], recv_sem=r_sem.at[k - 1],
            device_id=(grp, me_ex, peer(k)), device_id_type=MESH,
        )

    loads[0].wait()
    m_in = dot(r_ref[0], ab[...]).astype(BF16)
    loads[1].wait()
    part_in = dot(m_in, xb[...], NT)
    loads[2].wait()
    m_out = dot(r_ref[1], bb[...], NT).astype(BF16)
    loads[3].wait()
    part_out = dot(m_out, cb[...], NT)
    part = jnp.concatenate([part_in, part_out], axis=0)
    right_own[...] = part.astype(BF16)
    copies = [swap(k, right_own, right_in, rs_sem, rr_sem) for k in range(1, n_proj)]
    for copy in copies:
        copy.start()

    queue = [(t, c) for t in range(n_ex - 2) for c in range(chunks)] if n_ex <= 4 else []

    def poll():
        if queue:
            relay(*queue.pop(0))

    loads[4].wait()
    half = k1 // 2
    own.wait()
    left[0, :, :half] = dot(cb[...], wb[:, :half]).astype(BF16)
    squares(me_ex, 0, v_rows)
    poll()
    left[0, :, half:] = dot(cb[...], wb[:, half:]).astype(BF16)
    left[1, :, :half] = dot(xb[...], wb[:, :half]).astype(BF16)
    poll()
    left[1, :, half:] = dot(xb[...], wb[:, half:]).astype(BF16)

    for copy in copies:
        copy.wait()
    total = part
    for k in range(n_proj - 1):
        total = total + right_in[k].astype(F32)
    total = total.astype(BF16)

    position = lax.broadcasted_iota(jnp.int32, (k2, seq), 1)
    for e in range(ex_dev):
        live = position < len_ref[e]
        for p in range(2):
            piece = total[p * k2:(p + 1) * k2, e * seq:(e + 1) * seq].astype(F32)
            piece = jnp.where(live, piece, 0.0).astype(BF16)
            rows[e * pd + p * k2:e * pd + (p + 1) * k2, :] = dot(piece, left[p, e * seq:(e + 1) * seq, :])
    for j in range(n_proj):
        t_own[j] = rows[:, j * kc:(j + 1) * kc].astype(BF16)
    copies = [swap(k, t_own.at[peer(k)], t_in, ts_sem, tr_sem) for k in range(1, n_proj)]
    for copy in copies:
        copy.start()

    while queue:
        poll()

    mine = me * kc
    total_t = rows[:, pl.ds(pl.multiple_of(mine, 128), kc)]
    for copy in copies:
        copy.wait()
    for k in range(n_proj - 1):
        total_t = total_t + t_in[k].astype(F32)

    l_at = lax.broadcasted_iota(jnp.int32, (128, kc), 0)
    k_at = lax.broadcasted_iota(jnp.int32, (128, kc), 1)
    keep = (k_at % reps) == (l_at // pd)
    for e in range(ex_dev):
        one = total_t[e * pd:(e + 1) * pd, :] / len_ref[e].astype(F32)
        one = one.astype(BF16).astype(F32)
        tiled = jnp.concatenate([one] * reps, axis=0)
        shuf[e * 128:(e + 1) * 128, :] = jnp.where(keep, tiled, 0.0).astype(BF16)
    b_at = lax.broadcasted_iota(jnp.int32, (blocks, kc), 0)
    s_at = lax.broadcasted_iota(jnp.int32, (blocks, kc), 1)
    pick = jnp.where((s_at // reps) == b_at, 1.0, 0.0).astype(BF16)
    spread = dot(pick, shuf[...], NT)
    ep = flat.shape[0]
    flat[...] = jnp.zeros_like(flat)
    for b in range(blocks):
        for e in range(ex_dev):
            flat[e:e + 1, b * 128:(b + 1) * 128] = spread[b:b + 1, e * 128:(e + 1) * 128]
    train = flat[...]
    train_bf = train.astype(BF16)
    tp_ref[...] = train
    train_sq = jnp.sum(train * train, axis=1, keepdims=True)

    if n_ex > 4:
        @pl.loop(0, n_ex - 2)
        def _(t):
            for c in range(chunks):
                relay(t, c)

    for c in range(chunks):
        relay(n_ex - 2, c, False)
    nv = n_ex * v_rows
    per = 128 // v_rows
    cs = nv // n_proj
    ones = jnp.ones((8, 128), F32)
    dots = jnp.concatenate(
        [dot(train_bf, gath[i * per:(i + 1) * per].reshape(128, gath.shape[2]), NT) for i in range(nv // 128)],
        axis=1,
    )
    val_sq = lax.dot_general(
        ones, sums[...], NT, precision=lax.Precision.HIGHEST, preferred_element_type=F32
    )
    for j in range(n_proj):
        msg[j, :ep] = dots[:, j * cs:(j + 1) * cs]
        msg[j, ep:ep + 8] = val_sq[:, j * cs:(j + 1) * cs]
        msg[j, ep + 8:] = jnp.broadcast_to(train_sq, (ep, cs))
    copies = [swap(k, msg.at[peer(k)], msg_in, ms_sem, mr_sem) for k in range(1, n_proj)]
    for copy in copies:
        copy.start()
    for s in range(n_ex - 1):
        end_step(s)
    final = msg[me]
    for copy in copies:
        copy.wait()
    for k in range(n_proj - 1):
        final = final + msg_in[k]
    sc_ref[...] = final


def paired_kernel(
    sizes,
    len_ref, x_ref, c_ref, a_ref, b_ref, w_ref, r_ref, v_ref,
    tp_ref, sc_ref,
    xb, cb, ab, bb, wb, held, rows, right_own, right_in, t_send, t_in, shuf, flat, f_send, f_recv,
    load_sem, rs_sem, rr_sem, ts_sem, tr_sem, hs_sem, hr_sem, fs_sem, fr_sem, own_sem, ready,
):
    n_ex, n_proj, ex_dev, seq, pdim = sizes
    grp, me_ex, me = lax.axis_index("grp"), lax.axis_index("ex"), lax.axis_index("proj")
    side, core = me // 2, lax.rem(me, 2)
    home, slot = me_ex // 2, lax.rem(me_ex, 2)
    sides = n_proj // 2
    k2 = r_ref.shape[1]
    pd = 2 * k2
    kc = wb.shape[1] // n_proj
    reps = 128 // pd
    picks = kc // reps
    v_rows = v_ref.shape[0]
    ep = flat.shape[0] // (sides * picks)
    tokens = ex_dev * seq

    def peer(k):
        return lax.rem(me + k, n_proj)

    barrier = pltpu.get_barrier_semaphore()

    def greet(i, at):
        pl.semaphore_signal(barrier, inc=1, device_id=(grp, i, at), device_id_type=MESH)

    loads = []
    for i, (src, dst) in enumerate(
        ((a_ref, ab), (x_ref, xb), (b_ref, bb), (c_ref, cb), (w_ref, wb))
    ):
        copy = pltpu.make_async_copy(src, dst, load_sem.at[i])
        copy.start()
        loads.append(copy)
    for k in range(1, n_proj):
        greet(me_ex, peer(k))
    for i in range(1, n_ex):
        @pl.when(i > me_ex)
        def _():
            greet(i, home * 2 + core)
    for jj in range(2):
        @pl.when(side * 2 + jj > me_ex)
        def _():
            for s in range(sides):
                greet(side * 2 + jj, s * 2 + core)
    expected = n_proj - 1 + me_ex + sides * jnp.clip(me_ex - 2 * side, 0, 2)

    own = pltpu.make_async_copy(v_ref, held.at[side, pl.ds(slot * v_rows, v_rows)], own_sem)

    @pl.when(home == side)
    def _():
        own.start()

    def give(i):
        return pltpu.make_async_remote_copy(
            src_ref=v_ref, dst_ref=held.at[side, pl.ds(slot * v_rows, v_rows)],
            send_sem=hs_sem.at[i], recv_sem=hr_sem.at[side, slot],
            device_id=(grp, i, home * 2 + core), device_id_type=MESH,
        )

    def take(s, jj):
        block = held.at[s, pl.ds(jj * v_rows, v_rows)]
        return pltpu.make_async_remote_copy(
            src_ref=block, dst_ref=block, send_sem=hs_sem.at[0], recv_sem=hr_sem.at[s, jj],
            device_id=(grp, me_ex, me), device_id_type=MESH,
        )

    def swap(k, src, dst, s_sem, r_sem):
        return pltpu.make_async_remote_copy(
            src_ref=src, dst_ref=dst.at[k - 1], send_sem=s_sem.at[k - 1], recv_sem=r_sem.at[k - 1],
            device_id=(grp, me_ex, peer(k)), device_id_type=MESH,
        )

    @pl.when(me_ex > 0)
    def _():
        pl.semaphore_wait(barrier, expected)
        for jj in range(2):
            @pl.when(side * 2 + jj < me_ex)
            def _():
                for s in range(sides):
                    pl.semaphore_signal(
                        ready.at[me_ex], inc=1,
                        device_id=(grp, side * 2 + jj, s * 2 + core), device_id_type=MESH,
                    )

    flat[...] = jnp.zeros_like(flat)
    loads[0].wait()
    m_in = dot(r_ref[0], ab[...]).astype(BF16)
    loads[1].wait()
    part_in = dot(m_in, xb[...], NT)
    loads[2].wait()
    m_out = dot(r_ref[1], bb[...], NT).astype(BF16)
    loads[3].wait()
    part_out = dot(m_out, cb[...], NT)
    part = jnp.concatenate([part_in, part_out], axis=0)
    right_own[...] = part.astype(BF16)

    @pl.when(me_ex == 0)
    def _():
        pl.semaphore_wait(barrier, expected)

    moves = [swap(k, right_own, right_in, rs_sem, rr_sem) for k in range(1, n_proj)]
    for move in moves:
        move.start()
    for i in range(n_ex):
        @pl.when((i < me_ex) | ((i == me_ex) & (home != side)))
        def _():
            give(i).start()

    def give_later(k):
        for i in range(k, n_ex):
            @pl.when(i == me_ex + k)
            def _():
                pl.semaphore_wait(ready.at[i], 1)
                give(i).start()

    give_later(1)

    position = lax.broadcasted_iota(jnp.int32, (k2, tokens), 1)
    live = []
    scale = []
    for e in range(ex_dev):
        count = len_ref[e]
        live.append((position >= e * seq) & (position < e * seq + count))
        scale.append(1.0 / jnp.full((k2, 128), count.astype(F32), F32))

    total = part
    for k, move in enumerate(moves):
        move.wait_recv()
        total = total + right_in[k].astype(F32)
    total = total.astype(BF16).astype(F32)
    grown = []
    for p, other in enumerate((cb, xb)):
        piece = total[p * k2:(p + 1) * k2]
        spread = jnp.concatenate([jnp.where(one, piece, 0.0) for one in live], axis=0).astype(BF16)
        grown.append(dot(spread, other[...]))
    loads[4].wait()
    result = dot(jnp.concatenate(grown, axis=0).astype(BF16), wb[...])
    for p in range(2):
        for e in range(ex_dev):
            at = (p * ex_dev + e) * k2
            for q in range(n_proj):
                rows[at:at + k2, q * kc:(q + 1) * kc] = result[at:at + k2, q * kc:(q + 1) * kc] * scale[e]
    for q in range(n_proj):
        t_send[q % 2, q // 2] = rows[:, q * kc:(q + 1) * kc].astype(BF16)
    shares = [
        swap(k, t_send.at[lax.rem(peer(k), 2)], t_in, ts_sem, tr_sem) for k in range(1, n_proj)
    ]
    for share in shares:
        share.start()
    for k in range(2, n_ex):
        give_later(k)

    l_at = lax.broadcasted_iota(jnp.int32, (128, kc), 0)
    k_at = lax.broadcasted_iota(jnp.int32, (128, kc), 1)
    keep = (k_at % reps) == (l_at // pd)
    b_at = lax.broadcasted_iota(jnp.int32, (picks, kc), 0)
    s_at = lax.broadcasted_iota(jnp.int32, (picks, kc), 1)
    pick = jnp.where((s_at // reps) == b_at, 1.0, 0.0).astype(BF16)

    for s in range(sides):
        for jj in range(2):
            mine = (side * 2 + jj == me_ex) & (side == s)

            @pl.when(mine)
            def _():
                own.wait()

            @pl.when(jnp.logical_not(mine))
            def _():
                take(s, jj).wait_recv()
    acc = jnp.zeros((2 * v_rows, 128), F32)
    for s in range(sides):
        for c in range(v_ref.shape[1] // 128):
            wide = held[s, :, c * 128:(c + 1) * 128].astype(F32)
            acc = acc + wide * wide
    val_sq = lax.dot_general(
        jnp.ones((ep, 128), F32), acc, NT, precision=lax.Precision.HIGHEST, preferred_element_type=F32
    )

    for share in shares:
        share.wait_recv()
    for s in range(sides):
        block = rows[:, pl.ds(pl.multiple_of((s * 2 + core) * kc, 128), kc)]
        for k in range(n_proj - 1):
            block = block + t_in[k, s].astype(F32)
        block = block.astype(BF16).astype(F32)
        for e in range(ex_dev):
            one = [block[(p * ex_dev + e) * k2:(p * ex_dev + e + 1) * k2] for p in range(2)]
            tiled = jnp.where(keep, jnp.concatenate(one * reps, axis=0), 0.0)
            shuf[(s * ex_dev + e) * 128:(s * ex_dev + e + 1) * 128, :] = tiled.astype(BF16)
    spread = dot(pick, shuf[...], NT)
    for s in range(sides):
        for e in range(ex_dev):
            flat[pl.ds(s * picks * ep + e, picks, stride=ep), :] = (
                spread[:, (s * ex_dev + e) * 128:(s * ex_dev + e + 1) * 128]
            )
    dots = jnp.zeros((ep, 2 * v_rows), F32)
    train_sq = jnp.zeros((ep, 128), F32)
    for s in range(sides):
        tiles = [flat[(s * picks + b) * ep:(s * picks + b + 1) * ep, :] for b in range(picks)]
        for tile in tiles:
            train_sq = train_sq + tile * tile
        dots = dots + dot(jnp.concatenate(tiles, axis=1).astype(BF16), held[s], NT)
    train_sq = jnp.sum(train_sq, axis=1, keepdims=True)
    for jj in range(2):
        span = slice(jj * v_rows, (jj + 1) * v_rows)
        f_send[jj] = jnp.concatenate(
            [dots[:, span], val_sq[:, span], jnp.broadcast_to(train_sq, (ep, 128 - 2 * v_rows))], axis=1
        )
    last = pltpu.make_async_remote_copy(
        src_ref=f_send.at[1 - core], dst_ref=f_recv, send_sem=fs_sem, recv_sem=fr_sem,
        device_id=(grp, me_ex, side * 2 + 1 - core), device_id_type=MESH,
    )
    last.start()

    for b in range(picks):
        tp_ref[:, b * 128:(b + 1) * 128] = flat[pl.ds(pl.multiple_of((side * picks + b) * ep, 8), ep), :]
    for move in moves + shares:
        move.wait_send()
    for i in range(n_ex):
        @pl.when((i != me_ex) | (home != side))
        def _():
            give(i).wait_send()
    final = f_send[core]
    last.wait()
    sc_ref[...] = final + f_recv[...]


def paired_finish(pdim, train_ref, sums_ref, tp_ref, sc_ref):
    ex_dev, cs = sc_ref.shape
    tp_ref[...] = train_ref[:ex_dev, :].astype(BF16)
    final = sums_ref[:ex_dev, :]
    sc_ref[...] = (
        math.sqrt(pdim)
        * final[:, :cs]
        * lax.rsqrt(final[:, 2 * cs:3 * cs] + epsilon)
        * lax.rsqrt(final[:, cs:2 * cs] + epsilon)
    )


def finish(pdim, train_ref, sums_ref, tp_ref, sc_ref):
    ex_dev = tp_ref.shape[0]
    ep = train_ref.shape[0]
    tp_ref[...] = train_ref[:ex_dev, :].astype(BF16)
    final = sums_ref[...]
    scores = (
        math.sqrt(pdim)
        * final[:ep]
        * lax.rsqrt(final[ep + 8:] + epsilon)
        * lax.rsqrt(final[ep:ep + 1] + epsilon)
    )
    sc_ref[...] = scores[:ex_dev]


def shards(
    mesh, inputs, cotangents, lengths, adapter_down_matrix, adapter_up_matrix,
    width_side_sketch, rank_side_sketch, heldout_gradient_rows,
):
    n_ex, n_proj = mesh.shape["ex"], mesh.shape["proj"]
    ex_dev, seq, cols = inputs.shape
    tokens = ex_dev * seq
    rank = adapter_down_matrix.shape[0]
    k1 = width_side_sketch.shape[1]
    k2 = rank_side_sketch.shape[2]
    pd = 2 * k2
    kc = k1 // n_proj
    v_rows, v_cols = heldout_gradient_rows.shape
    nv = v_rows * n_ex
    cs = nv // n_proj
    ep = -(-ex_dev // 8) * 8
    pdim = pd * k1
    any_space = pl.BlockSpec(memory_space=pltpu.HBM)
    vmem = pl.BlockSpec(memory_space=pltpu.VMEM)
    dma = pltpu.SemaphoreType.DMA
    peers = n_proj - 1
    sides = n_proj // 2
    paired = (
        n_ex == n_proj and n_proj % 2 == 0 and kc == 128 and 3 * v_rows <= 128 and v_rows % 16 == 0
        and k2 == 8 and ex_dev <= ep and v_cols == kc * pd
    )
    head = [
        pltpu.VMEM((tokens, cols), BF16),
        pltpu.VMEM((tokens, cols), BF16),
        pltpu.VMEM((rank, cols), BF16),
        pltpu.VMEM((cols, rank), BF16),
        pltpu.VMEM((cols, k1), BF16),
    ]
    if paired:
        body, end = paired_kernel, paired_finish
        sums_shape = (ep, 128)
        picks = kc * pd // 128
        scratch = head + [
            pltpu.VMEM((sides, 2 * v_rows, v_cols), BF16),
            pltpu.VMEM((ex_dev * pd, k1), F32),
            pltpu.VMEM((pd, tokens), BF16),
            pltpu.VMEM((peers, pd, tokens), BF16),
            pltpu.VMEM((2, sides, ex_dev * pd, kc), BF16),
            pltpu.VMEM((peers, sides, ex_dev * pd, kc), BF16),
            pltpu.VMEM((sides * ex_dev * 128, kc), BF16),
            pltpu.VMEM((sides * picks * ep, 128), F32),
            pltpu.VMEM((2, ep, 128), F32),
            pltpu.VMEM((ep, 128), F32),
            dma((5,)),
            dma((peers,)), dma((peers,)),
            dma((peers,)), dma((peers,)),
            dma((n_ex,)), dma((sides, 2)),
            dma, dma, dma,
            pltpu.SemaphoreType.REGULAR((n_ex,)),
        ]
    else:
        chunks = 2 if v_rows % 32 == 0 else 1
        body, end = kernel, finish
        sums_shape = (2 * ep + 8, cs)
        scratch = head + [
            pltpu.VMEM((ex_dev * pd, k1), F32),
            pltpu.VMEM((2, tokens, k1), BF16),
            pltpu.VMEM((n_ex, v_rows, v_cols), BF16),
            pltpu.VMEM((pd, tokens), BF16),
            pltpu.VMEM((peers, pd, tokens), BF16),
            pltpu.VMEM((n_proj, ex_dev * pd, kc), BF16),
            pltpu.VMEM((peers, ex_dev * pd, kc), BF16),
            pltpu.VMEM((ex_dev * 128, kc), BF16),
            pltpu.VMEM((ep, v_cols), F32),
            pltpu.VMEM((nv, 128), F32),
            pltpu.VMEM((n_proj, 2 * ep + 8, cs), F32),
            pltpu.VMEM((peers, 2 * ep + 8, cs), F32),
            dma((5,)),
            dma((peers,)), dma((peers,)),
            dma((peers,)), dma((peers,)),
            dma((peers,)), dma((peers,)),
            dma((2, n_ex - 1, chunks)), dma((2, n_ex - 1, chunks)),
            dma,
        ]
    train, final = pl.pallas_call(
        functools.partial(body, (n_ex, n_proj, ex_dev, seq, pdim)),
        out_shape=(
            pltpu.VMEM((ep, v_cols), F32),
            pltpu.VMEM(sums_shape, F32),
        ),
        in_specs=[pl.BlockSpec(memory_space=pltpu.SMEM)] + [any_space] * 5 + [vmem, any_space],
        out_specs=(vmem, vmem),
        scratch_shapes=scratch,
        compiler_params=pltpu.CompilerParams(
            collective_id=0, has_side_effects=True, vmem_limit_bytes=62 * 1024 * 1024
        ),
        name="project",
    )(
        lengths, inputs.reshape(tokens, cols), cotangents.reshape(tokens, cols),
        adapter_down_matrix, adapter_up_matrix, width_side_sketch,
        rank_side_sketch.swapaxes(1, 2), heldout_gradient_rows,
    )
    return pl.pallas_call(
        functools.partial(end, pdim),
        out_shape=(
            jax.ShapeDtypeStruct((ex_dev, v_cols), BF16),
            jax.ShapeDtypeStruct((ex_dev, cs), F32),
        ),
        in_specs=[vmem, vmem],
        out_specs=(vmem, vmem),
        compiler_params=pltpu.CompilerParams(vmem_limit_bytes=8 * 1024 * 1024),
        name="finish",
    )(train, final)


def solution(mesh):
    in_specs = (
        P(("grp", "ex"), None, "proj"),
        P(("grp", "ex"), None, "proj"),
        P(("grp", "ex")),
        P(None, "proj"),
        P("proj", None),
        P("proj", None),
        P(),
        P(("grp", "ex"), "proj"),
    )
    out_specs = (P(("grp", "ex"), "proj"), P(("grp", "ex"), "proj"))
    return jax.shard_map(
        functools.partial(shards, mesh), mesh=mesh, in_specs=in_specs, out_specs=out_specs, check_vma=False
    )
```

```python
import functools
import math

import jax
import jax.numpy as jnp
from jax import lax
from jax.experimental import pallas as pl
from jax.experimental.pallas import tpu as pltpu
from jax.sharding import PartitionSpec as P

epsilon = 1e-06
MESH = pl.DeviceIdType.MESH
F32 = jnp.float32
BF16 = jnp.bfloat16
NT = (((1,), (1,)), ((), ()))


def dot(a, b, dims=(((1,), (0,)), ((), ()))):
    return lax.dot_general(a, b, dims, preferred_element_type=F32)


def kernel(
    sizes,
    len_ref, x_ref, c_ref, a_ref, b_ref, w_ref, r_ref, v_ref,
    tp_ref, sc_ref,
    xb, cb, ab, bb, wb, rows, left, gath,
    right_own, right_in, t_own, t_in, shuf, flat, sums, msg, msg_in,
    load_sem, rs_sem, rr_sem, ts_sem, tr_sem, ms_sem, mr_sem,
    gs_sem, gr_sem, own_sem,
):
    n_ex, n_proj, ex_dev, seq, pdim = sizes
    grp, me_ex, me = lax.axis_index("grp"), lax.axis_index("ex"), lax.axis_index("proj")
    k2 = r_ref.shape[1]
    pd = 2 * k2
    k1 = wb.shape[1]
    kc = k1 // n_proj
    reps = 128 // pd
    blocks = kc * pd // 128

    loads = []
    for i, (src, dst) in enumerate(
        ((a_ref, ab), (x_ref, xb), (b_ref, bb), (c_ref, cb), (w_ref, wb))
    ):
        copy = pltpu.make_async_copy(src, dst, load_sem.at[i])
        copy.start()
        loads.append(copy)
    own = pltpu.make_async_copy(v_ref, gath.at[me_ex], own_sem)
    own.start()

    def peer(k):
        return lax.rem(me + k, n_proj)

    barrier = pltpu.get_barrier_semaphore()
    for k in range(1, n_proj):
        pl.semaphore_signal(barrier, inc=1, device_id=(grp, me_ex, peer(k)), device_id_type=MESH)

    @pl.when(me_ex > 0)
    def _():
        pl.semaphore_signal(barrier, inc=1, device_id=(grp, me_ex - 1, me), device_id_type=MESH)

    @pl.when(me_ex < n_ex - 1)
    def _():
        pl.semaphore_signal(barrier, inc=1, device_id=(grp, me_ex + 1, me), device_id_type=MESH)

    sides = jnp.minimum(me_ex, 1) + jnp.minimum(n_ex - 1 - me_ex, 1)
    pl.semaphore_wait(barrier, n_proj - 1 + sides)

    chunks = gs_sem.shape[2]
    v_rows = gath.shape[1]
    part_rows = v_rows // chunks

    def hop(way, s, c, src=None):
        if way == 0:
            at, to = jnp.maximum(me_ex - s, 0), jnp.minimum(me_ex + 1, n_ex - 1)
        else:
            at, to = jnp.minimum(me_ex + s, n_ex - 1), jnp.maximum(me_ex - 1, 0)
        span = pl.ds(c * part_rows, part_rows)
        here = gath.at[at, span]
        return pltpu.make_async_remote_copy(
            src_ref=here if src is None else src.at[span],
            dst_ref=here,
            send_sem=gs_sem.at[way, s, c],
            recv_sem=gr_sem.at[way, s, c],
            device_id=(grp, to, me),
            device_id_type=MESH,
        )

    def sends(way, s):
        if way == 0:
            return (me_ex - s >= 0) & (me_ex < n_ex - 1)
        return (me_ex + s <= n_ex - 1) & (me_ex > 0)

    def receives(way, s):
        return (me_ex - 1 - s >= 0) if way == 0 else (me_ex + 1 + s <= n_ex - 1)

    def send_own():
        for way in range(2):
            @pl.when(sends(way, 0))
            def _():
                for c in range(chunks):
                    hop(way, 0, c, v_ref).start()

    def squares(at, first, count):
        held = gath[at, pl.ds(first, count)].astype(F32)
        held = held * held
        acc = held[:, :128]
        for c in range(1, gath.shape[2] // 128):
            acc = acc + held[:, c * 128:(c + 1) * 128]
        sums[pl.ds(pl.multiple_of(at * v_rows + first, part_rows), count), :] = acc

    def relay(s, c, forward=True):
        for way in range(2):
            @pl.when(receives(way, s))
            def _():
                hop(way, s, c).wait_recv()

            if forward:
                @pl.when(sends(way, s + 1))
                def _():
                    hop(way, s + 1, c).start()

            @pl.when(receives(way, s))
            def _():
                squares(me_ex - 1 - s if way == 0 else me_ex + 1 + s, c * part_rows, part_rows)

    def end_step(s):
        for way in range(2):
            @pl.when(sends(way, s))
            def _():
                for c in range(chunks):
                    hop(way, s, c).wait_send()

    send_own()

    def swap(k, src, dst, s_sem, r_sem):
        return pltpu.make_async_remote_copy(
            src_ref=src, dst_ref=dst.at[k - 1], send_sem=s_sem.at[k - 1], recv_sem=r_sem.at[k - 1],
            device_id=(grp, me_ex, peer(k)), device_id_type=MESH,
        )

    loads[0].wait()
    m_in = dot(r_ref[0], ab[...]).astype(BF16)
    loads[1].wait()
    part_in = dot(m_in, xb[...], NT)
    loads[2].wait()
    m_out = dot(r_ref[1], bb[...], NT).astype(BF16)
    loads[3].wait()
    part_out = dot(m_out, cb[...], NT)
    part = jnp.concatenate([part_in, part_out], axis=0)
    right_own[...] = part.astype(BF16)
    copies = [swap(k, right_own, right_in, rs_sem, rr_sem) for k in range(1, n_proj)]
    for copy in copies:
        copy.start()

    queue = [(t, c) for t in range(n_ex - 2) for c in range(chunks)] if n_ex <= 4 else []

    def poll():
        if queue:
            relay(*queue.pop(0))

    loads[4].wait()
    half = k1 // 2
    own.wait()
    left[0, :, :half] = dot(cb[...], wb[:, :half]).astype(BF16)
    squares(me_ex, 0, v_rows)
    poll()
    left[0, :, half:] = dot(cb[...], wb[:, half:]).astype(BF16)
    left[1, :, :half] = dot(xb[...], wb[:, :half]).astype(BF16)
    poll()
    left[1, :, half:] = dot(xb[...], wb[:, half:]).astype(BF16)

    for copy in copies:
        copy.wait()
    total = part
    for k in range(n_proj - 1):
        total = total + right_in[k].astype(F32)
    total = total.astype(BF16)

    position = lax.broadcasted_iota(jnp.int32, (k2, seq), 1)
    for e in range(ex_dev):
        live = position < len_ref[e]
        for p in range(2):
            piece = total[p * k2:(p + 1) * k2, e * seq:(e + 1) * seq].astype(F32)
            piece = jnp.where(live, piece, 0.0).astype(BF16)
            rows[e * pd + p * k2:e * pd + (p + 1) * k2, :] = dot(piece, left[p, e * seq:(e + 1) * seq, :])
    for j in range(n_proj):
        t_own[j] = rows[:, j * kc:(j + 1) * kc].astype(BF16)
    copies = [swap(k, t_own.at[peer(k)], t_in, ts_sem, tr_sem) for k in range(1, n_proj)]
    for copy in copies:
        copy.start()

    while queue:
        poll()

    mine = me * kc
    total_t = rows[:, pl.ds(pl.multiple_of(mine, 128), kc)]
    for copy in copies:
        copy.wait()
    for k in range(n_proj - 1):
        total_t = total_t + t_in[k].astype(F32)

    l_at = lax.broadcasted_iota(jnp.int32, (128, kc), 0)
    k_at = lax.broadcasted_iota(jnp.int32, (128, kc), 1)
    keep = (k_at % reps) == (l_at // pd)
    for e in range(ex_dev):
        one = total_t[e * pd:(e + 1) * pd, :] / len_ref[e].astype(F32)
        one = one.astype(BF16).astype(F32)
        tiled = jnp.concatenate([one] * reps, axis=0)
        shuf[e * 128:(e + 1) * 128, :] = jnp.where(keep, tiled, 0.0).astype(BF16)
    b_at = lax.broadcasted_iota(jnp.int32, (blocks, kc), 0)
    s_at = lax.broadcasted_iota(jnp.int32, (blocks, kc), 1)
    pick = jnp.where((s_at // reps) == b_at, 1.0, 0.0).astype(BF16)
    spread = dot(pick, shuf[...], NT)
    ep = flat.shape[0]
    flat[...] = jnp.zeros_like(flat)
    for b in range(blocks):
        for e in range(ex_dev):
            flat[e:e + 1, b * 128:(b + 1) * 128] = spread[b:b + 1, e * 128:(e + 1) * 128]
    train = flat[...]
    train_bf = train.astype(BF16)
    tp_ref[...] = train
    train_sq = jnp.sum(train * train, axis=1, keepdims=True)

    if n_ex > 4:
        @pl.loop(0, n_ex - 2)
        def _(t):
            for c in range(chunks):
                relay(t, c)

    for c in range(chunks):
        relay(n_ex - 2, c, False)
    nv = n_ex * v_rows
    per = 128 // v_rows
    cs = nv // n_proj
    ones = jnp.ones((8, 128), F32)
    dots = jnp.concatenate(
        [dot(train_bf, gath[i * per:(i + 1) * per].reshape(128, gath.shape[2]), NT) for i in range(nv // 128)],
        axis=1,
    )
    val_sq = lax.dot_general(
        ones, sums[...], NT, precision=lax.Precision.HIGHEST, preferred_element_type=F32
    )
    for j in range(n_proj):
        msg[j, :ep] = dots[:, j * cs:(j + 1) * cs]
        msg[j, ep:ep + 8] = val_sq[:, j * cs:(j + 1) * cs]
        msg[j, ep + 8:] = jnp.broadcast_to(train_sq, (ep, cs))
    copies = [swap(k, msg.at[peer(k)], msg_in, ms_sem, mr_sem) for k in range(1, n_proj)]
    for copy in copies:
        copy.start()
    for s in range(n_ex - 1):
        end_step(s)
    final = msg[me]
    for copy in copies:
        copy.wait()
    for k in range(n_proj - 1):
        final = final + msg_in[k]
    sc_ref[...] = final


def paired_kernel(
    sizes,
    len_hbm, x_ref, c_ref, a_ref, b_ref, w_ref, r_hbm, v_ref,
    tp_ref, sc_ref,
    xb, cb, ab, bb, wb, r_ref, len_ref, held, rows, right_own, right_in, t_send, t_in, t_mate, shuf, flat, f_send, f_recv,
    load_sem, rs_sem, rr_sem, ts_sem, tr_sem, us_sem, ur_sem, hs_sem, hr_sem, fs_sem, fr_sem, own_sem, ready, met,
):
    n_ex, n_proj, ex_dev, seq, pdim = sizes
    grp, me_ex, me = lax.axis_index("grp"), lax.axis_index("ex"), lax.axis_index("proj")
    flank = lax.rem(me_ex, 2)
    mate = me_ex + 1 - 2 * flank
    per = n_ex // 2
    home, slot = me_ex // per, lax.rem(me_ex, per)
    k2 = r_ref.shape[1]
    pd = 2 * k2
    kc = wb.shape[1] // n_proj
    reps = 128 // pd
    picks = kc // reps
    v_rows = v_ref.shape[0]
    ep = flat.shape[1] // picks
    tokens = ex_dev * seq

    def peer(k):
        return lax.rem(me + k, n_proj)

    barrier = pltpu.get_barrier_semaphore()

    def greet(i, at):
        pl.semaphore_signal(barrier, inc=1, device_id=(grp, i, at), device_id_type=MESH)

    loads = []
    for i, (src, dst) in enumerate(
        ((r_hbm, r_ref), (a_ref, ab), (x_ref, xb), (b_ref, bb), (c_ref, cb), (w_ref, wb), (len_hbm, len_ref))
    ):
        copy = pltpu.make_async_copy(src, dst, load_sem.at[i])
        copy.start()
        loads.append(copy)
    for k in range(1, n_proj):
        greet(me_ex, peer(k))
    for i in range(1, n_ex):
        @pl.when(i > me_ex)
        def _():
            greet(i, me)

    @pl.when(flank == 0)
    def _():
        for k in range(1, n_proj):
            greet(mate, peer(k))
    expected = n_proj - 1 + me_ex + flank * (n_proj - 1)

    def place(jj):
        return held.at[pl.ds(jj * v_rows, v_rows)]

    own = pltpu.make_async_copy(v_ref, place(slot), own_sem)

    @pl.when(home == flank)
    def _():
        own.start()

    def give(i):
        return pltpu.make_async_remote_copy(
            src_ref=v_ref, dst_ref=place(slot), send_sem=hs_sem.at[i], recv_sem=hr_sem.at[slot],
            device_id=(grp, i, me), device_id_type=MESH,
        )

    def take(jj):
        return pltpu.make_async_remote_copy(
            src_ref=place(jj), dst_ref=place(jj), send_sem=hs_sem.at[0], recv_sem=hr_sem.at[jj],
            device_id=(grp, me_ex, me), device_id_type=MESH,
        )

    def pass_on(k, src, dst, s_sem, r_sem):
        return pltpu.make_async_remote_copy(
            src_ref=src, dst_ref=dst.at[k], send_sem=s_sem.at[k], recv_sem=r_sem.at[k],
            device_id=(grp, mate, peer(k)), device_id_type=MESH,
        )

    def swap(k, src, dst, s_sem, r_sem):
        return pltpu.make_async_remote_copy(
            src_ref=src, dst_ref=dst.at[k - 1], send_sem=s_sem.at[k - 1], recv_sem=r_sem.at[k - 1],
            device_id=(grp, me_ex, peer(k)), device_id_type=MESH,
        )

    @pl.when(me_ex > 0)
    def _():
        pl.semaphore_wait(barrier, expected)
        for j in range(n_ex - 1):
            @pl.when((j < me_ex) & (j // per == flank))
            def _():
                pl.semaphore_signal(
                    ready.at[me_ex], inc=1, device_id=(grp, j, me), device_id_type=MESH
                )

        @pl.when(flank == 1)
        def _():
            for k in range(n_proj):
                pl.semaphore_signal(
                    met, inc=1, device_id=(grp, mate, peer(k)), device_id_type=MESH
                )

    flat[...] = jnp.zeros_like(flat)
    loads[0].wait()
    loads[1].wait()
    m_in = dot(r_ref[0], ab[...]).astype(BF16)
    loads[2].wait()
    part_in = dot(m_in, xb[...], NT)
    loads[3].wait()
    m_out = dot(r_ref[1], bb[...], NT).astype(BF16)
    loads[4].wait()
    part_out = dot(m_out, cb[...], NT)
    part = jnp.concatenate([part_in, part_out], axis=0)
    right_own[...] = part.astype(BF16)

    @pl.when(me_ex == 0)
    def _():
        pl.semaphore_wait(barrier, expected)

    moves = [swap(k, right_own, right_in, rs_sem, rr_sem) for k in range(1, n_proj)]
    for move in moves:
        move.start()
    for i in range(n_ex - 1):
        @pl.when((i < me_ex) & (i % 2 == home))
        def _():
            give(i).start()

    def give_later(k):
        for i in range(k, n_ex):
            @pl.when((i == me_ex + k) & (i % 2 == home))
            def _():
                pl.semaphore_wait(ready.at[i], 1)
                give(i).start()

    give_later(1)

    loads[6].wait()
    position = lax.broadcasted_iota(jnp.int32, (k2, tokens), 1)
    live = []
    scale = []
    for e in range(ex_dev):
        count = len_ref[e]
        live.append((position >= e * seq) & (position < e * seq + count))
        scale.append(1.0 / jnp.full((k2, 128), count.astype(F32), F32))

    total = part
    for k, move in enumerate(moves):
        move.wait_recv()
        total = total + right_in[k].astype(F32)
    total = total.astype(BF16).astype(F32)
    grown = []
    for p, other in enumerate((cb, xb)):
        piece = total[p * k2:(p + 1) * k2]
        spread = jnp.concatenate([jnp.where(one, piece, 0.0) for one in live], axis=0).astype(BF16)
        grown.append(dot(spread, other[...]))
    loads[5].wait()
    result = dot(jnp.concatenate(grown, axis=0).astype(BF16), wb[...])
    for p in range(2):
        for e in range(ex_dev):
            at = (p * ex_dev + e) * k2
            for q in range(n_proj):
                rows[at:at + k2, q * kc:(q + 1) * kc] = result[at:at + k2, q * kc:(q + 1) * kc] * scale[e]
    for q in range(n_proj):
        t_send[q] = rows[:, q * kc:(q + 1) * kc].astype(BF16)
    shares = [swap(k, t_send.at[peer(k)], t_in, ts_sem, tr_sem) for k in range(1, n_proj)]
    for share in shares:
        share.start()

    @pl.when(flank == 0)
    def _():
        pl.semaphore_wait(met, n_proj)

    across = [pass_on(k, t_send.at[peer(k)], t_mate, us_sem, ur_sem) for k in range(n_proj)]
    for share in across:
        share.start()
    for k in range(2, n_ex):
        give_later(k)

    l_at = lax.broadcasted_iota(jnp.int32, (128, kc), 0)
    k_at = lax.broadcasted_iota(jnp.int32, (128, kc), 1)
    keep = (k_at % reps) == (l_at // pd)
    b_at = lax.broadcasted_iota(jnp.int32, (picks, kc), 0)
    s_at = lax.broadcasted_iota(jnp.int32, (picks, kc), 1)
    pick = jnp.where((s_at // reps) == b_at, 1.0, 0.0).astype(BF16)

    for jj in range(per):
        @pl.when(flank * per + jj == me_ex)
        def _():
            own.wait()

        @pl.when(flank * per + jj != me_ex)
        def _():
            take(jj).wait_recv()
    acc = jnp.zeros((per * v_rows, 128), F32)
    for c in range(v_ref.shape[1] // 128):
        wide = held[:, c * 128:(c + 1) * 128].astype(F32)
        acc = acc + wide * wide
    val_sq = lax.dot_general(
        jnp.ones((ep, 128), F32), acc, NT, precision=lax.Precision.HIGHEST, preferred_element_type=F32
    )

    def score(w, block):
        block = block.astype(BF16).astype(F32)
        for e in range(ex_dev):
            one = [block[(p * ex_dev + e) * k2:(p * ex_dev + e + 1) * k2] for p in range(2)]
            tiled = jnp.where(keep, jnp.concatenate(one * reps, axis=0), 0.0)
            shuf[w, e * 128:(e + 1) * 128, :] = tiled.astype(BF16)
        spread = dot(pick, shuf[w], NT)
        for e in range(ex_dev):
            flat[w, pl.ds(e, picks, stride=ep), :] = spread[:, e * 128:(e + 1) * 128]
        tiles = [flat[w, b * ep:(b + 1) * ep, :] for b in range(picks)]
        train_sq = jnp.zeros((ep, 128), F32)
        for tile in tiles:
            train_sq = train_sq + tile * tile
        train_sq = jnp.sum(train_sq, axis=1, keepdims=True)
        train = jnp.concatenate(tiles, axis=1)
        dots = dot(train.astype(BF16), held[...], NT)
        for jj in range(per):
            span = slice(jj * v_rows, (jj + 1) * v_rows)
            f_send[w, jj] = jnp.concatenate(
                [dots[:, span], val_sq[:, span], jnp.broadcast_to(train_sq, (ep, 128 - 2 * v_rows))],
                axis=1,
            )
        return train

    def report(w, jj):
        return pltpu.make_async_remote_copy(
            src_ref=f_send.at[w, jj], dst_ref=f_recv.at[me], send_sem=fs_sem.at[w, jj], recv_sem=fr_sem.at[me],
            device_id=(grp, mate if w else me_ex, flank * per + jj), device_id_type=MESH,
        )

    def hear(q):
        return pltpu.make_async_remote_copy(
            src_ref=f_recv.at[q], dst_ref=f_recv.at[q], send_sem=fs_sem.at[0, 0], recv_sem=fr_sem.at[q],
            device_id=(grp, me_ex, me), device_id_type=MESH,
        )

    block = rows[:, pl.ds(pl.multiple_of(me * kc, 128), kc)]
    for k, share in enumerate(shares):
        share.wait_recv()
        block = block + t_in[k].astype(F32)
    train = score(0, block)
    for jj in range(per):
        @pl.when(me != flank * per + jj)
        def _():
            report(0, jj).start()

        @pl.when(me == flank * per + jj)
        def _():
            f_recv[me] = f_send[0, jj]
    block = jnp.zeros((ex_dev * pd, kc), F32)
    for k, share in enumerate(across):
        share.wait_recv()
        block = block + t_mate[k].astype(F32)
    score(1, block)
    for jj in range(per):
        report(1, jj).start()

    tp_ref[...] = train
    for move in moves + shares + across:
        move.wait_send()
    for i in range(n_ex):
        @pl.when((i != me_ex) & (i % 2 == home))
        def _():
            give(i).wait_send()
    for q in range(n_proj):
        @pl.when((me // per != flank) | (me != q))
        def _():
            hear(q).wait_recv()
    final = f_recv[0]
    for q in range(1, n_proj):
        final = final + f_recv[q]
    sc_ref[...] = final
    for jj in range(per):
        @pl.when(me != flank * per + jj)
        def _():
            report(0, jj).wait_send()

        report(1, jj).wait_send()


def paired_finish(pdim, train_ref, sums_ref, tp_ref, sc_ref):
    ex_dev, cs = sc_ref.shape
    tp_ref[...] = train_ref[:ex_dev, :].astype(BF16)
    final = sums_ref[:ex_dev, :]
    sc_ref[...] = (
        math.sqrt(pdim)
        * final[:, :cs]
        * lax.rsqrt(final[:, 2 * cs:3 * cs] + epsilon)
        * lax.rsqrt(final[:, cs:2 * cs] + epsilon)
    )


def finish(pdim, train_ref, sums_ref, tp_ref, sc_ref):
    ex_dev = tp_ref.shape[0]
    ep = train_ref.shape[0]
    tp_ref[...] = train_ref[:ex_dev, :].astype(BF16)
    final = sums_ref[...]
    scores = (
        math.sqrt(pdim)
        * final[:ep]
        * lax.rsqrt(final[ep + 8:] + epsilon)
        * lax.rsqrt(final[ep:ep + 1] + epsilon)
    )
    sc_ref[...] = scores[:ex_dev]


def shards(
    mesh, inputs, cotangents, lengths, adapter_down_matrix, adapter_up_matrix,
    width_side_sketch, rank_side_sketch, heldout_gradient_rows,
):
    n_ex, n_proj = mesh.shape["ex"], mesh.shape["proj"]
    ex_dev, seq, cols = inputs.shape
    tokens = ex_dev * seq
    rank = adapter_down_matrix.shape[0]
    k1 = width_side_sketch.shape[1]
    k2 = rank_side_sketch.shape[2]
    pd = 2 * k2
    kc = k1 // n_proj
    v_rows, v_cols = heldout_gradient_rows.shape
    nv = v_rows * n_ex
    cs = nv // n_proj
    ep = -(-ex_dev // 8) * 8
    pdim = pd * k1
    any_space = pl.BlockSpec(memory_space=pltpu.HBM)
    vmem = pl.BlockSpec(memory_space=pltpu.VMEM)
    dma = pltpu.SemaphoreType.DMA
    peers = n_proj - 1
    per = n_ex // 2
    paired = (
        n_ex == n_proj and n_ex % 2 == 0 and kc == 128 and 3 * v_rows <= 128 and v_rows % 16 == 0
        and k2 % 8 == 0 and v_cols == kc * pd
    )
    head = [
        pltpu.VMEM((tokens, cols), BF16),
        pltpu.VMEM((tokens, cols), BF16),
        pltpu.VMEM((rank, cols), BF16),
        pltpu.VMEM((cols, rank), BF16),
        pltpu.VMEM((cols, k1), BF16),
    ]
    if paired:
        body, end = paired_kernel, paired_finish
        sums_shape = (ep, 128)
        picks = kc * pd // 128
        firsts = [any_space] * 8
        scratch = head + [
            pltpu.VMEM((2, k2, rank), BF16),
            pltpu.SMEM((ex_dev,), jnp.int32),
            pltpu.VMEM((per * v_rows, v_cols), BF16),
            pltpu.VMEM((ex_dev * pd, k1), F32),
            pltpu.VMEM((pd, tokens), BF16),
            pltpu.VMEM((peers, pd, tokens), BF16),
            pltpu.VMEM((n_proj, ex_dev * pd, kc), BF16),
            pltpu.VMEM((peers, ex_dev * pd, kc), BF16),
            pltpu.VMEM((n_proj, ex_dev * pd, kc), BF16),
            pltpu.VMEM((2, ex_dev * 128, kc), BF16),
            pltpu.VMEM((2, picks * ep, 128), F32),
            pltpu.VMEM((2, per, ep, 128), F32),
            pltpu.VMEM((n_proj, ep, 128), F32),
            dma((7,)),
            dma((peers,)), dma((peers,)),
            dma((peers,)), dma((peers,)),
            dma((n_proj,)), dma((n_proj,)),
            dma((n_ex,)), dma((per,)),
            dma((2, per)), dma((n_proj,)),
            dma,
            pltpu.SemaphoreType.REGULAR((n_ex,)),
            pltpu.SemaphoreType.REGULAR,
        ]
    else:
        firsts = [pl.BlockSpec(memory_space=pltpu.SMEM)] + [any_space] * 5 + [vmem, any_space]
        chunks = 2 if v_rows % 32 == 0 else 1
        body, end = kernel, finish
        sums_shape = (2 * ep + 8, cs)
        scratch = head + [
            pltpu.VMEM((ex_dev * pd, k1), F32),
            pltpu.VMEM((2, tokens, k1), BF16),
            pltpu.VMEM((n_ex, v_rows, v_cols), BF16),
            pltpu.VMEM((pd, tokens), BF16),
            pltpu.VMEM((peers, pd, tokens), BF16),
            pltpu.VMEM((n_proj, ex_dev * pd, kc), BF16),
            pltpu.VMEM((peers, ex_dev * pd, kc), BF16),
            pltpu.VMEM((ex_dev * 128, kc), BF16),
            pltpu.VMEM((ep, v_cols), F32),
            pltpu.VMEM((nv, 128), F32),
            pltpu.VMEM((n_proj, 2 * ep + 8, cs), F32),
            pltpu.VMEM((peers, 2 * ep + 8, cs), F32),
            dma((5,)),
            dma((peers,)), dma((peers,)),
            dma((peers,)), dma((peers,)),
            dma((peers,)), dma((peers,)),
            dma((2, n_ex - 1, chunks)), dma((2, n_ex - 1, chunks)),
            dma,
        ]
    train, final = pl.pallas_call(
        functools.partial(body, (n_ex, n_proj, ex_dev, seq, pdim)),
        out_shape=(
            pltpu.VMEM((ep, v_cols), F32),
            pltpu.VMEM(sums_shape, F32),
        ),
        in_specs=firsts,
        out_specs=(vmem, vmem),
        scratch_shapes=scratch,
        compiler_params=pltpu.CompilerParams(
            collective_id=0, has_side_effects=True, vmem_limit_bytes=62 * 1024 * 1024
        ),
        name="project",
    )(
        lengths, inputs.reshape(tokens, cols), cotangents.reshape(tokens, cols),
        adapter_down_matrix, adapter_up_matrix, width_side_sketch,
        rank_side_sketch.swapaxes(1, 2), heldout_gradient_rows,
    )
    return pl.pallas_call(
        functools.partial(end, pdim),
        out_shape=(
            jax.ShapeDtypeStruct((ex_dev, v_cols), BF16),
            jax.ShapeDtypeStruct((ex_dev, cs), F32),
        ),
        in_specs=[vmem, vmem],
        out_specs=(vmem, vmem),
        compiler_params=pltpu.CompilerParams(vmem_limit_bytes=8 * 1024 * 1024),
        name="finish",
    )(train, final)


def solution(mesh):
    in_specs = (
        P(("grp", "ex"), None, "proj"),
        P(("grp", "ex"), None, "proj"),
        P(("grp", "ex")),
        P(None, "proj"),
        P("proj", None),
        P("proj", None),
        P(),
        P(("grp", "ex"), "proj"),
    )
    out_specs = (P(("grp", "ex"), "proj"), P(("grp", "ex"), "proj"))
    return jax.shard_map(
        functools.partial(shards, mesh), mesh=mesh, in_specs=in_specs, out_specs=out_specs, check_vma=False
    )
```

```python
import functools
import math

import jax
import jax.numpy as jnp
from jax import lax
from jax.experimental import pallas as pl
from jax.experimental.pallas import tpu as pltpu
from jax.sharding import PartitionSpec as P

epsilon = 1e-06
MESH = pl.DeviceIdType.MESH
F32 = jnp.float32
BF16 = jnp.bfloat16
NT = (((1,), (1,)), ((), ()))


def dot(a, b, dims=(((1,), (0,)), ((), ()))):
    return lax.dot_general(a, b, dims, preferred_element_type=F32)


def kernel(
    sizes,
    len_ref, x_ref, c_ref, a_ref, b_ref, w_ref, r_ref, v_ref,
    tp_ref, sc_ref,
    xb, cb, ab, bb, wb, rows, left, gath,
    right_own, right_in, t_own, t_in, shuf, flat, sums, msg, msg_in,
    load_sem, rs_sem, rr_sem, ts_sem, tr_sem, ms_sem, mr_sem,
    gs_sem, gr_sem, own_sem,
):
    n_ex, n_proj, ex_dev, seq, pdim = sizes
    grp, me_ex, me = lax.axis_index("grp"), lax.axis_index("ex"), lax.axis_index("proj")
    k2 = r_ref.shape[1]
    pd = 2 * k2
    k1 = wb.shape[1]
    kc = k1 // n_proj
    reps = 128 // pd
    blocks = kc * pd // 128

    loads = []
    for i, (src, dst) in enumerate(
        ((a_ref, ab), (x_ref, xb), (b_ref, bb), (c_ref, cb), (w_ref, wb))
    ):
        copy = pltpu.make_async_copy(src, dst, load_sem.at[i])
        copy.start()
        loads.append(copy)
    own = pltpu.make_async_copy(v_ref, gath.at[me_ex], own_sem)
    own.start()

    def peer(k):
        return lax.rem(me + k, n_proj)

    barrier = pltpu.get_barrier_semaphore()
    for k in range(1, n_proj):
        pl.semaphore_signal(barrier, inc=1, device_id=(grp, me_ex, peer(k)), device_id_type=MESH)

    @pl.when(me_ex > 0)
    def _():
        pl.semaphore_signal(barrier, inc=1, device_id=(grp, me_ex - 1, me), device_id_type=MESH)

    @pl.when(me_ex < n_ex - 1)
    def _():
        pl.semaphore_signal(barrier, inc=1, device_id=(grp, me_ex + 1, me), device_id_type=MESH)

    sides = jnp.minimum(me_ex, 1) + jnp.minimum(n_ex - 1 - me_ex, 1)
    pl.semaphore_wait(barrier, n_proj - 1 + sides)

    chunks = gs_sem.shape[2]
    v_rows = gath.shape[1]
    part_rows = v_rows // chunks

    def hop(way, s, c, src=None):
        if way == 0:
            at, to = jnp.maximum(me_ex - s, 0), jnp.minimum(me_ex + 1, n_ex - 1)
        else:
            at, to = jnp.minimum(me_ex + s, n_ex - 1), jnp.maximum(me_ex - 1, 0)
        span = pl.ds(c * part_rows, part_rows)
        here = gath.at[at, span]
        return pltpu.make_async_remote_copy(
            src_ref=here if src is None else src.at[span],
            dst_ref=here,
            send_sem=gs_sem.at[way, s, c],
            recv_sem=gr_sem.at[way, s, c],
            device_id=(grp, to, me),
            device_id_type=MESH,
        )

    def sends(way, s):
        if way == 0:
            return (me_ex - s >= 0) & (me_ex < n_ex - 1)
        return (me_ex + s <= n_ex - 1) & (me_ex > 0)

    def receives(way, s):
        return (me_ex - 1 - s >= 0) if way == 0 else (me_ex + 1 + s <= n_ex - 1)

    def send_own():
        for way in range(2):
            @pl.when(sends(way, 0))
            def _():
                for c in range(chunks):
                    hop(way, 0, c, v_ref).start()

    def squares(at, first, count):
        held = gath[at, pl.ds(first, count)].astype(F32)
        held = held * held
        acc = held[:, :128]
        for c in range(1, gath.shape[2] // 128):
            acc = acc + held[:, c * 128:(c + 1) * 128]
        sums[pl.ds(pl.multiple_of(at * v_rows + first, part_rows), count), :] = acc

    def relay(s, c, forward=True):
        for way in range(2):
            @pl.when(receives(way, s))
            def _():
                hop(way, s, c).wait_recv()

            if forward:
                @pl.when(sends(way, s + 1))
                def _():
                    hop(way, s + 1, c).start()

            @pl.when(receives(way, s))
            def _():
                squares(me_ex - 1 - s if way == 0 else me_ex + 1 + s, c * part_rows, part_rows)

    def end_step(s):
        for way in range(2):
            @pl.when(sends(way, s))
            def _():
                for c in range(chunks):
                    hop(way, s, c).wait_send()

    send_own()

    def swap(k, src, dst, s_sem, r_sem):
        return pltpu.make_async_remote_copy(
            src_ref=src, dst_ref=dst.at[k - 1], send_sem=s_sem.at[k - 1], recv_sem=r_sem.at[k - 1],
            device_id=(grp, me_ex, peer(k)), device_id_type=MESH,
        )

    loads[0].wait()
    m_in = dot(r_ref[0], ab[...]).astype(BF16)
    loads[1].wait()
    part_in = dot(m_in, xb[...], NT)
    loads[2].wait()
    m_out = dot(r_ref[1], bb[...], NT).astype(BF16)
    loads[3].wait()
    part_out = dot(m_out, cb[...], NT)
    part = jnp.concatenate([part_in, part_out], axis=0)
    right_own[...] = part.astype(BF16)
    copies = [swap(k, right_own, right_in, rs_sem, rr_sem) for k in range(1, n_proj)]
    for copy in copies:
        copy.start()

    queue = [(t, c) for t in range(n_ex - 2) for c in range(chunks)] if n_ex <= 4 else []

    def poll():
        if queue:
            relay(*queue.pop(0))

    loads[4].wait()
    half = k1 // 2
    own.wait()
    left[0, :, :half] = dot(cb[...], wb[:, :half]).astype(BF16)
    squares(me_ex, 0, v_rows)
    poll()
    left[0, :, half:] = dot(cb[...], wb[:, half:]).astype(BF16)
    left[1, :, :half] = dot(xb[...], wb[:, :half]).astype(BF16)
    poll()
    left[1, :, half:] = dot(xb[...], wb[:, half:]).astype(BF16)

    for copy in copies:
        copy.wait()
    total = part
    for k in range(n_proj - 1):
        total = total + right_in[k].astype(F32)
    total = total.astype(BF16)

    position = lax.broadcasted_iota(jnp.int32, (k2, seq), 1)
    for e in range(ex_dev):
        live = position < len_ref[e]
        for p in range(2):
            piece = total[p * k2:(p + 1) * k2, e * seq:(e + 1) * seq].astype(F32)
            piece = jnp.where(live, piece, 0.0).astype(BF16)
            rows[e * pd + p * k2:e * pd + (p + 1) * k2, :] = dot(piece, left[p, e * seq:(e + 1) * seq, :])
    for j in range(n_proj):
        t_own[j] = rows[:, j * kc:(j + 1) * kc].astype(BF16)
    copies = [swap(k, t_own.at[peer(k)], t_in, ts_sem, tr_sem) for k in range(1, n_proj)]
    for copy in copies:
        copy.start()

    while queue:
        poll()

    mine = me * kc
    total_t = rows[:, pl.ds(pl.multiple_of(mine, 128), kc)]
    for copy in copies:
        copy.wait()
    for k in range(n_proj - 1):
        total_t = total_t + t_in[k].astype(F32)

    l_at = lax.broadcasted_iota(jnp.int32, (128, kc), 0)
    k_at = lax.broadcasted_iota(jnp.int32, (128, kc), 1)
    keep = (k_at % reps) == (l_at // pd)
    for e in range(ex_dev):
        one = total_t[e * pd:(e + 1) * pd, :] / len_ref[e].astype(F32)
        one = one.astype(BF16).astype(F32)
        tiled = jnp.concatenate([one] * reps, axis=0)
        shuf[e * 128:(e + 1) * 128, :] = jnp.where(keep, tiled, 0.0).astype(BF16)
    b_at = lax.broadcasted_iota(jnp.int32, (blocks, kc), 0)
    s_at = lax.broadcasted_iota(jnp.int32, (blocks, kc), 1)
    pick = jnp.where((s_at // reps) == b_at, 1.0, 0.0).astype(BF16)
    spread = dot(pick, shuf[...], NT)
    ep = flat.shape[0]
    flat[...] = jnp.zeros_like(flat)
    for b in range(blocks):
        for e in range(ex_dev):
            flat[e:e + 1, b * 128:(b + 1) * 128] = spread[b:b + 1, e * 128:(e + 1) * 128]
    train = flat[...]
    train_bf = train.astype(BF16)
    tp_ref[...] = train
    train_sq = jnp.sum(train * train, axis=1, keepdims=True)

    if n_ex > 4:
        @pl.loop(0, n_ex - 2)
        def _(t):
            for c in range(chunks):
                relay(t, c)

    for c in range(chunks):
        relay(n_ex - 2, c, False)
    nv = n_ex * v_rows
    per = 128 // v_rows
    cs = nv // n_proj
    ones = jnp.ones((8, 128), F32)
    dots = jnp.concatenate(
        [dot(train_bf, gath[i * per:(i + 1) * per].reshape(128, gath.shape[2]), NT) for i in range(nv // 128)],
        axis=1,
    )
    val_sq = lax.dot_general(
        ones, sums[...], NT, precision=lax.Precision.HIGHEST, preferred_element_type=F32
    )
    for j in range(n_proj):
        msg[j, :ep] = dots[:, j * cs:(j + 1) * cs]
        msg[j, ep:ep + 8] = val_sq[:, j * cs:(j + 1) * cs]
        msg[j, ep + 8:] = jnp.broadcast_to(train_sq, (ep, cs))
    copies = [swap(k, msg.at[peer(k)], msg_in, ms_sem, mr_sem) for k in range(1, n_proj)]
    for copy in copies:
        copy.start()
    for s in range(n_ex - 1):
        end_step(s)
    final = msg[me]
    for copy in copies:
        copy.wait()
    for k in range(n_proj - 1):
        final = final + msg_in[k]
    sc_ref[...] = final


def paired_kernel(
    sizes,
    len_hbm, x_ref, c_ref, a_ref, b_ref, w_ref, r_hbm, v_ref,
    tp_ref, sc_ref,
    xb, cb, ab, bb, wb, r_ref, len_ref, held, rows, right_own, right_in, t_send, t_in, t_mate, shuf, flat, f_send, f_recv,
    load_sem, rs_sem, rr_sem, ts_sem, tr_sem, us_sem, ur_sem, hs_sem, hr_sem, fs_sem, fr_sem, own_sem, ready, met,
):
    n_ex, n_proj, ex_dev, seq, pdim = sizes
    grp, me_ex, me = lax.axis_index("grp"), lax.axis_index("ex"), lax.axis_index("proj")
    flank = lax.rem(me_ex, 2)
    mate = me_ex + 1 - 2 * flank
    per = n_ex // 2
    home, slot = me_ex // per, lax.rem(me_ex, per)
    k2 = r_ref.shape[1]
    pd = 2 * k2
    kc = wb.shape[1] // n_proj
    reps = 128 // pd
    picks = kc // reps
    v_rows = v_ref.shape[0]
    ep = flat.shape[1] // picks
    tokens = ex_dev * seq

    def peer(k):
        return lax.rem(me + k, n_proj)

    barrier = pltpu.get_barrier_semaphore()

    def greet(i, at):
        pl.semaphore_signal(barrier, inc=1, device_id=(grp, i, at), device_id_type=MESH)

    loads = []
    for i, (src, dst) in enumerate(
        ((r_hbm, r_ref), (a_ref, ab), (x_ref, xb), (b_ref, bb), (c_ref, cb), (w_ref, wb), (len_hbm, len_ref))
    ):
        copy = pltpu.make_async_copy(src, dst, load_sem.at[i])
        copy.start()
        loads.append(copy)
    for k in range(1, n_proj):
        greet(me_ex, peer(k))
    for i in range(1, n_ex):
        @pl.when(i > me_ex)
        def _():
            greet(i, me)

    @pl.when(flank == 0)
    def _():
        for k in range(1, n_proj):
            greet(mate, peer(k))
    expected = n_proj - 1 + me_ex + flank * (n_proj - 1)

    def place(jj):
        return held.at[pl.ds(jj * v_rows, v_rows)]

    own = pltpu.make_async_copy(v_ref, place(slot), own_sem)

    @pl.when(home == flank)
    def _():
        own.start()

    def give(i):
        return pltpu.make_async_remote_copy(
            src_ref=v_ref, dst_ref=place(slot), send_sem=hs_sem.at[i], recv_sem=hr_sem.at[slot],
            device_id=(grp, i, me), device_id_type=MESH,
        )

    def take(jj):
        return pltpu.make_async_remote_copy(
            src_ref=place(jj), dst_ref=place(jj), send_sem=hs_sem.at[0], recv_sem=hr_sem.at[jj],
            device_id=(grp, me_ex, me), device_id_type=MESH,
        )

    def pass_on(k, src, dst, s_sem, r_sem):
        return pltpu.make_async_remote_copy(
            src_ref=src, dst_ref=dst.at[k], send_sem=s_sem.at[k], recv_sem=r_sem.at[k],
            device_id=(grp, mate, peer(k)), device_id_type=MESH,
        )

    def swap(k, src, dst, s_sem, r_sem):
        return pltpu.make_async_remote_copy(
            src_ref=src, dst_ref=dst.at[k - 1], send_sem=s_sem.at[k - 1], recv_sem=r_sem.at[k - 1],
            device_id=(grp, me_ex, peer(k)), device_id_type=MESH,
        )

    @pl.when(me_ex > 0)
    def _():
        pl.semaphore_wait(barrier, expected)
        for j in range(n_ex - 1):
            @pl.when((j < me_ex) & (j // per == flank))
            def _():
                pl.semaphore_signal(
                    ready.at[me_ex], inc=1, device_id=(grp, j, me), device_id_type=MESH
                )

        for i in range(n_ex - 1):
            @pl.when((i < me_ex) & (i % 2 == home))
            def _():
                give(i).start()

        @pl.when(flank == 1)
        def _():
            for k in range(n_proj):
                pl.semaphore_signal(
                    met, inc=1, device_id=(grp, mate, peer(k)), device_id_type=MESH
                )

    flat[...] = jnp.zeros_like(flat)
    loads[0].wait()
    loads[1].wait()
    m_in = dot(r_ref[0], ab[...]).astype(BF16)
    loads[2].wait()
    part_in = dot(m_in, xb[...], NT)
    loads[3].wait()
    m_out = dot(r_ref[1], bb[...], NT).astype(BF16)
    loads[4].wait()
    part_out = dot(m_out, cb[...], NT)
    part = jnp.concatenate([part_in, part_out], axis=0)
    right_own[...] = part.astype(BF16)

    @pl.when(me_ex == 0)
    def _():
        pl.semaphore_wait(barrier, expected)

    moves = [swap(k, right_own, right_in, rs_sem, rr_sem) for k in range(1, n_proj)]
    for move in moves:
        move.start()
    def give_later(k):
        for i in range(k, n_ex):
            @pl.when((i == me_ex + k) & (i % 2 == home))
            def _():
                pl.semaphore_wait(ready.at[i], 1)
                give(i).start()

    for k in range(1, n_ex):
        give_later(k)

    loads[6].wait()
    position = lax.broadcasted_iota(jnp.int32, (k2, tokens), 1)
    live = []
    scale = []
    for e in range(ex_dev):
        count = len_ref[e]
        live.append((position >= e * seq) & (position < e * seq + count))
        scale.append(1.0 / jnp.full((k2, 128), count.astype(F32), F32))

    total = part
    for k, move in enumerate(moves):
        move.wait_recv()
        total = total + right_in[k].astype(F32)
    total = total.astype(BF16).astype(F32)
    grown = []
    for p, other in enumerate((cb, xb)):
        piece = total[p * k2:(p + 1) * k2]
        spread = jnp.concatenate([jnp.where(one, piece, 0.0) for one in live], axis=0).astype(BF16)
        grown.append(dot(spread, other[...]))
    loads[5].wait()
    result = dot(jnp.concatenate(grown, axis=0).astype(BF16), wb[...])
    for p in range(2):
        for e in range(ex_dev):
            at = (p * ex_dev + e) * k2
            for q in range(n_proj):
                rows[at:at + k2, q * kc:(q + 1) * kc] = result[at:at + k2, q * kc:(q + 1) * kc] * scale[e]
    for q in range(n_proj):
        t_send[q] = rows[:, q * kc:(q + 1) * kc].astype(BF16)
    shares = [swap(k, t_send.at[peer(k)], t_in, ts_sem, tr_sem) for k in range(1, n_proj)]
    for share in shares:
        share.start()

    @pl.when(flank == 0)
    def _():
        pl.semaphore_wait(met, n_proj)

    across = [pass_on(k, t_send.at[peer(k)], t_mate, us_sem, ur_sem) for k in range(n_proj)]
    for share in across:
        share.start()

    l_at = lax.broadcasted_iota(jnp.int32, (128, kc), 0)
    k_at = lax.broadcasted_iota(jnp.int32, (128, kc), 1)
    keep = (k_at % reps) == (l_at // pd)
    b_at = lax.broadcasted_iota(jnp.int32, (picks, kc), 0)
    s_at = lax.broadcasted_iota(jnp.int32, (picks, kc), 1)
    pick = jnp.where((s_at // reps) == b_at, 1.0, 0.0).astype(BF16)

    for jj in range(per):
        @pl.when(flank * per + jj == me_ex)
        def _():
            own.wait()

        @pl.when(flank * per + jj != me_ex)
        def _():
            take(jj).wait_recv()
    acc = jnp.zeros((per * v_rows, 128), F32)
    for c in range(v_ref.shape[1] // 128):
        wide = held[:, c * 128:(c + 1) * 128].astype(F32)
        acc = acc + wide * wide
    val_sq = lax.dot_general(
        jnp.ones((ep, 128), F32), acc, NT, precision=lax.Precision.HIGHEST, preferred_element_type=F32
    )

    def score(w, block):
        block = block.astype(BF16).astype(F32)
        for e in range(ex_dev):
            one = [block[(p * ex_dev + e) * k2:(p * ex_dev + e + 1) * k2] for p in range(2)]
            tiled = jnp.where(keep, jnp.concatenate(one * reps, axis=0), 0.0)
            shuf[w, e * 128:(e + 1) * 128, :] = tiled.astype(BF16)
        spread = dot(pick, shuf[w], NT)
        for e in range(ex_dev):
            flat[w, pl.ds(e, picks, stride=ep), :] = spread[:, e * 128:(e + 1) * 128]
        tiles = [flat[w, b * ep:(b + 1) * ep, :] for b in range(picks)]
        train_sq = jnp.zeros((ep, 128), F32)
        for tile in tiles:
            train_sq = train_sq + tile * tile
        train_sq = jnp.sum(train_sq, axis=1, keepdims=True)
        train = jnp.concatenate(tiles, axis=1)
        dots = dot(train.astype(BF16), held[...], NT)
        for jj in range(per):
            span = slice(jj * v_rows, (jj + 1) * v_rows)
            f_send[w, jj] = jnp.concatenate(
                [dots[:, span], val_sq[:, span], jnp.broadcast_to(train_sq, (ep, 128 - 2 * v_rows))],
                axis=1,
            )
        return train

    def report(w, jj):
        return pltpu.make_async_remote_copy(
            src_ref=f_send.at[w, jj], dst_ref=f_recv.at[me], send_sem=fs_sem.at[w, jj], recv_sem=fr_sem.at[me],
            device_id=(grp, mate if w else me_ex, flank * per + jj), device_id_type=MESH,
        )

    def hear(q):
        return pltpu.make_async_remote_copy(
            src_ref=f_recv.at[q], dst_ref=f_recv.at[q], send_sem=fs_sem.at[0, 0], recv_sem=fr_sem.at[q],
            device_id=(grp, me_ex, me), device_id_type=MESH,
        )

    block = rows[:, pl.ds(pl.multiple_of(me * kc, 128), kc)]
    for k, share in enumerate(shares):
        share.wait_recv()
        block = block + t_in[k].astype(F32)
    train = score(0, block)
    for jj in range(per):
        @pl.when(me != flank * per + jj)
        def _():
            report(0, jj).start()

        @pl.when(me == flank * per + jj)
        def _():
            f_recv[me] = f_send[0, jj]
    block = jnp.zeros((ex_dev * pd, kc), F32)
    for k, share in enumerate(across):
        share.wait_recv()
        block = block + t_mate[k].astype(F32)
    score(1, block)
    for jj in range(per):
        report(1, jj).start()

    tp_ref[...] = train
    for move in moves + shares + across:
        move.wait_send()
    for i in range(n_ex):
        @pl.when((i != me_ex) & (i % 2 == home))
        def _():
            give(i).wait_send()
    for q in range(n_proj):
        @pl.when((me // per != flank) | (me != q))
        def _():
            hear(q).wait_recv()
    final = f_recv[0]
    for q in range(1, n_proj):
        final = final + f_recv[q]
    sc_ref[...] = final
    for jj in range(per):
        @pl.when(me != flank * per + jj)
        def _():
            report(0, jj).wait_send()

        report(1, jj).wait_send()


def paired_finish(pdim, train_ref, sums_ref, tp_ref, sc_ref):
    ex_dev, cs = sc_ref.shape
    tp_ref[...] = train_ref[:ex_dev, :].astype(BF16)
    final = sums_ref[:ex_dev, :]
    sc_ref[...] = (
        math.sqrt(pdim)
        * final[:, :cs]
        * lax.rsqrt(final[:, 2 * cs:3 * cs] + epsilon)
        * lax.rsqrt(final[:, cs:2 * cs] + epsilon)
    )


def finish(pdim, train_ref, sums_ref, tp_ref, sc_ref):
    ex_dev = tp_ref.shape[0]
    ep = train_ref.shape[0]
    tp_ref[...] = train_ref[:ex_dev, :].astype(BF16)
    final = sums_ref[...]
    scores = (
        math.sqrt(pdim)
        * final[:ep]
        * lax.rsqrt(final[ep + 8:] + epsilon)
        * lax.rsqrt(final[ep:ep + 1] + epsilon)
    )
    sc_ref[...] = scores[:ex_dev]


def shards(
    mesh, inputs, cotangents, lengths, adapter_down_matrix, adapter_up_matrix,
    width_side_sketch, rank_side_sketch, heldout_gradient_rows,
):
    n_ex, n_proj = mesh.shape["ex"], mesh.shape["proj"]
    ex_dev, seq, cols = inputs.shape
    tokens = ex_dev * seq
    rank = adapter_down_matrix.shape[0]
    k1 = width_side_sketch.shape[1]
    k2 = rank_side_sketch.shape[2]
    pd = 2 * k2
    kc = k1 // n_proj
    v_rows, v_cols = heldout_gradient_rows.shape
    nv = v_rows * n_ex
    cs = nv // n_proj
    ep = -(-ex_dev // 8) * 8
    pdim = pd * k1
    any_space = pl.BlockSpec(memory_space=pltpu.HBM)
    vmem = pl.BlockSpec(memory_space=pltpu.VMEM)
    dma = pltpu.SemaphoreType.DMA
    peers = n_proj - 1
    per = n_ex // 2
    paired = (
        n_ex == n_proj and n_ex % 2 == 0 and kc == 128 and 3 * v_rows <= 128 and v_rows % 16 == 0
        and k2 % 8 == 0 and v_cols == kc * pd
    )
    head = [
        pltpu.VMEM((tokens, cols), BF16),
        pltpu.VMEM((tokens, cols), BF16),
        pltpu.VMEM((rank, cols), BF16),
        pltpu.VMEM((cols, rank), BF16),
        pltpu.VMEM((cols, k1), BF16),
    ]
    if paired:
        body, end = paired_kernel, paired_finish
        sums_shape = (ep, 128)
        picks = kc * pd // 128
        firsts = [any_space] * 8
        scratch = head + [
            pltpu.VMEM((2, k2, rank), BF16),
            pltpu.SMEM((ex_dev,), jnp.int32),
            pltpu.VMEM((per * v_rows, v_cols), BF16),
            pltpu.VMEM((ex_dev * pd, k1), F32),
            pltpu.VMEM((pd, tokens), BF16),
            pltpu.VMEM((peers, pd, tokens), BF16),
            pltpu.VMEM((n_proj, ex_dev * pd, kc), BF16),
            pltpu.VMEM((peers, ex_dev * pd, kc), BF16),
            pltpu.VMEM((n_proj, ex_dev * pd, kc), BF16),
            pltpu.VMEM((2, ex_dev * 128, kc), BF16),
            pltpu.VMEM((2, picks * ep, 128), F32),
            pltpu.VMEM((2, per, ep, 128), F32),
            pltpu.VMEM((n_proj, ep, 128), F32),
            dma((7,)),
            dma((peers,)), dma((peers,)),
            dma((peers,)), dma((peers,)),
            dma((n_proj,)), dma((n_proj,)),
            dma((n_ex,)), dma((per,)),
            dma((2, per)), dma((n_proj,)),
            dma,
            pltpu.SemaphoreType.REGULAR((n_ex,)),
            pltpu.SemaphoreType.REGULAR,
        ]
    else:
        firsts = [pl.BlockSpec(memory_space=pltpu.SMEM)] + [any_space] * 5 + [vmem, any_space]
        chunks = 2 if v_rows % 32 == 0 else 1
        body, end = kernel, finish
        sums_shape = (2 * ep + 8, cs)
        scratch = head + [
            pltpu.VMEM((ex_dev * pd, k1), F32),
            pltpu.VMEM((2, tokens, k1), BF16),
            pltpu.VMEM((n_ex, v_rows, v_cols), BF16),
            pltpu.VMEM((pd, tokens), BF16),
            pltpu.VMEM((peers, pd, tokens), BF16),
            pltpu.VMEM((n_proj, ex_dev * pd, kc), BF16),
            pltpu.VMEM((peers, ex_dev * pd, kc), BF16),
            pltpu.VMEM((ex_dev * 128, kc), BF16),
            pltpu.VMEM((ep, v_cols), F32),
            pltpu.VMEM((nv, 128), F32),
            pltpu.VMEM((n_proj, 2 * ep + 8, cs), F32),
            pltpu.VMEM((peers, 2 * ep + 8, cs), F32),
            dma((5,)),
            dma((peers,)), dma((peers,)),
            dma((peers,)), dma((peers,)),
            dma((peers,)), dma((peers,)),
            dma((2, n_ex - 1, chunks)), dma((2, n_ex - 1, chunks)),
            dma,
        ]
    train, final = pl.pallas_call(
        functools.partial(body, (n_ex, n_proj, ex_dev, seq, pdim)),
        out_shape=(
            pltpu.VMEM((ep, v_cols), F32),
            pltpu.VMEM(sums_shape, F32),
        ),
        in_specs=firsts,
        out_specs=(vmem, vmem),
        scratch_shapes=scratch,
        compiler_params=pltpu.CompilerParams(
            collective_id=0, has_side_effects=True, vmem_limit_bytes=62 * 1024 * 1024
        ),
        name="project",
    )(
        lengths, inputs.reshape(tokens, cols), cotangents.reshape(tokens, cols),
        adapter_down_matrix, adapter_up_matrix, width_side_sketch,
        rank_side_sketch.swapaxes(1, 2), heldout_gradient_rows,
    )
    return pl.pallas_call(
        functools.partial(end, pdim),
        out_shape=(
            jax.ShapeDtypeStruct((ex_dev, v_cols), BF16),
            jax.ShapeDtypeStruct((ex_dev, cs), F32),
        ),
        in_specs=[vmem, vmem],
        out_specs=(vmem, vmem),
        compiler_params=pltpu.CompilerParams(vmem_limit_bytes=8 * 1024 * 1024),
        name="finish",
    )(train, final)


def solution(mesh):
    in_specs = (
        P(("grp", "ex"), None, "proj"),
        P(("grp", "ex"), None, "proj"),
        P(("grp", "ex")),
        P(None, "proj"),
        P("proj", None),
        P("proj", None),
        P(),
        P(("grp", "ex"), "proj"),
    )
    out_specs = (P(("grp", "ex"), "proj"), P(("grp", "ex"), "proj"))
    return jax.shard_map(
        functools.partial(shards, mesh), mesh=mesh, in_specs=in_specs, out_specs=out_specs, check_vma=False
    )
```

```python
import functools
import math

import jax
import jax.numpy as jnp
from jax import lax
from jax.experimental import pallas as pl
from jax.experimental.pallas import tpu as pltpu
from jax.sharding import PartitionSpec as P

epsilon = 1e-06
MESH = pl.DeviceIdType.MESH
F32 = jnp.float32
BF16 = jnp.bfloat16
NT = (((1,), (1,)), ((), ()))


def dot(a, b, dims=(((1,), (0,)), ((), ()))):
    return lax.dot_general(a, b, dims, preferred_element_type=F32)


def kernel(
    sizes,
    len_ref, x_ref, c_ref, a_ref, b_ref, w_ref, r_ref, v_ref,
    tp_ref, sc_ref,
    xb, cb, ab, bb, wb, rows, left, gath,
    right_own, right_in, t_own, t_in, shuf, flat, sums, msg, msg_in,
    load_sem, rs_sem, rr_sem, ts_sem, tr_sem, ms_sem, mr_sem,
    gs_sem, gr_sem, own_sem,
):
    n_ex, n_proj, ex_dev, seq, pdim = sizes
    grp, me_ex, me = lax.axis_index("grp"), lax.axis_index("ex"), lax.axis_index("proj")
    k2 = r_ref.shape[1]
    pd = 2 * k2
    k1 = wb.shape[1]
    kc = k1 // n_proj
    reps = 128 // pd
    blocks = kc * pd // 128

    loads = []
    for i, (src, dst) in enumerate(
        ((a_ref, ab), (x_ref, xb), (b_ref, bb), (c_ref, cb), (w_ref, wb))
    ):
        copy = pltpu.make_async_copy(src, dst, load_sem.at[i])
        copy.start()
        loads.append(copy)
    own = pltpu.make_async_copy(v_ref, gath.at[me_ex], own_sem)
    own.start()

    def peer(k):
        return lax.rem(me + k, n_proj)

    barrier = pltpu.get_barrier_semaphore()
    for k in range(1, n_proj):
        pl.semaphore_signal(barrier, inc=1, device_id=(grp, me_ex, peer(k)), device_id_type=MESH)

    @pl.when(me_ex > 0)
    def _():
        pl.semaphore_signal(barrier, inc=1, device_id=(grp, me_ex - 1, me), device_id_type=MESH)

    @pl.when(me_ex < n_ex - 1)
    def _():
        pl.semaphore_signal(barrier, inc=1, device_id=(grp, me_ex + 1, me), device_id_type=MESH)

    sides = jnp.minimum(me_ex, 1) + jnp.minimum(n_ex - 1 - me_ex, 1)
    pl.semaphore_wait(barrier, n_proj - 1 + sides)

    chunks = gs_sem.shape[2]
    v_rows = gath.shape[1]
    part_rows = v_rows // chunks

    def hop(way, s, c, src=None):
        if way == 0:
            at, to = jnp.maximum(me_ex - s, 0), jnp.minimum(me_ex + 1, n_ex - 1)
        else:
            at, to = jnp.minimum(me_ex + s, n_ex - 1), jnp.maximum(me_ex - 1, 0)
        span = pl.ds(c * part_rows, part_rows)
        here = gath.at[at, span]
        return pltpu.make_async_remote_copy(
            src_ref=here if src is None else src.at[span],
            dst_ref=here,
            send_sem=gs_sem.at[way, s, c],
            recv_sem=gr_sem.at[way, s, c],
            device_id=(grp, to, me),
            device_id_type=MESH,
        )

    def sends(way, s):
        if way == 0:
            return (me_ex - s >= 0) & (me_ex < n_ex - 1)
        return (me_ex + s <= n_ex - 1) & (me_ex > 0)

    def receives(way, s):
        return (me_ex - 1 - s >= 0) if way == 0 else (me_ex + 1 + s <= n_ex - 1)

    def send_own():
        for way in range(2):
            @pl.when(sends(way, 0))
            def _():
                for c in range(chunks):
                    hop(way, 0, c, v_ref).start()

    def squares(at, first, count):
        held = gath[at, pl.ds(first, count)].astype(F32)
        held = held * held
        acc = held[:, :128]
        for c in range(1, gath.shape[2] // 128):
            acc = acc + held[:, c * 128:(c + 1) * 128]
        sums[pl.ds(pl.multiple_of(at * v_rows + first, part_rows), count), :] = acc

    def relay(s, c, forward=True):
        for way in range(2):
            @pl.when(receives(way, s))
            def _():
                hop(way, s, c).wait_recv()

            if forward:
                @pl.when(sends(way, s + 1))
                def _():
                    hop(way, s + 1, c).start()

            @pl.when(receives(way, s))
            def _():
                squares(me_ex - 1 - s if way == 0 else me_ex + 1 + s, c * part_rows, part_rows)

    def end_step(s):
        for way in range(2):
            @pl.when(sends(way, s))
            def _():
                for c in range(chunks):
                    hop(way, s, c).wait_send()

    send_own()

    def swap(k, src, dst, s_sem, r_sem):
        return pltpu.make_async_remote_copy(
            src_ref=src, dst_ref=dst.at[k - 1], send_sem=s_sem.at[k - 1], recv_sem=r_sem.at[k - 1],
            device_id=(grp, me_ex, peer(k)), device_id_type=MESH,
        )

    loads[0].wait()
    m_in = dot(r_ref[0], ab[...]).astype(BF16)
    loads[1].wait()
    part_in = dot(m_in, xb[...], NT)
    loads[2].wait()
    m_out = dot(r_ref[1], bb[...], NT).astype(BF16)
    loads[3].wait()
    part_out = dot(m_out, cb[...], NT)
    part = jnp.concatenate([part_in, part_out], axis=0)
    right_own[...] = part.astype(BF16)
    copies = [swap(k, right_own, right_in, rs_sem, rr_sem) for k in range(1, n_proj)]
    for copy in copies:
        copy.start()

    queue = [(t, c) for t in range(n_ex - 2) for c in range(chunks)] if n_ex <= 4 else []

    def poll():
        if queue:
            relay(*queue.pop(0))

    loads[4].wait()
    half = k1 // 2
    own.wait()
    left[0, :, :half] = dot(cb[...], wb[:, :half]).astype(BF16)
    squares(me_ex, 0, v_rows)
    poll()
    left[0, :, half:] = dot(cb[...], wb[:, half:]).astype(BF16)
    left[1, :, :half] = dot(xb[...], wb[:, :half]).astype(BF16)
    poll()
    left[1, :, half:] = dot(xb[...], wb[:, half:]).astype(BF16)

    for copy in copies:
        copy.wait()
    total = part
    for k in range(n_proj - 1):
        total = total + right_in[k].astype(F32)
    total = total.astype(BF16)

    position = lax.broadcasted_iota(jnp.int32, (k2, seq), 1)
    for e in range(ex_dev):
        live = position < len_ref[e]
        for p in range(2):
            piece = total[p * k2:(p + 1) * k2, e * seq:(e + 1) * seq].astype(F32)
            piece = jnp.where(live, piece, 0.0).astype(BF16)
            rows[e * pd + p * k2:e * pd + (p + 1) * k2, :] = dot(piece, left[p, e * seq:(e + 1) * seq, :])
    for j in range(n_proj):
        t_own[j] = rows[:, j * kc:(j + 1) * kc].astype(BF16)
    copies = [swap(k, t_own.at[peer(k)], t_in, ts_sem, tr_sem) for k in range(1, n_proj)]
    for copy in copies:
        copy.start()

    while queue:
        poll()

    mine = me * kc
    total_t = rows[:, pl.ds(pl.multiple_of(mine, 128), kc)]
    for copy in copies:
        copy.wait()
    for k in range(n_proj - 1):
        total_t = total_t + t_in[k].astype(F32)

    l_at = lax.broadcasted_iota(jnp.int32, (128, kc), 0)
    k_at = lax.broadcasted_iota(jnp.int32, (128, kc), 1)
    keep = (k_at % reps) == (l_at // pd)
    for e in range(ex_dev):
        one = total_t[e * pd:(e + 1) * pd, :] / len_ref[e].astype(F32)
        one = one.astype(BF16).astype(F32)
        tiled = jnp.concatenate([one] * reps, axis=0)
        shuf[e * 128:(e + 1) * 128, :] = jnp.where(keep, tiled, 0.0).astype(BF16)
    b_at = lax.broadcasted_iota(jnp.int32, (blocks, kc), 0)
    s_at = lax.broadcasted_iota(jnp.int32, (blocks, kc), 1)
    pick = jnp.where((s_at // reps) == b_at, 1.0, 0.0).astype(BF16)
    spread = dot(pick, shuf[...], NT)
    ep = flat.shape[0]
    flat[...] = jnp.zeros_like(flat)
    for b in range(blocks):
        for e in range(ex_dev):
            flat[e:e + 1, b * 128:(b + 1) * 128] = spread[b:b + 1, e * 128:(e + 1) * 128]
    train = flat[...]
    train_bf = train.astype(BF16)
    tp_ref[...] = train
    train_sq = jnp.sum(train * train, axis=1, keepdims=True)

    if n_ex > 4:
        @pl.loop(0, n_ex - 2)
        def _(t):
            for c in range(chunks):
                relay(t, c)

    for c in range(chunks):
        relay(n_ex - 2, c, False)
    nv = n_ex * v_rows
    per = 128 // v_rows
    cs = nv // n_proj
    ones = jnp.ones((8, 128), F32)
    dots = jnp.concatenate(
        [dot(train_bf, gath[i * per:(i + 1) * per].reshape(128, gath.shape[2]), NT) for i in range(nv // 128)],
        axis=1,
    )
    val_sq = lax.dot_general(
        ones, sums[...], NT, precision=lax.Precision.HIGHEST, preferred_element_type=F32
    )
    for j in range(n_proj):
        msg[j, :ep] = dots[:, j * cs:(j + 1) * cs]
        msg[j, ep:ep + 8] = val_sq[:, j * cs:(j + 1) * cs]
        msg[j, ep + 8:] = jnp.broadcast_to(train_sq, (ep, cs))
    copies = [swap(k, msg.at[peer(k)], msg_in, ms_sem, mr_sem) for k in range(1, n_proj)]
    for copy in copies:
        copy.start()
    for s in range(n_ex - 1):
        end_step(s)
    final = msg[me]
    for copy in copies:
        copy.wait()
    for k in range(n_proj - 1):
        final = final + msg_in[k]
    sc_ref[...] = final


def paired_kernel(
    sizes,
    len_hbm, x_ref, c_ref, a_ref, b_ref, w_ref, r_hbm, v_ref,
    tp_ref, sc_ref,
    xb, cb, ab, bb, wb, r_ref, len_ref, held, rows, right_own, right_in, t_send, t_in, t_mate, shuf, flat, f_send, f_recv,
    load_sem, rs_sem, rr_sem, ts_sem, tr_sem, us_sem, ur_sem, hs_sem, hr_sem, fs_sem, fr_sem, own_sem, ready, met,
):
    n_ex, n_proj, ex_dev, seq, pdim = sizes
    grp, me_ex, me = lax.axis_index("grp"), lax.axis_index("ex"), lax.axis_index("proj")
    flank = lax.rem(me_ex, 2)
    mate = me_ex + 1 - 2 * flank
    per = n_ex // 2
    home, slot = me_ex // per, lax.rem(me_ex, per)
    k2 = r_ref.shape[1]
    pd = 2 * k2
    kc = wb.shape[1] // n_proj
    reps = 128 // pd
    picks = kc // reps
    v_rows = v_ref.shape[0]
    ep = flat.shape[1] // picks
    tokens = ex_dev * seq

    def peer(k):
        return lax.rem(me + k, n_proj)

    barrier = pltpu.get_barrier_semaphore()

    def greet(i, at):
        pl.semaphore_signal(barrier, inc=1, device_id=(grp, i, at), device_id_type=MESH)

    loads = []
    for i, (src, dst) in enumerate(
        ((r_hbm, r_ref), (a_ref, ab), (b_ref, bb), (x_ref, xb), (c_ref, cb), (w_ref, wb), (len_hbm, len_ref))
    ):
        copy = pltpu.make_async_copy(src, dst, load_sem.at[i])
        copy.start()
        loads.append(copy)
    for k in range(1, n_proj):
        greet(me_ex, peer(k))
    for i in range(1, n_ex):
        @pl.when(i > me_ex)
        def _():
            greet(i, me)

    @pl.when(flank == 0)
    def _():
        for k in range(1, n_proj):
            greet(mate, peer(k))
    expected = n_proj - 1 + me_ex + flank * (n_proj - 1)

    def place(jj):
        return held.at[pl.ds(jj * v_rows, v_rows)]

    own = pltpu.make_async_copy(v_ref, place(slot), own_sem)

    @pl.when(home == flank)
    def _():
        own.start()

    def give(i):
        return pltpu.make_async_remote_copy(
            src_ref=v_ref, dst_ref=place(slot), send_sem=hs_sem.at[i], recv_sem=hr_sem.at[slot],
            device_id=(grp, i, me), device_id_type=MESH,
        )

    def take(jj):
        return pltpu.make_async_remote_copy(
            src_ref=place(jj), dst_ref=place(jj), send_sem=hs_sem.at[0], recv_sem=hr_sem.at[jj],
            device_id=(grp, me_ex, me), device_id_type=MESH,
        )

    def pass_on(k, src, dst, s_sem, r_sem):
        return pltpu.make_async_remote_copy(
            src_ref=src, dst_ref=dst.at[k], send_sem=s_sem.at[k], recv_sem=r_sem.at[k],
            device_id=(grp, mate, peer(k)), device_id_type=MESH,
        )

    def swap(k, src, dst, s_sem, r_sem):
        return pltpu.make_async_remote_copy(
            src_ref=src, dst_ref=dst.at[k - 1], send_sem=s_sem.at[k - 1], recv_sem=r_sem.at[k - 1],
            device_id=(grp, me_ex, peer(k)), device_id_type=MESH,
        )

    flat[...] = jnp.zeros_like(flat)
    for copy in loads[:3]:
        copy.wait()
    m_in = dot(r_ref[0], ab[...]).astype(BF16)
    m_out = dot(r_ref[1], bb[...], NT).astype(BF16)
    @pl.when(me_ex > 0)
    def _():
        pl.semaphore_wait(barrier, expected)
        for j in range(n_ex - 1):
            @pl.when((j < me_ex) & (j // per == flank))
            def _():
                pl.semaphore_signal(
                    ready.at[me_ex], inc=1, device_id=(grp, j, me), device_id_type=MESH
                )

        for i in range(n_ex - 1):
            @pl.when((i < me_ex) & (i % 2 == home))
            def _():
                give(i).start()

        @pl.when(flank == 1)
        def _():
            for k in range(n_proj):
                pl.semaphore_signal(
                    met, inc=1, device_id=(grp, mate, peer(k)), device_id_type=MESH
                )

    loads[3].wait()
    part_in = dot(m_in, xb[...], NT)
    loads[4].wait()
    part_out = dot(m_out, cb[...], NT)
    part = jnp.concatenate([part_in, part_out], axis=0)
    right_own[...] = part.astype(BF16)

    @pl.when(me_ex == 0)
    def _():
        pl.semaphore_wait(barrier, expected)

    moves = [swap(k, right_own, right_in, rs_sem, rr_sem) for k in range(1, n_proj)]
    for move in moves:
        move.start()
    def give_later(k):
        for i in range(k, n_ex):
            @pl.when((i == me_ex + k) & (i % 2 == home))
            def _():
                pl.semaphore_wait(ready.at[i], 1)
                give(i).start()

    for k in range(1, n_ex):
        give_later(k)

    loads[6].wait()
    position = lax.broadcasted_iota(jnp.int32, (k2, tokens), 1)
    live = []
    scale = []
    for e in range(ex_dev):
        count = len_ref[e]
        live.append((position >= e * seq) & (position < e * seq + count))
        scale.append(1.0 / jnp.full((k2, 128), count.astype(F32), F32))

    total = part
    for k, move in enumerate(moves):
        move.wait_recv()
        total = total + right_in[k].astype(F32)
    total = total.astype(BF16).astype(F32)
    grown = []
    for p, other in enumerate((cb, xb)):
        piece = total[p * k2:(p + 1) * k2]
        spread = jnp.concatenate([jnp.where(one, piece, 0.0) for one in live], axis=0).astype(BF16)
        grown.append(dot(spread, other[...]))
    loads[5].wait()
    result = dot(jnp.concatenate(grown, axis=0).astype(BF16), wb[...])
    for p in range(2):
        for e in range(ex_dev):
            at = (p * ex_dev + e) * k2
            for q in range(n_proj):
                rows[at:at + k2, q * kc:(q + 1) * kc] = result[at:at + k2, q * kc:(q + 1) * kc] * scale[e]
    for q in range(n_proj):
        t_send[q] = rows[:, q * kc:(q + 1) * kc].astype(BF16)
    shares = [swap(k, t_send.at[peer(k)], t_in, ts_sem, tr_sem) for k in range(1, n_proj)]
    across = [pass_on(k, t_send.at[peer(k)], t_mate, us_sem, ur_sem) for k in range(n_proj)]

    @pl.when(flank == 1)
    def _():
        for share in (across[2], across[1], across[3], across[0]):
            share.start()

    for share in shares:
        share.start()

    @pl.when(flank == 0)
    def _():
        pl.semaphore_wait(met, n_proj)
        for share in across:
            share.start()

    l_at = lax.broadcasted_iota(jnp.int32, (128, kc), 0)
    k_at = lax.broadcasted_iota(jnp.int32, (128, kc), 1)
    keep = (k_at % reps) == (l_at // pd)
    b_at = lax.broadcasted_iota(jnp.int32, (picks, kc), 0)
    s_at = lax.broadcasted_iota(jnp.int32, (picks, kc), 1)
    pick = jnp.where((s_at // reps) == b_at, 1.0, 0.0).astype(BF16)

    for jj in range(per):
        @pl.when(flank * per + jj == me_ex)
        def _():
            own.wait()

        @pl.when(flank * per + jj != me_ex)
        def _():
            take(jj).wait_recv()
    acc = jnp.zeros((per * v_rows, 128), F32)
    for c in range(v_ref.shape[1] // 128):
        wide = held[:, c * 128:(c + 1) * 128].astype(F32)
        acc = acc + wide * wide
    val_sq = lax.dot_general(
        jnp.ones((ep, 128), F32), acc, NT, precision=lax.Precision.HIGHEST, preferred_element_type=F32
    )

    def score(w, block):
        block = block.astype(BF16).astype(F32)
        for e in range(ex_dev):
            one = [block[(p * ex_dev + e) * k2:(p * ex_dev + e + 1) * k2] for p in range(2)]
            tiled = jnp.where(keep, jnp.concatenate(one * reps, axis=0), 0.0)
            shuf[w, e * 128:(e + 1) * 128, :] = tiled.astype(BF16)
        spread = dot(pick, shuf[w], NT)
        for e in range(ex_dev):
            flat[w, pl.ds(e, picks, stride=ep), :] = spread[:, e * 128:(e + 1) * 128]
        tiles = [flat[w, b * ep:(b + 1) * ep, :] for b in range(picks)]
        train_sq = jnp.zeros((ep, 128), F32)
        for tile in tiles:
            train_sq = train_sq + tile * tile
        train_sq = jnp.sum(train_sq, axis=1, keepdims=True)
        train = jnp.concatenate(tiles, axis=1)
        dots = dot(train.astype(BF16), held[...], NT)
        for jj in range(per):
            span = slice(jj * v_rows, (jj + 1) * v_rows)
            f_send[w, jj] = jnp.concatenate(
                [dots[:, span], val_sq[:, span], jnp.broadcast_to(train_sq, (ep, 128 - 2 * v_rows))],
                axis=1,
            )
        return train

    def report(w, jj):
        return pltpu.make_async_remote_copy(
            src_ref=f_send.at[w, jj], dst_ref=f_recv.at[me], send_sem=fs_sem.at[w, jj], recv_sem=fr_sem.at[me],
            device_id=(grp, mate if w else me_ex, flank * per + jj), device_id_type=MESH,
        )

    def hear(q):
        return pltpu.make_async_remote_copy(
            src_ref=f_recv.at[q], dst_ref=f_recv.at[q], send_sem=fs_sem.at[0, 0], recv_sem=fr_sem.at[q],
            device_id=(grp, me_ex, me), device_id_type=MESH,
        )

    def own_stage():
        block = rows[:, pl.ds(pl.multiple_of(me * kc, 128), kc)]
        for k, share in enumerate(shares):
            share.wait_recv()
            block = block + t_in[k].astype(F32)
        tp_ref[...] = score(0, block)
        for jj in range(per):
            @pl.when(me != flank * per + jj)
            def _():
                report(0, jj).start()

            @pl.when(me == flank * per + jj)
            def _():
                f_recv[me] = f_send[0, jj]

    def mate_stage():
        block = jnp.zeros((ex_dev * pd, kc), F32)
        for k, share in enumerate(across):
            share.wait_recv()
            block = block + t_mate[k].astype(F32)
        score(1, block)
        for jj in range(per):
            report(1, jj).start()

    @pl.when(flank == 0)
    def _():
        own_stage()
        mate_stage()

    @pl.when(flank == 1)
    def _():
        mate_stage()
        own_stage()

    for move in moves + shares + across:
        move.wait_send()
    for i in range(n_ex):
        @pl.when((i != me_ex) & (i % 2 == home))
        def _():
            give(i).wait_send()
    for q in range(n_proj):
        @pl.when((me // per != flank) | (me != q))
        def _():
            hear(q).wait_recv()
    final = f_recv[0]
    for q in range(1, n_proj):
        final = final + f_recv[q]
    sc_ref[...] = final
    for jj in range(per):
        @pl.when(me != flank * per + jj)
        def _():
            report(0, jj).wait_send()

        report(1, jj).wait_send()


def paired_finish(pdim, train_ref, sums_ref, tp_ref, sc_ref):
    ex_dev, cs = sc_ref.shape
    tp_ref[...] = train_ref[:ex_dev, :].astype(BF16)
    final = sums_ref[:ex_dev, :]
    sc_ref[...] = (
        math.sqrt(pdim)
        * final[:, :cs]
        * lax.rsqrt(final[:, 2 * cs:3 * cs] + epsilon)
        * lax.rsqrt(final[:, cs:2 * cs] + epsilon)
    )


def finish(pdim, train_ref, sums_ref, tp_ref, sc_ref):
    ex_dev = tp_ref.shape[0]
    ep = train_ref.shape[0]
    tp_ref[...] = train_ref[:ex_dev, :].astype(BF16)
    final = sums_ref[...]
    scores = (
        math.sqrt(pdim)
        * final[:ep]
        * lax.rsqrt(final[ep + 8:] + epsilon)
        * lax.rsqrt(final[ep:ep + 1] + epsilon)
    )
    sc_ref[...] = scores[:ex_dev]


def shards(
    mesh, inputs, cotangents, lengths, adapter_down_matrix, adapter_up_matrix,
    width_side_sketch, rank_side_sketch, heldout_gradient_rows,
):
    n_ex, n_proj = mesh.shape["ex"], mesh.shape["proj"]
    ex_dev, seq, cols = inputs.shape
    tokens = ex_dev * seq
    rank = adapter_down_matrix.shape[0]
    k1 = width_side_sketch.shape[1]
    k2 = rank_side_sketch.shape[2]
    pd = 2 * k2
    kc = k1 // n_proj
    v_rows, v_cols = heldout_gradient_rows.shape
    nv = v_rows * n_ex
    cs = nv // n_proj
    ep = -(-ex_dev // 8) * 8
    pdim = pd * k1
    any_space = pl.BlockSpec(memory_space=pltpu.HBM)
    vmem = pl.BlockSpec(memory_space=pltpu.VMEM)
    dma = pltpu.SemaphoreType.DMA
    peers = n_proj - 1
    per = n_ex // 2
    paired = (
        n_ex == n_proj and n_ex % 2 == 0 and kc == 128 and 3 * v_rows <= 128 and v_rows % 16 == 0
        and k2 % 8 == 0 and v_cols == kc * pd
    )
    head = [
        pltpu.VMEM((tokens, cols), BF16),
        pltpu.VMEM((tokens, cols), BF16),
        pltpu.VMEM((rank, cols), BF16),
        pltpu.VMEM((cols, rank), BF16),
        pltpu.VMEM((cols, k1), BF16),
    ]
    if paired:
        body, end = paired_kernel, paired_finish
        sums_shape = (ep, 128)
        picks = kc * pd // 128
        firsts = [any_space] * 8
        scratch = head + [
            pltpu.VMEM((2, k2, rank), BF16),
            pltpu.SMEM((ex_dev,), jnp.int32),
            pltpu.VMEM((per * v_rows, v_cols), BF16),
            pltpu.VMEM((ex_dev * pd, k1), F32),
            pltpu.VMEM((pd, tokens), BF16),
            pltpu.VMEM((peers, pd, tokens), BF16),
            pltpu.VMEM((n_proj, ex_dev * pd, kc), BF16),
            pltpu.VMEM((peers, ex_dev * pd, kc), BF16),
            pltpu.VMEM((n_proj, ex_dev * pd, kc), BF16),
            pltpu.VMEM((2, ex_dev * 128, kc), BF16),
            pltpu.VMEM((2, picks * ep, 128), F32),
            pltpu.VMEM((2, per, ep, 128), F32),
            pltpu.VMEM((n_proj, ep, 128), F32),
            dma((7,)),
            dma((peers,)), dma((peers,)),
            dma((peers,)), dma((peers,)),
            dma((n_proj,)), dma((n_proj,)),
            dma((n_ex,)), dma((per,)),
            dma((2, per)), dma((n_proj,)),
            dma,
            pltpu.SemaphoreType.REGULAR((n_ex,)),
            pltpu.SemaphoreType.REGULAR,
        ]
    else:
        firsts = [pl.BlockSpec(memory_space=pltpu.SMEM)] + [any_space] * 5 + [vmem, any_space]
        chunks = 2 if v_rows % 32 == 0 else 1
        body, end = kernel, finish
        sums_shape = (2 * ep + 8, cs)
        scratch = head + [
            pltpu.VMEM((ex_dev * pd, k1), F32),
            pltpu.VMEM((2, tokens, k1), BF16),
            pltpu.VMEM((n_ex, v_rows, v_cols), BF16),
            pltpu.VMEM((pd, tokens), BF16),
            pltpu.VMEM((peers, pd, tokens), BF16),
            pltpu.VMEM((n_proj, ex_dev * pd, kc), BF16),
            pltpu.VMEM((peers, ex_dev * pd, kc), BF16),
            pltpu.VMEM((ex_dev * 128, kc), BF16),
            pltpu.VMEM((ep, v_cols), F32),
            pltpu.VMEM((nv, 128), F32),
            pltpu.VMEM((n_proj, 2 * ep + 8, cs), F32),
            pltpu.VMEM((peers, 2 * ep + 8, cs), F32),
            dma((5,)),
            dma((peers,)), dma((peers,)),
            dma((peers,)), dma((peers,)),
            dma((peers,)), dma((peers,)),
            dma((2, n_ex - 1, chunks)), dma((2, n_ex - 1, chunks)),
            dma,
        ]
    train, final = pl.pallas_call(
        functools.partial(body, (n_ex, n_proj, ex_dev, seq, pdim)),
        out_shape=(
            pltpu.VMEM((ep, v_cols), F32),
            pltpu.VMEM(sums_shape, F32),
        ),
        in_specs=firsts,
        out_specs=(vmem, vmem),
        scratch_shapes=scratch,
        compiler_params=pltpu.CompilerParams(
            collective_id=0, has_side_effects=True, vmem_limit_bytes=62 * 1024 * 1024
        ),
        name="project",
    )(
        lengths, inputs.reshape(tokens, cols), cotangents.reshape(tokens, cols),
        adapter_down_matrix, adapter_up_matrix, width_side_sketch,
        rank_side_sketch.swapaxes(1, 2), heldout_gradient_rows,
    )
    return pl.pallas_call(
        functools.partial(end, pdim),
        out_shape=(
            jax.ShapeDtypeStruct((ex_dev, v_cols), BF16),
            jax.ShapeDtypeStruct((ex_dev, cs), F32),
        ),
        in_specs=[vmem, vmem],
        out_specs=(vmem, vmem),
        compiler_params=pltpu.CompilerParams(vmem_limit_bytes=8 * 1024 * 1024),
        name="finish",
    )(train, final)


def solution(mesh):
    in_specs = (
        P(("grp", "ex"), None, "proj"),
        P(("grp", "ex"), None, "proj"),
        P(("grp", "ex")),
        P(None, "proj"),
        P("proj", None),
        P("proj", None),
        P(),
        P(("grp", "ex"), "proj"),
    )
    out_specs = (P(("grp", "ex"), "proj"), P(("grp", "ex"), "proj"))
    return jax.shard_map(
        functools.partial(shards, mesh), mesh=mesh, in_specs=in_specs, out_specs=out_specs, check_vma=False
    )
```

```python
import functools
import math

import jax
import jax.numpy as jnp
from jax import lax
from jax.experimental import pallas as pl
from jax.experimental.pallas import tpu as pltpu
from jax.sharding import PartitionSpec as P

epsilon = 1e-06
MESH = pl.DeviceIdType.MESH
F32 = jnp.float32
BF16 = jnp.bfloat16
NT = (((1,), (1,)), ((), ()))


def dot(a, b, dims=(((1,), (0,)), ((), ()))):
    return lax.dot_general(a, b, dims, preferred_element_type=F32)


def kernel(
    sizes,
    len_ref, x_ref, c_ref, a_ref, b_ref, w_ref, r_ref, v_ref,
    tp_ref, sc_ref,
    xb, cb, ab, bb, wb, rows, left, gath,
    right_own, right_in, t_own, t_in, shuf, flat, sums, msg, msg_in,
    load_sem, rs_sem, rr_sem, ts_sem, tr_sem, ms_sem, mr_sem,
    gs_sem, gr_sem, own_sem,
):
    n_ex, n_proj, ex_dev, seq, pdim = sizes
    grp, me_ex, me = lax.axis_index("grp"), lax.axis_index("ex"), lax.axis_index("proj")
    k2 = r_ref.shape[1]
    pd = 2 * k2
    k1 = wb.shape[1]
    kc = k1 // n_proj
    reps = 128 // pd
    blocks = kc * pd // 128

    loads = []
    for i, (src, dst) in enumerate(
        ((a_ref, ab), (x_ref, xb), (b_ref, bb), (c_ref, cb), (w_ref, wb))
    ):
        copy = pltpu.make_async_copy(src, dst, load_sem.at[i])
        copy.start()
        loads.append(copy)
    own = pltpu.make_async_copy(v_ref, gath.at[me_ex], own_sem)
    own.start()

    def peer(k):
        return lax.rem(me + k, n_proj)

    barrier = pltpu.get_barrier_semaphore()
    for k in range(1, n_proj):
        pl.semaphore_signal(barrier, inc=1, device_id=(grp, me_ex, peer(k)), device_id_type=MESH)

    @pl.when(me_ex > 0)
    def _():
        pl.semaphore_signal(barrier, inc=1, device_id=(grp, me_ex - 1, me), device_id_type=MESH)

    @pl.when(me_ex < n_ex - 1)
    def _():
        pl.semaphore_signal(barrier, inc=1, device_id=(grp, me_ex + 1, me), device_id_type=MESH)

    sides = jnp.minimum(me_ex, 1) + jnp.minimum(n_ex - 1 - me_ex, 1)
    pl.semaphore_wait(barrier, n_proj - 1 + sides)

    chunks = gs_sem.shape[2]
    v_rows = gath.shape[1]
    part_rows = v_rows // chunks

    def hop(way, s, c, src=None):
        if way == 0:
            at, to = jnp.maximum(me_ex - s, 0), jnp.minimum(me_ex + 1, n_ex - 1)
        else:
            at, to = jnp.minimum(me_ex + s, n_ex - 1), jnp.maximum(me_ex - 1, 0)
        span = pl.ds(c * part_rows, part_rows)
        here = gath.at[at, span]
        return pltpu.make_async_remote_copy(
            src_ref=here if src is None else src.at[span],
            dst_ref=here,
            send_sem=gs_sem.at[way, s, c],
            recv_sem=gr_sem.at[way, s, c],
            device_id=(grp, to, me),
            device_id_type=MESH,
        )

    def sends(way, s):
        if way == 0:
            return (me_ex - s >= 0) & (me_ex < n_ex - 1)
        return (me_ex + s <= n_ex - 1) & (me_ex > 0)

    def receives(way, s):
        return (me_ex - 1 - s >= 0) if way == 0 else (me_ex + 1 + s <= n_ex - 1)

    def send_own():
        for way in range(2):
            @pl.when(sends(way, 0))
            def _():
                for c in range(chunks):
                    hop(way, 0, c, v_ref).start()

    def squares(at, first, count):
        held = gath[at, pl.ds(first, count)].astype(F32)
        held = held * held
        acc = held[:, :128]
        for c in range(1, gath.shape[2] // 128):
            acc = acc + held[:, c * 128:(c + 1) * 128]
        sums[pl.ds(pl.multiple_of(at * v_rows + first, part_rows), count), :] = acc

    def relay(s, c, forward=True):
        for way in range(2):
            @pl.when(receives(way, s))
            def _():
                hop(way, s, c).wait_recv()

            if forward:
                @pl.when(sends(way, s + 1))
                def _():
                    hop(way, s + 1, c).start()

            @pl.when(receives(way, s))
            def _():
                squares(me_ex - 1 - s if way == 0 else me_ex + 1 + s, c * part_rows, part_rows)

    def end_step(s):
        for way in range(2):
            @pl.when(sends(way, s))
            def _():
                for c in range(chunks):
                    hop(way, s, c).wait_send()

    send_own()

    def swap(k, src, dst, s_sem, r_sem):
        return pltpu.make_async_remote_copy(
            src_ref=src, dst_ref=dst.at[k - 1], send_sem=s_sem.at[k - 1], recv_sem=r_sem.at[k - 1],
            device_id=(grp, me_ex, peer(k)), device_id_type=MESH,
        )

    loads[0].wait()
    m_in = dot(r_ref[0], ab[...]).astype(BF16)
    loads[1].wait()
    part_in = dot(m_in, xb[...], NT)
    loads[2].wait()
    m_out = dot(r_ref[1], bb[...], NT).astype(BF16)
    loads[3].wait()
    part_out = dot(m_out, cb[...], NT)
    part = jnp.concatenate([part_in, part_out], axis=0)
    right_own[...] = part.astype(BF16)
    copies = [swap(k, right_own, right_in, rs_sem, rr_sem) for k in range(1, n_proj)]
    for copy in copies:
        copy.start()

    queue = [(t, c) for t in range(n_ex - 2) for c in range(chunks)] if n_ex <= 4 else []

    def poll():
        if queue:
            relay(*queue.pop(0))

    loads[4].wait()
    half = k1 // 2
    own.wait()
    left[0, :, :half] = dot(cb[...], wb[:, :half]).astype(BF16)
    squares(me_ex, 0, v_rows)
    poll()
    left[0, :, half:] = dot(cb[...], wb[:, half:]).astype(BF16)
    left[1, :, :half] = dot(xb[...], wb[:, :half]).astype(BF16)
    poll()
    left[1, :, half:] = dot(xb[...], wb[:, half:]).astype(BF16)

    for copy in copies:
        copy.wait()
    total = part
    for k in range(n_proj - 1):
        total = total + right_in[k].astype(F32)
    total = total.astype(BF16)

    position = lax.broadcasted_iota(jnp.int32, (k2, seq), 1)
    for e in range(ex_dev):
        live = position < len_ref[e]
        for p in range(2):
            piece = total[p * k2:(p + 1) * k2, e * seq:(e + 1) * seq].astype(F32)
            piece = jnp.where(live, piece, 0.0).astype(BF16)
            rows[e * pd + p * k2:e * pd + (p + 1) * k2, :] = dot(piece, left[p, e * seq:(e + 1) * seq, :])
    for j in range(n_proj):
        t_own[j] = rows[:, j * kc:(j + 1) * kc].astype(BF16)
    copies = [swap(k, t_own.at[peer(k)], t_in, ts_sem, tr_sem) for k in range(1, n_proj)]
    for copy in copies:
        copy.start()

    while queue:
        poll()

    mine = me * kc
    total_t = rows[:, pl.ds(pl.multiple_of(mine, 128), kc)]
    for copy in copies:
        copy.wait()
    for k in range(n_proj - 1):
        total_t = total_t + t_in[k].astype(F32)

    l_at = lax.broadcasted_iota(jnp.int32, (128, kc), 0)
    k_at = lax.broadcasted_iota(jnp.int32, (128, kc), 1)
    keep = (k_at % reps) == (l_at // pd)
    for e in range(ex_dev):
        one = total_t[e * pd:(e + 1) * pd, :] / len_ref[e].astype(F32)
        one = one.astype(BF16).astype(F32)
        tiled = jnp.concatenate([one] * reps, axis=0)
        shuf[e * 128:(e + 1) * 128, :] = jnp.where(keep, tiled, 0.0).astype(BF16)
    b_at = lax.broadcasted_iota(jnp.int32, (blocks, kc), 0)
    s_at = lax.broadcasted_iota(jnp.int32, (blocks, kc), 1)
    pick = jnp.where((s_at // reps) == b_at, 1.0, 0.0).astype(BF16)
    spread = dot(pick, shuf[...], NT)
    ep = flat.shape[0]
    flat[...] = jnp.zeros_like(flat)
    for b in range(blocks):
        for e in range(ex_dev):
            flat[e:e + 1, b * 128:(b + 1) * 128] = spread[b:b + 1, e * 128:(e + 1) * 128]
    train = flat[...]
    train_bf = train.astype(BF16)
    tp_ref[...] = train
    train_sq = jnp.sum(train * train, axis=1, keepdims=True)

    if n_ex > 4:
        @pl.loop(0, n_ex - 2)
        def _(t):
            for c in range(chunks):
                relay(t, c)

    for c in range(chunks):
        relay(n_ex - 2, c, False)
    nv = n_ex * v_rows
    per = 128 // v_rows
    cs = nv // n_proj
    ones = jnp.ones((8, 128), F32)
    dots = jnp.concatenate(
        [dot(train_bf, gath[i * per:(i + 1) * per].reshape(128, gath.shape[2]), NT) for i in range(nv // 128)],
        axis=1,
    )
    val_sq = lax.dot_general(
        ones, sums[...], NT, precision=lax.Precision.HIGHEST, preferred_element_type=F32
    )
    for j in range(n_proj):
        msg[j, :ep] = dots[:, j * cs:(j + 1) * cs]
        msg[j, ep:ep + 8] = val_sq[:, j * cs:(j + 1) * cs]
        msg[j, ep + 8:] = jnp.broadcast_to(train_sq, (ep, cs))
    copies = [swap(k, msg.at[peer(k)], msg_in, ms_sem, mr_sem) for k in range(1, n_proj)]
    for copy in copies:
        copy.start()
    for s in range(n_ex - 1):
        end_step(s)
    final = msg[me]
    for copy in copies:
        copy.wait()
    for k in range(n_proj - 1):
        final = final + msg_in[k]
    sc_ref[...] = final


def paired_kernel(
    sizes,
    len_hbm, x_ref, c_ref, a_ref, b_ref, w_ref, r_hbm, v_ref,
    tp_ref, sc_ref,
    xb, cb, ab, bb, wb, r_ref, len_ref, held, left, rows, right_own, right_in, t_send, t_in, t_mate, shuf, flat, f_send, f_recv,
    load_sem, rs_sem, rr_sem, ts_sem, tr_sem, us_sem, ur_sem, hs_sem, hr_sem, fs_sem, fr_sem, own_sem, ready, met, near,
):
    n_ex, n_proj, ex_dev, seq, pdim = sizes
    grp, me_ex, me = lax.axis_index("grp"), lax.axis_index("ex"), lax.axis_index("proj")
    flank = lax.rem(me_ex, 2)
    mate = me_ex + 1 - 2 * flank
    per = n_ex // 2
    home, slot = me_ex // per, lax.rem(me_ex, per)
    k2 = r_ref.shape[1]
    pd = 2 * k2
    kc = wb.shape[1] // n_proj
    reps = 128 // pd
    picks = kc // reps
    v_rows = v_ref.shape[0]
    ep = flat.shape[1] // picks
    tokens = ex_dev * seq

    def peer(k):
        return lax.rem(me + k, n_proj)

    barrier = pltpu.get_barrier_semaphore()

    def greet(i, at):
        pl.semaphore_signal(barrier, inc=1, device_id=(grp, i, at), device_id_type=MESH)

    loads = []
    for i, (src, dst) in enumerate(
        ((r_hbm, r_ref), (a_ref, ab), (b_ref, bb), (x_ref, xb), (c_ref, cb), (w_ref, wb), (len_hbm, len_ref))
    ):
        copy = pltpu.make_async_copy(src, dst, load_sem.at[i])
        copy.start()
        loads.append(copy)
    for q in range(1, n_proj):
        @pl.when(q > me)
        def _():
            greet(me_ex, q)
    for i in range(1, n_ex):
        @pl.when(i > me_ex)
        def _():
            greet(i, me)

    @pl.when(flank == 0)
    def _():
        for k in range(1, n_proj):
            greet(mate, peer(k))
    expected = me + me_ex + flank * (n_proj - 1)

    def place(jj):
        return held.at[pl.ds(jj * v_rows, v_rows)]

    own = pltpu.make_async_copy(v_ref, place(slot), own_sem)

    @pl.when(home == flank)
    def _():
        own.start()

    def give(i):
        return pltpu.make_async_remote_copy(
            src_ref=v_ref, dst_ref=place(slot), send_sem=hs_sem.at[i], recv_sem=hr_sem.at[slot],
            device_id=(grp, i, me), device_id_type=MESH,
        )

    def take(jj):
        return pltpu.make_async_remote_copy(
            src_ref=place(jj), dst_ref=place(jj), send_sem=hs_sem.at[0], recv_sem=hr_sem.at[jj],
            device_id=(grp, me_ex, me), device_id_type=MESH,
        )

    def pass_on(k, src, dst, s_sem, r_sem):
        return pltpu.make_async_remote_copy(
            src_ref=src, dst_ref=dst.at[k], send_sem=s_sem.at[k], recv_sem=r_sem.at[k],
            device_id=(grp, mate, peer(k)), device_id_type=MESH,
        )

    def swap(k, src, dst, s_sem, r_sem):
        return pltpu.make_async_remote_copy(
            src_ref=src, dst_ref=dst.at[k - 1], send_sem=s_sem.at[k - 1], recv_sem=r_sem.at[k - 1],
            device_id=(grp, me_ex, peer(k)), device_id_type=MESH,
        )

    @pl.when(expected > 0)
    def _():
        pl.semaphore_wait(barrier, expected)

    for j in range(n_ex - 1):
        @pl.when((j < me_ex) & (j // per == flank))
        def _():
            pl.semaphore_signal(
                ready.at[me_ex], inc=1, device_id=(grp, j, me), device_id_type=MESH
            )

    for i in range(n_ex - 1):
        @pl.when((i < me_ex) & (i % 2 == home))
        def _():
            give(i).start()

    @pl.when(flank == 1)
    def _():
        for k in range(n_proj):
            pl.semaphore_signal(
                met, inc=1, device_id=(grp, mate, peer(k)), device_id_type=MESH
            )

    for q in range(n_proj - 1):
        @pl.when(q < me)
        def _():
            pl.semaphore_signal(near, inc=1, device_id=(grp, me_ex, q), device_id_type=MESH)

    flat[...] = jnp.zeros_like(flat)
    for copy in loads[:3]:
        copy.wait()
    m_in = dot(r_ref[0], ab[...]).astype(BF16)
    m_out = dot(r_ref[1], bb[...], NT).astype(BF16)
    loads[3].wait()
    part_in = dot(m_in, xb[...], NT)
    def give_later(k):
        for i in range(k, n_ex):
            @pl.when((i == me_ex + k) & (i % 2 == home))
            def _():
                pl.semaphore_wait(ready.at[i], 1)
                give(i).start()

    @pl.when(flank == 1)
    def _():
        give_later(1)

    loads[4].wait()
    part_out = dot(m_out, cb[...], NT)
    part = jnp.concatenate([part_in, part_out], axis=0)
    right_own[...] = part.astype(BF16)

    @pl.when(me < n_proj - 1)
    def _():
        pl.semaphore_wait(near, n_proj - 1 - me)

    moves = [swap(k, right_own, right_in, rs_sem, rr_sem) for k in range(1, n_proj)]
    for move in moves:
        move.start()
    @pl.when(flank == 0)
    def _():
        give_later(1)

    for k in range(2, n_ex):
        give_later(k)
    loads[5].wait()
    left[0] = dot(cb[...], wb[...]).astype(BF16)
    left[1] = dot(xb[...], wb[...]).astype(BF16)

    loads[6].wait()
    position = lax.broadcasted_iota(jnp.int32, (k2, tokens), 1)
    live = []
    scale = []
    for e in range(ex_dev):
        count = len_ref[e]
        live.append((position >= e * seq) & (position < e * seq + count))
        scale.append(1.0 / jnp.full((k2, 128), count.astype(F32), F32))

    total = part
    for k, move in enumerate(moves):
        move.wait_recv()
        total = total + right_in[k].astype(F32)
    total = total.astype(BF16).astype(F32)
    result = []
    for p in range(2):
        piece = total[p * k2:(p + 1) * k2]
        spread = jnp.concatenate([jnp.where(one, piece, 0.0) for one in live], axis=0).astype(BF16)
        result.append(dot(spread, left[p]))
    result = jnp.concatenate(result, axis=0)
    for p in range(2):
        for e in range(ex_dev):
            at = (p * ex_dev + e) * k2
            for q in range(n_proj):
                rows[at:at + k2, q * kc:(q + 1) * kc] = result[at:at + k2, q * kc:(q + 1) * kc] * scale[e]
    for q in range(n_proj):
        t_send[q] = rows[:, q * kc:(q + 1) * kc].astype(BF16)
    shares = [swap(k, t_send.at[peer(k)], t_in, ts_sem, tr_sem) for k in range(1, n_proj)]
    across = [pass_on(k, t_send.at[peer(k)], t_mate, us_sem, ur_sem) for k in range(n_proj)]

    @pl.when(flank == 1)
    def _():
        for share in (across[2], across[1], across[3], across[0]):
            share.start()

    for share in shares:
        share.start()

    @pl.when(flank == 0)
    def _():
        pl.semaphore_wait(met, n_proj)
        for share in across:
            share.start()

    l_at = lax.broadcasted_iota(jnp.int32, (128, kc), 0)
    k_at = lax.broadcasted_iota(jnp.int32, (128, kc), 1)
    keep = (k_at % reps) == (l_at // pd)
    b_at = lax.broadcasted_iota(jnp.int32, (picks, kc), 0)
    s_at = lax.broadcasted_iota(jnp.int32, (picks, kc), 1)
    pick = jnp.where((s_at // reps) == b_at, 1.0, 0.0).astype(BF16)

    for jj in range(per):
        @pl.when(flank * per + jj == me_ex)
        def _():
            own.wait()

        @pl.when(flank * per + jj != me_ex)
        def _():
            take(jj).wait_recv()
    acc = jnp.zeros((per * v_rows, 128), F32)
    for c in range(v_ref.shape[1] // 128):
        wide = held[:, c * 128:(c + 1) * 128].astype(F32)
        acc = acc + wide * wide
    val_sq = lax.dot_general(
        jnp.ones((ep, 128), F32), acc, NT, precision=lax.Precision.HIGHEST, preferred_element_type=F32
    )

    def score(w, block):
        block = block.astype(BF16).astype(F32)
        for e in range(ex_dev):
            one = [block[(p * ex_dev + e) * k2:(p * ex_dev + e + 1) * k2] for p in range(2)]
            tiled = jnp.where(keep, jnp.concatenate(one * reps, axis=0), 0.0)
            shuf[w, e * 128:(e + 1) * 128, :] = tiled.astype(BF16)
        spread = dot(pick, shuf[w], NT)
        for e in range(ex_dev):
            flat[w, pl.ds(e, picks, stride=ep), :] = spread[:, e * 128:(e + 1) * 128]
        tiles = [flat[w, b * ep:(b + 1) * ep, :] for b in range(picks)]
        train_sq = jnp.zeros((ep, 128), F32)
        for tile in tiles:
            train_sq = train_sq + tile * tile
        train_sq = jnp.sum(train_sq, axis=1, keepdims=True)
        train = jnp.concatenate(tiles, axis=1)
        dots = dot(train.astype(BF16), held[...], NT)
        for jj in range(per):
            span = slice(jj * v_rows, (jj + 1) * v_rows)
            f_send[w, jj] = jnp.concatenate(
                [dots[:, span], val_sq[:, span], jnp.broadcast_to(train_sq, (ep, 128 - 2 * v_rows))],
                axis=1,
            )
        return train

    def report(w, jj):
        return pltpu.make_async_remote_copy(
            src_ref=f_send.at[w, jj], dst_ref=f_recv.at[me], send_sem=fs_sem.at[w, jj], recv_sem=fr_sem.at[me],
            device_id=(grp, mate if w else me_ex, flank * per + jj), device_id_type=MESH,
        )

    def hear(q):
        return pltpu.make_async_remote_copy(
            src_ref=f_recv.at[q], dst_ref=f_recv.at[q], send_sem=fs_sem.at[0, 0], recv_sem=fr_sem.at[q],
            device_id=(grp, me_ex, me), device_id_type=MESH,
        )

    def own_stage():
        block = rows[:, pl.ds(pl.multiple_of(me * kc, 128), kc)]
        for k, share in enumerate(shares):
            share.wait_recv()
            block = block + t_in[k].astype(F32)
        tp_ref[...] = score(0, block)
        for jj in range(per):
            @pl.when(me != flank * per + jj)
            def _():
                report(0, jj).start()

            @pl.when(me == flank * per + jj)
            def _():
                f_recv[me] = f_send[0, jj]

    def mate_stage():
        block = jnp.zeros((ex_dev * pd, kc), F32)
        for k, share in enumerate(across):
            share.wait_recv()
            block = block + t_mate[k].astype(F32)
        score(1, block)
        for jj in range(per):
            report(1, jj).start()

    @pl.when(flank == 0)
    def _():
        own_stage()
        mate_stage()

    @pl.when(flank == 1)
    def _():
        mate_stage()
        own_stage()

    for move in moves + shares + across:
        move.wait_send()
    for i in range(n_ex):
        @pl.when((i != me_ex) & (i % 2 == home))
        def _():
            give(i).wait_send()
    for q in range(n_proj):
        @pl.when((me // per != flank) | (me != q))
        def _():
            hear(q).wait_recv()
    final = f_recv[0]
    for q in range(1, n_proj):
        final = final + f_recv[q]
    sc_ref[...] = final
    for jj in range(per):
        @pl.when(me != flank * per + jj)
        def _():
            report(0, jj).wait_send()

        report(1, jj).wait_send()


def paired_finish(pdim, train_ref, sums_ref, tp_ref, sc_ref):
    ex_dev, cs = sc_ref.shape
    tp_ref[...] = train_ref[:ex_dev, :].astype(BF16)
    final = sums_ref[:ex_dev, :]
    sc_ref[...] = (
        math.sqrt(pdim)
        * final[:, :cs]
        * lax.rsqrt(final[:, 2 * cs:3 * cs] + epsilon)
        * lax.rsqrt(final[:, cs:2 * cs] + epsilon)
    )


def finish(pdim, train_ref, sums_ref, tp_ref, sc_ref):
    ex_dev = tp_ref.shape[0]
    ep = train_ref.shape[0]
    tp_ref[...] = train_ref[:ex_dev, :].astype(BF16)
    final = sums_ref[...]
    scores = (
        math.sqrt(pdim)
        * final[:ep]
        * lax.rsqrt(final[ep + 8:] + epsilon)
        * lax.rsqrt(final[ep:ep + 1] + epsilon)
    )
    sc_ref[...] = scores[:ex_dev]


def shards(
    mesh, inputs, cotangents, lengths, adapter_down_matrix, adapter_up_matrix,
    width_side_sketch, rank_side_sketch, heldout_gradient_rows,
):
    n_ex, n_proj = mesh.shape["ex"], mesh.shape["proj"]
    ex_dev, seq, cols = inputs.shape
    tokens = ex_dev * seq
    rank = adapter_down_matrix.shape[0]
    k1 = width_side_sketch.shape[1]
    k2 = rank_side_sketch.shape[2]
    pd = 2 * k2
    kc = k1 // n_proj
    v_rows, v_cols = heldout_gradient_rows.shape
    nv = v_rows * n_ex
    cs = nv // n_proj
    ep = -(-ex_dev // 8) * 8
    pdim = pd * k1
    any_space = pl.BlockSpec(memory_space=pltpu.HBM)
    vmem = pl.BlockSpec(memory_space=pltpu.VMEM)
    dma = pltpu.SemaphoreType.DMA
    peers = n_proj - 1
    per = n_ex // 2
    paired = (
        n_ex == n_proj and n_ex % 2 == 0 and kc == 128 and 3 * v_rows <= 128 and v_rows % 16 == 0
        and k2 % 8 == 0 and v_cols == kc * pd
    )
    head = [
        pltpu.VMEM((tokens, cols), BF16),
        pltpu.VMEM((tokens, cols), BF16),
        pltpu.VMEM((rank, cols), BF16),
        pltpu.VMEM((cols, rank), BF16),
        pltpu.VMEM((cols, k1), BF16),
    ]
    if paired:
        body, end = paired_kernel, paired_finish
        sums_shape = (ep, 128)
        picks = kc * pd // 128
        firsts = [any_space] * 8
        scratch = head + [
            pltpu.VMEM((2, k2, rank), BF16),
            pltpu.SMEM((ex_dev,), jnp.int32),
            pltpu.VMEM((per * v_rows, v_cols), BF16),
            pltpu.VMEM((2, tokens, k1), BF16),
            pltpu.VMEM((ex_dev * pd, k1), F32),
            pltpu.VMEM((pd, tokens), BF16),
            pltpu.VMEM((peers, pd, tokens), BF16),
            pltpu.VMEM((n_proj, ex_dev * pd, kc), BF16),
            pltpu.VMEM((peers, ex_dev * pd, kc), BF16),
            pltpu.VMEM((n_proj, ex_dev * pd, kc), BF16),
            pltpu.VMEM((2, ex_dev * 128, kc), BF16),
            pltpu.VMEM((2, picks * ep, 128), F32),
            pltpu.VMEM((2, per, ep, 128), F32),
            pltpu.VMEM((n_proj, ep, 128), F32),
            dma((7,)),
            dma((peers,)), dma((peers,)),
            dma((peers,)), dma((peers,)),
            dma((n_proj,)), dma((n_proj,)),
            dma((n_ex,)), dma((per,)),
            dma((2, per)), dma((n_proj,)),
            dma,
            pltpu.SemaphoreType.REGULAR((n_ex,)),
            pltpu.SemaphoreType.REGULAR,
            pltpu.SemaphoreType.REGULAR,
        ]
    else:
        firsts = [pl.BlockSpec(memory_space=pltpu.SMEM)] + [any_space] * 5 + [vmem, any_space]
        chunks = 2 if v_rows % 32 == 0 else 1
        body, end = kernel, finish
        sums_shape = (2 * ep + 8, cs)
        scratch = head + [
            pltpu.VMEM((ex_dev * pd, k1), F32),
            pltpu.VMEM((2, tokens, k1), BF16),
            pltpu.VMEM((n_ex, v_rows, v_cols), BF16),
            pltpu.VMEM((pd, tokens), BF16),
            pltpu.VMEM((peers, pd, tokens), BF16),
            pltpu.VMEM((n_proj, ex_dev * pd, kc), BF16),
            pltpu.VMEM((peers, ex_dev * pd, kc), BF16),
            pltpu.VMEM((ex_dev * 128, kc), BF16),
            pltpu.VMEM((ep, v_cols), F32),
            pltpu.VMEM((nv, 128), F32),
            pltpu.VMEM((n_proj, 2 * ep + 8, cs), F32),
            pltpu.VMEM((peers, 2 * ep + 8, cs), F32),
            dma((5,)),
            dma((peers,)), dma((peers,)),
            dma((peers,)), dma((peers,)),
            dma((peers,)), dma((peers,)),
            dma((2, n_ex - 1, chunks)), dma((2, n_ex - 1, chunks)),
            dma,
        ]
    train, final = pl.pallas_call(
        functools.partial(body, (n_ex, n_proj, ex_dev, seq, pdim)),
        out_shape=(
            pltpu.VMEM((ep, v_cols), F32),
            pltpu.VMEM(sums_shape, F32),
        ),
        in_specs=firsts,
        out_specs=(vmem, vmem),
        scratch_shapes=scratch,
        compiler_params=pltpu.CompilerParams(
            collective_id=0, has_side_effects=True, vmem_limit_bytes=62 * 1024 * 1024
        ),
        name="project",
    )(
        lengths, inputs.reshape(tokens, cols), cotangents.reshape(tokens, cols),
        adapter_down_matrix, adapter_up_matrix, width_side_sketch,
        rank_side_sketch.swapaxes(1, 2), heldout_gradient_rows,
    )
    return pl.pallas_call(
        functools.partial(end, pdim),
        out_shape=(
            jax.ShapeDtypeStruct((ex_dev, v_cols), BF16),
            jax.ShapeDtypeStruct((ex_dev, cs), F32),
        ),
        in_specs=[vmem, vmem],
        out_specs=(vmem, vmem),
        compiler_params=pltpu.CompilerParams(vmem_limit_bytes=8 * 1024 * 1024),
        name="finish",
    )(train, final)


def solution(mesh):
    in_specs = (
        P(("grp", "ex"), None, "proj"),
        P(("grp", "ex"), None, "proj"),
        P(("grp", "ex")),
        P(None, "proj"),
        P("proj", None),
        P("proj", None),
        P(),
        P(("grp", "ex"), "proj"),
    )
    out_specs = (P(("grp", "ex"), "proj"), P(("grp", "ex"), "proj"))
    return jax.shard_map(
        functools.partial(shards, mesh), mesh=mesh, in_specs=in_specs, out_specs=out_specs, check_vma=False
    )
```

```python
import functools
import math

import jax
import jax.numpy as jnp
from jax import lax
from jax.experimental import pallas as pl
from jax.experimental.pallas import tpu as pltpu
from jax.sharding import PartitionSpec as P

epsilon = 1e-06
MESH = pl.DeviceIdType.MESH
F32 = jnp.float32
BF16 = jnp.bfloat16
NT = (((1,), (1,)), ((), ()))


def dot(a, b, dims=(((1,), (0,)), ((), ()))):
    return lax.dot_general(a, b, dims, preferred_element_type=F32)


def kernel(
    sizes,
    len_ref, x_ref, c_ref, a_ref, b_ref, w_ref, r_ref, v_ref,
    tp_ref, sc_ref,
    xb, cb, ab, bb, wb, rows, left, gath,
    right_own, right_in, t_own, t_in, shuf, flat, sums, msg, msg_in,
    load_sem, rs_sem, rr_sem, ts_sem, tr_sem, ms_sem, mr_sem,
    gs_sem, gr_sem, own_sem,
):
    n_ex, n_proj, ex_dev, seq, pdim = sizes
    grp, me_ex, me = lax.axis_index("grp"), lax.axis_index("ex"), lax.axis_index("proj")
    k2 = r_ref.shape[1]
    pd = 2 * k2
    k1 = wb.shape[1]
    kc = k1 // n_proj
    reps = 128 // pd
    blocks = kc * pd // 128

    loads = []
    for i, (src, dst) in enumerate(
        ((a_ref, ab), (x_ref, xb), (b_ref, bb), (c_ref, cb), (w_ref, wb))
    ):
        copy = pltpu.make_async_copy(src, dst, load_sem.at[i])
        copy.start()
        loads.append(copy)
    own = pltpu.make_async_copy(v_ref, gath.at[me_ex], own_sem)
    own.start()

    def peer(k):
        return lax.rem(me + k, n_proj)

    barrier = pltpu.get_barrier_semaphore()
    for k in range(1, n_proj):
        pl.semaphore_signal(barrier, inc=1, device_id=(grp, me_ex, peer(k)), device_id_type=MESH)

    @pl.when(me_ex > 0)
    def _():
        pl.semaphore_signal(barrier, inc=1, device_id=(grp, me_ex - 1, me), device_id_type=MESH)

    @pl.when(me_ex < n_ex - 1)
    def _():
        pl.semaphore_signal(barrier, inc=1, device_id=(grp, me_ex + 1, me), device_id_type=MESH)

    sides = jnp.minimum(me_ex, 1) + jnp.minimum(n_ex - 1 - me_ex, 1)
    pl.semaphore_wait(barrier, n_proj - 1 + sides)

    chunks = gs_sem.shape[2]
    v_rows = gath.shape[1]
    part_rows = v_rows // chunks

    def hop(way, s, c, src=None):
        if way == 0:
            at, to = jnp.maximum(me_ex - s, 0), jnp.minimum(me_ex + 1, n_ex - 1)
        else:
            at, to = jnp.minimum(me_ex + s, n_ex - 1), jnp.maximum(me_ex - 1, 0)
        span = pl.ds(c * part_rows, part_rows)
        here = gath.at[at, span]
        return pltpu.make_async_remote_copy(
            src_ref=here if src is None else src.at[span],
            dst_ref=here,
            send_sem=gs_sem.at[way, s, c],
            recv_sem=gr_sem.at[way, s, c],
            device_id=(grp, to, me),
            device_id_type=MESH,
        )

    def sends(way, s):
        if way == 0:
            return (me_ex - s >= 0) & (me_ex < n_ex - 1)
        return (me_ex + s <= n_ex - 1) & (me_ex > 0)

    def receives(way, s):
        return (me_ex - 1 - s >= 0) if way == 0 else (me_ex + 1 + s <= n_ex - 1)

    def send_own():
        for way in range(2):
            @pl.when(sends(way, 0))
            def _():
                for c in range(chunks):
                    hop(way, 0, c, v_ref).start()

    def squares(at, first, count):
        held = gath[at, pl.ds(first, count)].astype(F32)
        held = held * held
        acc = held[:, :128]
        for c in range(1, gath.shape[2] // 128):
            acc = acc + held[:, c * 128:(c + 1) * 128]
        sums[pl.ds(pl.multiple_of(at * v_rows + first, part_rows), count), :] = acc

    def relay(s, c, forward=True):
        for way in range(2):
            @pl.when(receives(way, s))
            def _():
                hop(way, s, c).wait_recv()

            if forward:
                @pl.when(sends(way, s + 1))
                def _():
                    hop(way, s + 1, c).start()

            @pl.when(receives(way, s))
            def _():
                squares(me_ex - 1 - s if way == 0 else me_ex + 1 + s, c * part_rows, part_rows)

    def end_step(s):
        for way in range(2):
            @pl.when(sends(way, s))
            def _():
                for c in range(chunks):
                    hop(way, s, c).wait_send()

    send_own()

    def swap(k, src, dst, s_sem, r_sem):
        return pltpu.make_async_remote_copy(
            src_ref=src, dst_ref=dst.at[k - 1], send_sem=s_sem.at[k - 1], recv_sem=r_sem.at[k - 1],
            device_id=(grp, me_ex, peer(k)), device_id_type=MESH,
        )

    loads[0].wait()
    m_in = dot(r_ref[0], ab[...]).astype(BF16)
    loads[1].wait()
    part_in = dot(m_in, xb[...], NT)
    loads[2].wait()
    m_out = dot(r_ref[1], bb[...], NT).astype(BF16)
    loads[3].wait()
    part_out = dot(m_out, cb[...], NT)
    part = jnp.concatenate([part_in, part_out], axis=0)
    right_own[...] = part.astype(BF16)
    copies = [swap(k, right_own, right_in, rs_sem, rr_sem) for k in range(1, n_proj)]
    for copy in copies:
        copy.start()

    queue = [(t, c) for t in range(n_ex - 2) for c in range(chunks)] if n_ex <= 4 else []

    def poll():
        if queue:
            relay(*queue.pop(0))

    loads[4].wait()
    half = k1 // 2
    own.wait()
    left[0, :, :half] = dot(cb[...], wb[:, :half]).astype(BF16)
    squares(me_ex, 0, v_rows)
    poll()
    left[0, :, half:] = dot(cb[...], wb[:, half:]).astype(BF16)
    left[1, :, :half] = dot(xb[...], wb[:, :half]).astype(BF16)
    poll()
    left[1, :, half:] = dot(xb[...], wb[:, half:]).astype(BF16)

    for copy in copies:
        copy.wait()
    total = part
    for k in range(n_proj - 1):
        total = total + right_in[k].astype(F32)
    total = total.astype(BF16)

    position = lax.broadcasted_iota(jnp.int32, (k2, seq), 1)
    for e in range(ex_dev):
        live = position < len_ref[e]
        for p in range(2):
            piece = total[p * k2:(p + 1) * k2, e * seq:(e + 1) * seq].astype(F32)
            piece = jnp.where(live, piece, 0.0).astype(BF16)
            rows[e * pd + p * k2:e * pd + (p + 1) * k2, :] = dot(piece, left[p, e * seq:(e + 1) * seq, :])
    for j in range(n_proj):
        t_own[j] = rows[:, j * kc:(j + 1) * kc].astype(BF16)
    copies = [swap(k, t_own.at[peer(k)], t_in, ts_sem, tr_sem) for k in range(1, n_proj)]
    for copy in copies:
        copy.start()

    while queue:
        poll()

    mine = me * kc
    total_t = rows[:, pl.ds(pl.multiple_of(mine, 128), kc)]
    for copy in copies:
        copy.wait()
    for k in range(n_proj - 1):
        total_t = total_t + t_in[k].astype(F32)

    l_at = lax.broadcasted_iota(jnp.int32, (128, kc), 0)
    k_at = lax.broadcasted_iota(jnp.int32, (128, kc), 1)
    keep = (k_at % reps) == (l_at // pd)
    for e in range(ex_dev):
        one = total_t[e * pd:(e + 1) * pd, :] / len_ref[e].astype(F32)
        one = one.astype(BF16).astype(F32)
        tiled = jnp.concatenate([one] * reps, axis=0)
        shuf[e * 128:(e + 1) * 128, :] = jnp.where(keep, tiled, 0.0).astype(BF16)
    b_at = lax.broadcasted_iota(jnp.int32, (blocks, kc), 0)
    s_at = lax.broadcasted_iota(jnp.int32, (blocks, kc), 1)
    pick = jnp.where((s_at // reps) == b_at, 1.0, 0.0).astype(BF16)
    spread = dot(pick, shuf[...], NT)
    ep = flat.shape[0]
    flat[...] = jnp.zeros_like(flat)
    for b in range(blocks):
        for e in range(ex_dev):
            flat[e:e + 1, b * 128:(b + 1) * 128] = spread[b:b + 1, e * 128:(e + 1) * 128]
    train = flat[...]
    train_bf = train.astype(BF16)
    tp_ref[...] = train
    train_sq = jnp.sum(train * train, axis=1, keepdims=True)

    if n_ex > 4:
        @pl.loop(0, n_ex - 2)
        def _(t):
            for c in range(chunks):
                relay(t, c)

    for c in range(chunks):
        relay(n_ex - 2, c, False)
    nv = n_ex * v_rows
    per = 128 // v_rows
    cs = nv // n_proj
    ones = jnp.ones((8, 128), F32)
    dots = jnp.concatenate(
        [dot(train_bf, gath[i * per:(i + 1) * per].reshape(128, gath.shape[2]), NT) for i in range(nv // 128)],
        axis=1,
    )
    val_sq = lax.dot_general(
        ones, sums[...], NT, precision=lax.Precision.HIGHEST, preferred_element_type=F32
    )
    for j in range(n_proj):
        msg[j, :ep] = dots[:, j * cs:(j + 1) * cs]
        msg[j, ep:ep + 8] = val_sq[:, j * cs:(j + 1) * cs]
        msg[j, ep + 8:] = jnp.broadcast_to(train_sq, (ep, cs))
    copies = [swap(k, msg.at[peer(k)], msg_in, ms_sem, mr_sem) for k in range(1, n_proj)]
    for copy in copies:
        copy.start()
    for s in range(n_ex - 1):
        end_step(s)
    final = msg[me]
    for copy in copies:
        copy.wait()
    for k in range(n_proj - 1):
        final = final + msg_in[k]
    sc_ref[...] = final


def paired_kernel(
    sizes,
    len_hbm, x_ref, c_ref, a_ref, b_ref, w_ref, r_hbm, v_ref,
    tp_ref, sc_ref,
    xb, cb, ab, bb, wb, r_ref, len_ref, held, left, rows, right_own, right_in, t_send, t_in, t_mate, shuf, flat, f_send, f_recv,
    load_sem, rs_sem, rr_sem, ts_sem, tr_sem, us_sem, ur_sem, hs_sem, hr_sem, fs_sem, fr_sem, own_sem, ready, met, near,
):
    n_ex, n_proj, ex_dev, seq, pdim = sizes
    grp, me_ex, me = lax.axis_index("grp"), lax.axis_index("ex"), lax.axis_index("proj")
    flank = lax.rem(me_ex, 2)
    mate = me_ex + 1 - 2 * flank
    per = n_ex // 2
    home, slot = me_ex // per, lax.rem(me_ex, per)
    k2 = r_ref.shape[1]
    pd = 2 * k2
    kc = wb.shape[1] // n_proj
    reps = 128 // pd
    picks = kc // reps
    v_rows = v_ref.shape[0]
    ep = flat.shape[1] // picks
    tokens = ex_dev * seq

    def peer(k):
        return lax.rem(me + k, n_proj)

    barrier = pltpu.get_barrier_semaphore()

    def greet(i, at):
        pl.semaphore_signal(barrier, inc=1, device_id=(grp, i, at), device_id_type=MESH)

    loads = []
    for i, (src, dst) in enumerate(
        ((r_hbm, r_ref), (a_ref, ab), (b_ref, bb), (x_ref, xb), (c_ref, cb), (w_ref, wb), (len_hbm, len_ref))
    ):
        copy = pltpu.make_async_copy(src, dst, load_sem.at[i])
        copy.start()
        loads.append(copy)
    for q in range(1, n_proj):
        @pl.when(q > me)
        def _():
            greet(me_ex, q)
    for i in range(1, n_ex):
        @pl.when(i > me_ex)
        def _():
            greet(i, me)

    @pl.when(flank == 0)
    def _():
        for k in range(1, n_proj):
            greet(mate, peer(k))
    expected = me + me_ex + flank * (n_proj - 1)

    def place(jj):
        return held.at[pl.ds(jj * v_rows, v_rows)]

    own = pltpu.make_async_copy(v_ref, place(slot), own_sem)

    @pl.when(home == flank)
    def _():
        own.start()

    def give(i):
        return pltpu.make_async_remote_copy(
            src_ref=v_ref, dst_ref=place(slot), send_sem=hs_sem.at[i], recv_sem=hr_sem.at[slot],
            device_id=(grp, i, me), device_id_type=MESH,
        )

    def take(jj):
        return pltpu.make_async_remote_copy(
            src_ref=place(jj), dst_ref=place(jj), send_sem=hs_sem.at[0], recv_sem=hr_sem.at[jj],
            device_id=(grp, me_ex, me), device_id_type=MESH,
        )

    def pass_on(k, src, dst, s_sem, r_sem):
        return pltpu.make_async_remote_copy(
            src_ref=src, dst_ref=dst.at[k], send_sem=s_sem.at[k], recv_sem=r_sem.at[k],
            device_id=(grp, mate, peer(k)), device_id_type=MESH,
        )

    def swap(k, src, dst, s_sem, r_sem):
        return pltpu.make_async_remote_copy(
            src_ref=src, dst_ref=dst.at[k - 1], send_sem=s_sem.at[k - 1], recv_sem=r_sem.at[k - 1],
            device_id=(grp, me_ex, peer(k)), device_id_type=MESH,
        )

    @pl.when(expected > 0)
    def _():
        pl.semaphore_wait(barrier, expected)

    for j in range(n_ex - 1):
        @pl.when((j < me_ex) & (j // per == flank))
        def _():
            pl.semaphore_signal(
                ready.at[me_ex], inc=1, device_id=(grp, j, me), device_id_type=MESH
            )

    for i in range(n_ex - 1):
        @pl.when((i < me_ex) & (i % 2 == home))
        def _():
            give(i).start()

    @pl.when(flank == 1)
    def _():
        for k in range(n_proj):
            pl.semaphore_signal(
                met, inc=1, device_id=(grp, mate, peer(k)), device_id_type=MESH
            )

    for q in range(n_proj - 1):
        @pl.when(q < me)
        def _():
            pl.semaphore_signal(near, inc=1, device_id=(grp, me_ex, q), device_id_type=MESH)

    flat[...] = jnp.zeros_like(flat)
    for copy in loads[:3]:
        copy.wait()
    m_in = dot(r_ref[0], ab[...]).astype(BF16)
    m_out = dot(r_ref[1], bb[...], NT).astype(BF16)
    loads[3].wait()
    part_in = dot(m_in, xb[...], NT)
    right_own[0] = part_in.astype(BF16)

    @pl.when(me < n_proj - 1)
    def _():
        pl.semaphore_wait(near, n_proj - 1 - me)

    def share_right(p):
        started = [
            swap(k, right_own.at[p], right_in.at[p], rs_sem.at[p], rr_sem.at[p]) for k in range(1, n_proj)
        ]
        for move in started:
            move.start()
        return started

    moves = [share_right(0)]
    def give_later(k):
        for i in range(k, n_ex):
            @pl.when((i == me_ex + k) & (i % 2 == home))
            def _():
                pl.semaphore_wait(ready.at[i], 1)
                give(i).start()

    @pl.when(flank == 1)
    def _():
        give_later(1)

    loads[4].wait()
    part_out = dot(m_out, cb[...], NT)
    right_own[1] = part_out.astype(BF16)
    moves.append(share_right(1))

    @pl.when(flank == 0)
    def _():
        give_later(1)

    for k in range(2, n_ex):
        give_later(k)
    loads[5].wait()
    left[0] = dot(cb[...], wb[...]).astype(BF16)
    left[1] = dot(xb[...], wb[...]).astype(BF16)

    loads[6].wait()
    position = lax.broadcasted_iota(jnp.int32, (k2, tokens), 1)
    live = []
    scale = []
    for e in range(ex_dev):
        count = len_ref[e]
        live.append((position >= e * seq) & (position < e * seq + count))
        scale.append(1.0 / jnp.full((k2, 128), count.astype(F32), F32))

    result = []
    for p, piece in enumerate((part_in, part_out)):
        for k, move in enumerate(moves[p]):
            move.wait_recv()
            piece = piece + right_in[p, k].astype(F32)
        piece = piece.astype(BF16).astype(F32)
        spread = jnp.concatenate([jnp.where(one, piece, 0.0) for one in live], axis=0).astype(BF16)
        result.append(dot(spread, left[p]))
    result = jnp.concatenate(result, axis=0)
    for p in range(2):
        for e in range(ex_dev):
            at = (p * ex_dev + e) * k2
            for q in range(n_proj):
                rows[at:at + k2, q * kc:(q + 1) * kc] = result[at:at + k2, q * kc:(q + 1) * kc] * scale[e]
    for q in range(n_proj):
        t_send[q] = rows[:, q * kc:(q + 1) * kc].astype(BF16)
    shares = [swap(k, t_send.at[peer(k)], t_in, ts_sem, tr_sem) for k in range(1, n_proj)]
    across = [pass_on(k, t_send.at[peer(k)], t_mate, us_sem, ur_sem) for k in range(n_proj)]

    @pl.when(flank == 1)
    def _():
        for share in (across[2], across[1], across[3], across[0]):
            share.start()

    for share in shares:
        share.start()

    @pl.when(flank == 0)
    def _():
        pl.semaphore_wait(met, n_proj)
        for share in across:
            share.start()

    l_at = lax.broadcasted_iota(jnp.int32, (128, kc), 0)
    k_at = lax.broadcasted_iota(jnp.int32, (128, kc), 1)
    keep = (k_at % reps) == (l_at // pd)
    b_at = lax.broadcasted_iota(jnp.int32, (picks, kc), 0)
    s_at = lax.broadcasted_iota(jnp.int32, (picks, kc), 1)
    pick = jnp.where((s_at // reps) == b_at, 1.0, 0.0).astype(BF16)

    for jj in range(per):
        @pl.when(flank * per + jj == me_ex)
        def _():
            own.wait()

        @pl.when(flank * per + jj != me_ex)
        def _():
            take(jj).wait_recv()
    acc = jnp.zeros((per * v_rows, 128), F32)
    for c in range(v_ref.shape[1] // 128):
        wide = held[:, c * 128:(c + 1) * 128].astype(F32)
        acc = acc + wide * wide
    val_sq = lax.dot_general(
        jnp.ones((ep, 128), F32), acc, NT, precision=lax.Precision.HIGHEST, preferred_element_type=F32
    )

    def score(w, block):
        block = block.astype(BF16).astype(F32)
        for e in range(ex_dev):
            one = [block[(p * ex_dev + e) * k2:(p * ex_dev + e + 1) * k2] for p in range(2)]
            tiled = jnp.where(keep, jnp.concatenate(one * reps, axis=0), 0.0)
            shuf[w, e * 128:(e + 1) * 128, :] = tiled.astype(BF16)
        spread = dot(pick, shuf[w], NT)
        for e in range(ex_dev):
            flat[w, pl.ds(e, picks, stride=ep), :] = spread[:, e * 128:(e + 1) * 128]
        tiles = [flat[w, b * ep:(b + 1) * ep, :] for b in range(picks)]
        train_sq = jnp.zeros((ep, 128), F32)
        for tile in tiles:
            train_sq = train_sq + tile * tile
        train_sq = jnp.sum(train_sq, axis=1, keepdims=True)
        train = jnp.concatenate(tiles, axis=1)
        dots = dot(train.astype(BF16), held[...], NT)
        for jj in range(per):
            span = slice(jj * v_rows, (jj + 1) * v_rows)
            f_send[w, jj] = jnp.concatenate(
                [dots[:, span], val_sq[:, span], jnp.broadcast_to(train_sq, (ep, 128 - 2 * v_rows))],
                axis=1,
            )
        return train

    def report(w, jj):
        return pltpu.make_async_remote_copy(
            src_ref=f_send.at[w, jj], dst_ref=f_recv.at[me], send_sem=fs_sem.at[w, jj], recv_sem=fr_sem.at[me],
            device_id=(grp, mate if w else me_ex, flank * per + jj), device_id_type=MESH,
        )

    def hear(q):
        return pltpu.make_async_remote_copy(
            src_ref=f_recv.at[q], dst_ref=f_recv.at[q], send_sem=fs_sem.at[0, 0], recv_sem=fr_sem.at[q],
            device_id=(grp, me_ex, me), device_id_type=MESH,
        )

    def own_stage():
        block = rows[:, pl.ds(pl.multiple_of(me * kc, 128), kc)]
        for k, share in enumerate(shares):
            share.wait_recv()
            block = block + t_in[k].astype(F32)
        tp_ref[...] = score(0, block)
        for jj in range(per):
            @pl.when(me != flank * per + jj)
            def _():
                report(0, jj).start()

            @pl.when(me == flank * per + jj)
            def _():
                f_recv[me] = f_send[0, jj]

    def mate_stage():
        block = jnp.zeros((ex_dev * pd, kc), F32)
        for k, share in enumerate(across):
            share.wait_recv()
            block = block + t_mate[k].astype(F32)
        score(1, block)
        for jj in range(per):
            report(1, jj).start()

    @pl.when(flank == 0)
    def _():
        own_stage()
        mate_stage()

    @pl.when(flank == 1)
    def _():
        mate_stage()
        own_stage()

    for move in moves[0] + moves[1] + shares + across:
        move.wait_send()
    for i in range(n_ex):
        @pl.when((i != me_ex) & (i % 2 == home))
        def _():
            give(i).wait_send()
    for q in range(n_proj):
        @pl.when((me // per != flank) | (me != q))
        def _():
            hear(q).wait_recv()
    final = f_recv[0]
    for q in range(1, n_proj):
        final = final + f_recv[q]
    sc_ref[...] = final
    for jj in range(per):
        @pl.when(me != flank * per + jj)
        def _():
            report(0, jj).wait_send()

        report(1, jj).wait_send()


def paired_finish(pdim, train_ref, sums_ref, tp_ref, sc_ref):
    ex_dev, cs = sc_ref.shape
    tp_ref[...] = train_ref[:ex_dev, :].astype(BF16)
    final = sums_ref[:ex_dev, :]
    sc_ref[...] = (
        math.sqrt(pdim)
        * final[:, :cs]
        * lax.rsqrt(final[:, 2 * cs:3 * cs] + epsilon)
        * lax.rsqrt(final[:, cs:2 * cs] + epsilon)
    )


def finish(pdim, train_ref, sums_ref, tp_ref, sc_ref):
    ex_dev = tp_ref.shape[0]
    ep = train_ref.shape[0]
    tp_ref[...] = train_ref[:ex_dev, :].astype(BF16)
    final = sums_ref[...]
    scores = (
        math.sqrt(pdim)
        * final[:ep]
        * lax.rsqrt(final[ep + 8:] + epsilon)
        * lax.rsqrt(final[ep:ep + 1] + epsilon)
    )
    sc_ref[...] = scores[:ex_dev]


def shards(
    mesh, inputs, cotangents, lengths, adapter_down_matrix, adapter_up_matrix,
    width_side_sketch, rank_side_sketch, heldout_gradient_rows,
):
    n_ex, n_proj = mesh.shape["ex"], mesh.shape["proj"]
    ex_dev, seq, cols = inputs.shape
    tokens = ex_dev * seq
    rank = adapter_down_matrix.shape[0]
    k1 = width_side_sketch.shape[1]
    k2 = rank_side_sketch.shape[2]
    pd = 2 * k2
    kc = k1 // n_proj
    v_rows, v_cols = heldout_gradient_rows.shape
    nv = v_rows * n_ex
    cs = nv // n_proj
    ep = -(-ex_dev // 8) * 8
    pdim = pd * k1
    any_space = pl.BlockSpec(memory_space=pltpu.HBM)
    vmem = pl.BlockSpec(memory_space=pltpu.VMEM)
    dma = pltpu.SemaphoreType.DMA
    peers = n_proj - 1
    per = n_ex // 2
    paired = (
        n_ex == n_proj and n_ex % 2 == 0 and kc == 128 and 3 * v_rows <= 128 and v_rows % 16 == 0
        and k2 % 8 == 0 and v_cols == kc * pd
    )
    head = [
        pltpu.VMEM((tokens, cols), BF16),
        pltpu.VMEM((tokens, cols), BF16),
        pltpu.VMEM((rank, cols), BF16),
        pltpu.VMEM((cols, rank), BF16),
        pltpu.VMEM((cols, k1), BF16),
    ]
    if paired:
        body, end = paired_kernel, paired_finish
        sums_shape = (ep, 128)
        picks = kc * pd // 128
        firsts = [any_space] * 8
        scratch = head + [
            pltpu.VMEM((2, k2, rank), BF16),
            pltpu.SMEM((ex_dev,), jnp.int32),
            pltpu.VMEM((per * v_rows, v_cols), BF16),
            pltpu.VMEM((2, tokens, k1), BF16),
            pltpu.VMEM((ex_dev * pd, k1), F32),
            pltpu.VMEM((2, k2, tokens), BF16),
            pltpu.VMEM((2, peers, k2, tokens), BF16),
            pltpu.VMEM((n_proj, ex_dev * pd, kc), BF16),
            pltpu.VMEM((peers, ex_dev * pd, kc), BF16),
            pltpu.VMEM((n_proj, ex_dev * pd, kc), BF16),
            pltpu.VMEM((2, ex_dev * 128, kc), BF16),
            pltpu.VMEM((2, picks * ep, 128), F32),
            pltpu.VMEM((2, per, ep, 128), F32),
            pltpu.VMEM((n_proj, ep, 128), F32),
            dma((7,)),
            dma((2, peers)), dma((2, peers)),
            dma((peers,)), dma((peers,)),
            dma((n_proj,)), dma((n_proj,)),
            dma((n_ex,)), dma((per,)),
            dma((2, per)), dma((n_proj,)),
            dma,
            pltpu.SemaphoreType.REGULAR((n_ex,)),
            pltpu.SemaphoreType.REGULAR,
            pltpu.SemaphoreType.REGULAR,
        ]
    else:
        firsts = [pl.BlockSpec(memory_space=pltpu.SMEM)] + [any_space] * 5 + [vmem, any_space]
        chunks = 2 if v_rows % 32 == 0 else 1
        body, end = kernel, finish
        sums_shape = (2 * ep + 8, cs)
        scratch = head + [
            pltpu.VMEM((ex_dev * pd, k1), F32),
            pltpu.VMEM((2, tokens, k1), BF16),
            pltpu.VMEM((n_ex, v_rows, v_cols), BF16),
            pltpu.VMEM((pd, tokens), BF16),
            pltpu.VMEM((peers, pd, tokens), BF16),
            pltpu.VMEM((n_proj, ex_dev * pd, kc), BF16),
            pltpu.VMEM((peers, ex_dev * pd, kc), BF16),
            pltpu.VMEM((ex_dev * 128, kc), BF16),
            pltpu.VMEM((ep, v_cols), F32),
            pltpu.VMEM((nv, 128), F32),
            pltpu.VMEM((n_proj, 2 * ep + 8, cs), F32),
            pltpu.VMEM((peers, 2 * ep + 8, cs), F32),
            dma((5,)),
            dma((peers,)), dma((peers,)),
            dma((peers,)), dma((peers,)),
            dma((peers,)), dma((peers,)),
            dma((2, n_ex - 1, chunks)), dma((2, n_ex - 1, chunks)),
            dma,
        ]
    train, final = pl.pallas_call(
        functools.partial(body, (n_ex, n_proj, ex_dev, seq, pdim)),
        out_shape=(
            pltpu.VMEM((ep, v_cols), F32),
            pltpu.VMEM(sums_shape, F32),
        ),
        in_specs=firsts,
        out_specs=(vmem, vmem),
        scratch_shapes=scratch,
        compiler_params=pltpu.CompilerParams(
            collective_id=0, has_side_effects=True, vmem_limit_bytes=62 * 1024 * 1024
        ),
        name="project",
    )(
        lengths, inputs.reshape(tokens, cols), cotangents.reshape(tokens, cols),
        adapter_down_matrix, adapter_up_matrix, width_side_sketch,
        rank_side_sketch.swapaxes(1, 2), heldout_gradient_rows,
    )
    return pl.pallas_call(
        functools.partial(end, pdim),
        out_shape=(
            jax.ShapeDtypeStruct((ex_dev, v_cols), BF16),
            jax.ShapeDtypeStruct((ex_dev, cs), F32),
        ),
        in_specs=[vmem, vmem],
        out_specs=(vmem, vmem),
        compiler_params=pltpu.CompilerParams(vmem_limit_bytes=8 * 1024 * 1024),
        name="finish",
    )(train, final)


def solution(mesh):
    in_specs = (
        P(("grp", "ex"), None, "proj"),
        P(("grp", "ex"), None, "proj"),
        P(("grp", "ex")),
        P(None, "proj"),
        P("proj", None),
        P("proj", None),
        P(),
        P(("grp", "ex"), "proj"),
    )
    out_specs = (P(("grp", "ex"), "proj"), P(("grp", "ex"), "proj"))
    return jax.shard_map(
        functools.partial(shards, mesh), mesh=mesh, in_specs=in_specs, out_specs=out_specs, check_vma=False
    )
```

```python
import functools
import math

import jax
import jax.numpy as jnp
from jax import lax
from jax.experimental import pallas as pl
from jax.experimental.pallas import tpu as pltpu
from jax.sharding import PartitionSpec as P

epsilon = 1e-06
MESH = pl.DeviceIdType.MESH
F32 = jnp.float32
BF16 = jnp.bfloat16
NT = (((1,), (1,)), ((), ()))


def dot(a, b, dims=(((1,), (0,)), ((), ()))):
    return lax.dot_general(a, b, dims, preferred_element_type=F32)


def kernel(
    sizes,
    len_ref, x_ref, c_ref, a_ref, b_ref, w_ref, r_ref, v_ref,
    tp_ref, sc_ref,
    xb, cb, ab, bb, wb, rows, left, gath,
    right_own, right_in, t_own, t_in, shuf, flat, sums, msg, msg_in,
    load_sem, rs_sem, rr_sem, ts_sem, tr_sem, ms_sem, mr_sem,
    gs_sem, gr_sem, own_sem,
):
    n_ex, n_proj, ex_dev, seq, pdim = sizes
    grp, me_ex, me = lax.axis_index("grp"), lax.axis_index("ex"), lax.axis_index("proj")
    k2 = r_ref.shape[1]
    pd = 2 * k2
    k1 = wb.shape[1]
    kc = k1 // n_proj
    reps = 128 // pd
    blocks = kc * pd // 128

    loads = []
    for i, (src, dst) in enumerate(
        ((a_ref, ab), (x_ref, xb), (b_ref, bb), (c_ref, cb), (w_ref, wb))
    ):
        copy = pltpu.make_async_copy(src, dst, load_sem.at[i])
        copy.start()
        loads.append(copy)
    own = pltpu.make_async_copy(v_ref, gath.at[me_ex], own_sem)
    own.start()

    def peer(k):
        return lax.rem(me + k, n_proj)

    barrier = pltpu.get_barrier_semaphore()
    for k in range(1, n_proj):
        pl.semaphore_signal(barrier, inc=1, device_id=(grp, me_ex, peer(k)), device_id_type=MESH)

    @pl.when(me_ex > 0)
    def _():
        pl.semaphore_signal(barrier, inc=1, device_id=(grp, me_ex - 1, me), device_id_type=MESH)

    @pl.when(me_ex < n_ex - 1)
    def _():
        pl.semaphore_signal(barrier, inc=1, device_id=(grp, me_ex + 1, me), device_id_type=MESH)

    sides = jnp.minimum(me_ex, 1) + jnp.minimum(n_ex - 1 - me_ex, 1)
    pl.semaphore_wait(barrier, n_proj - 1 + sides)

    chunks = gs_sem.shape[2]
    v_rows = gath.shape[1]
    part_rows = v_rows // chunks

    def hop(way, s, c, src=None):
        if way == 0:
            at, to = jnp.maximum(me_ex - s, 0), jnp.minimum(me_ex + 1, n_ex - 1)
        else:
            at, to = jnp.minimum(me_ex + s, n_ex - 1), jnp.maximum(me_ex - 1, 0)
        span = pl.ds(c * part_rows, part_rows)
        here = gath.at[at, span]
        return pltpu.make_async_remote_copy(
            src_ref=here if src is None else src.at[span],
            dst_ref=here,
            send_sem=gs_sem.at[way, s, c],
            recv_sem=gr_sem.at[way, s, c],
            device_id=(grp, to, me),
            device_id_type=MESH,
        )

    def sends(way, s):
        if way == 0:
            return (me_ex - s >= 0) & (me_ex < n_ex - 1)
        return (me_ex + s <= n_ex - 1) & (me_ex > 0)

    def receives(way, s):
        return (me_ex - 1 - s >= 0) if way == 0 else (me_ex + 1 + s <= n_ex - 1)

    def send_own():
        for way in range(2):
            @pl.when(sends(way, 0))
            def _():
                for c in range(chunks):
                    hop(way, 0, c, v_ref).start()

    def squares(at, first, count):
        held = gath[at, pl.ds(first, count)].astype(F32)
        held = held * held
        acc = held[:, :128]
        for c in range(1, gath.shape[2] // 128):
            acc = acc + held[:, c * 128:(c + 1) * 128]
        sums[pl.ds(pl.multiple_of(at * v_rows + first, part_rows), count), :] = acc

    def relay(s, c, forward=True):
        for way in range(2):
            @pl.when(receives(way, s))
            def _():
                hop(way, s, c).wait_recv()

            if forward:
                @pl.when(sends(way, s + 1))
                def _():
                    hop(way, s + 1, c).start()

            @pl.when(receives(way, s))
            def _():
                squares(me_ex - 1 - s if way == 0 else me_ex + 1 + s, c * part_rows, part_rows)

    def end_step(s):
        for way in range(2):
            @pl.when(sends(way, s))
            def _():
                for c in range(chunks):
                    hop(way, s, c).wait_send()

    send_own()

    def swap(k, src, dst, s_sem, r_sem):
        return pltpu.make_async_remote_copy(
            src_ref=src, dst_ref=dst.at[k - 1], send_sem=s_sem.at[k - 1], recv_sem=r_sem.at[k - 1],
            device_id=(grp, me_ex, peer(k)), device_id_type=MESH,
        )

    loads[0].wait()
    m_in = dot(r_ref[0], ab[...]).astype(BF16)
    loads[1].wait()
    part_in = dot(m_in, xb[...], NT)
    loads[2].wait()
    m_out = dot(r_ref[1], bb[...], NT).astype(BF16)
    loads[3].wait()
    part_out = dot(m_out, cb[...], NT)
    part = jnp.concatenate([part_in, part_out], axis=0)
    right_own[...] = part.astype(BF16)
    copies = [swap(k, right_own, right_in, rs_sem, rr_sem) for k in range(1, n_proj)]
    for copy in copies:
        copy.start()

    queue = [(t, c) for t in range(n_ex - 2) for c in range(chunks)] if n_ex <= 4 else []

    def poll():
        if queue:
            relay(*queue.pop(0))

    loads[4].wait()
    half = k1 // 2
    own.wait()
    left[0, :, :half] = dot(cb[...], wb[:, :half]).astype(BF16)
    squares(me_ex, 0, v_rows)
    poll()
    left[0, :, half:] = dot(cb[...], wb[:, half:]).astype(BF16)
    left[1, :, :half] = dot(xb[...], wb[:, :half]).astype(BF16)
    poll()
    left[1, :, half:] = dot(xb[...], wb[:, half:]).astype(BF16)

    for copy in copies:
        copy.wait()
    total = part
    for k in range(n_proj - 1):
        total = total + right_in[k].astype(F32)
    total = total.astype(BF16)

    position = lax.broadcasted_iota(jnp.int32, (k2, seq), 1)
    for e in range(ex_dev):
        live = position < len_ref[e]
        for p in range(2):
            piece = total[p * k2:(p + 1) * k2, e * seq:(e + 1) * seq].astype(F32)
            piece = jnp.where(live, piece, 0.0).astype(BF16)
            rows[e * pd + p * k2:e * pd + (p + 1) * k2, :] = dot(piece, left[p, e * seq:(e + 1) * seq, :])
    for j in range(n_proj):
        t_own[j] = rows[:, j * kc:(j + 1) * kc].astype(BF16)
    copies = [swap(k, t_own.at[peer(k)], t_in, ts_sem, tr_sem) for k in range(1, n_proj)]
    for copy in copies:
        copy.start()

    while queue:
        poll()

    mine = me * kc
    total_t = rows[:, pl.ds(pl.multiple_of(mine, 128), kc)]
    for copy in copies:
        copy.wait()
    for k in range(n_proj - 1):
        total_t = total_t + t_in[k].astype(F32)

    l_at = lax.broadcasted_iota(jnp.int32, (128, kc), 0)
    k_at = lax.broadcasted_iota(jnp.int32, (128, kc), 1)
    keep = (k_at % reps) == (l_at // pd)
    for e in range(ex_dev):
        one = total_t[e * pd:(e + 1) * pd, :] / len_ref[e].astype(F32)
        one = one.astype(BF16).astype(F32)
        tiled = jnp.concatenate([one] * reps, axis=0)
        shuf[e * 128:(e + 1) * 128, :] = jnp.where(keep, tiled, 0.0).astype(BF16)
    b_at = lax.broadcasted_iota(jnp.int32, (blocks, kc), 0)
    s_at = lax.broadcasted_iota(jnp.int32, (blocks, kc), 1)
    pick = jnp.where((s_at // reps) == b_at, 1.0, 0.0).astype(BF16)
    spread = dot(pick, shuf[...], NT)
    ep = flat.shape[0]
    flat[...] = jnp.zeros_like(flat)
    for b in range(blocks):
        for e in range(ex_dev):
            flat[e:e + 1, b * 128:(b + 1) * 128] = spread[b:b + 1, e * 128:(e + 1) * 128]
    train = flat[...]
    train_bf = train.astype(BF16)
    tp_ref[...] = train
    train_sq = jnp.sum(train * train, axis=1, keepdims=True)

    if n_ex > 4:
        @pl.loop(0, n_ex - 2)
        def _(t):
            for c in range(chunks):
                relay(t, c)

    for c in range(chunks):
        relay(n_ex - 2, c, False)
    nv = n_ex * v_rows
    per = 128 // v_rows
    cs = nv // n_proj
    ones = jnp.ones((8, 128), F32)
    dots = jnp.concatenate(
        [dot(train_bf, gath[i * per:(i + 1) * per].reshape(128, gath.shape[2]), NT) for i in range(nv // 128)],
        axis=1,
    )
    val_sq = lax.dot_general(
        ones, sums[...], NT, precision=lax.Precision.HIGHEST, preferred_element_type=F32
    )
    for j in range(n_proj):
        msg[j, :ep] = dots[:, j * cs:(j + 1) * cs]
        msg[j, ep:ep + 8] = val_sq[:, j * cs:(j + 1) * cs]
        msg[j, ep + 8:] = jnp.broadcast_to(train_sq, (ep, cs))
    copies = [swap(k, msg.at[peer(k)], msg_in, ms_sem, mr_sem) for k in range(1, n_proj)]
    for copy in copies:
        copy.start()
    for s in range(n_ex - 1):
        end_step(s)
    final = msg[me]
    for copy in copies:
        copy.wait()
    for k in range(n_proj - 1):
        final = final + msg_in[k]
    sc_ref[...] = final


def paired_kernel(
    sizes,
    len_hbm, x_ref, c_ref, a_ref, b_ref, w_ref, r_hbm, v_ref,
    tp_ref, sc_ref,
    xb, cb, ab, bb, wb, r_ref, len_ref, held, left, rows, right_own, right_in, t_send, t_in, t_mate, shuf, flat, f_send, f_recv,
    load_sem, rs_sem, rr_sem, ts_sem, tr_sem, us_sem, ur_sem, hs_sem, hr_sem, fs_sem, fr_sem, own_sem, ready, met, near,
):
    n_ex, n_proj, ex_dev, seq, pdim = sizes
    grp, me_ex, me = lax.axis_index("grp"), lax.axis_index("ex"), lax.axis_index("proj")
    flank = lax.rem(me_ex, 2)
    mate = me_ex + 1 - 2 * flank
    per = n_ex // 2
    home, slot = me_ex // per, lax.rem(me_ex, per)
    k2 = r_ref.shape[1]
    pd = 2 * k2
    kc = wb.shape[1] // n_proj
    reps = 128 // pd
    picks = kc // reps
    v_rows = v_ref.shape[0]
    ep = flat.shape[1] // picks
    tokens = ex_dev * seq

    def peer(k):
        return lax.rem(me + k, n_proj)

    barrier = pltpu.get_barrier_semaphore()

    def greet(i, at):
        pl.semaphore_signal(barrier, inc=1, device_id=(grp, i, at), device_id_type=MESH)

    loads = []
    for i, (src, dst) in enumerate(
        ((r_hbm, r_ref), (a_ref, ab), (b_ref, bb), (x_ref, xb), (c_ref, cb), (w_ref, wb), (len_hbm, len_ref))
    ):
        copy = pltpu.make_async_copy(src, dst, load_sem.at[i])
        copy.start()
        loads.append(copy)
    for q in range(1, n_proj):
        @pl.when(q > me)
        def _():
            greet(me_ex, q)
    for i in range(1, n_ex):
        @pl.when(i > me_ex)
        def _():
            greet(i, me)

    @pl.when(flank == 0)
    def _():
        for k in range(1, n_proj):
            greet(mate, peer(k))
    expected = me + me_ex + flank * (n_proj - 1)

    def place(jj):
        return held.at[pl.ds(jj * v_rows, v_rows)]

    own = pltpu.make_async_copy(v_ref, place(slot), own_sem)

    @pl.when(home == flank)
    def _():
        own.start()

    def give(i):
        return pltpu.make_async_remote_copy(
            src_ref=v_ref, dst_ref=place(slot), send_sem=hs_sem.at[i], recv_sem=hr_sem.at[slot],
            device_id=(grp, i, me), device_id_type=MESH,
        )

    def take(jj):
        return pltpu.make_async_remote_copy(
            src_ref=place(jj), dst_ref=place(jj), send_sem=hs_sem.at[0], recv_sem=hr_sem.at[jj],
            device_id=(grp, me_ex, me), device_id_type=MESH,
        )

    def pass_on(k, src, dst, s_sem, r_sem):
        return pltpu.make_async_remote_copy(
            src_ref=src, dst_ref=dst.at[k], send_sem=s_sem.at[k], recv_sem=r_sem.at[k],
            device_id=(grp, mate, peer(k)), device_id_type=MESH,
        )

    def swap(k, src, dst, s_sem, r_sem):
        return pltpu.make_async_remote_copy(
            src_ref=src, dst_ref=dst.at[k - 1], send_sem=s_sem.at[k - 1], recv_sem=r_sem.at[k - 1],
            device_id=(grp, me_ex, peer(k)), device_id_type=MESH,
        )

    @pl.when(expected > 0)
    def _():
        pl.semaphore_wait(barrier, expected)

    for j in range(n_ex - 1):
        @pl.when((j < me_ex) & (j // per == flank))
        def _():
            pl.semaphore_signal(
                ready.at[me_ex], inc=1, device_id=(grp, j, me), device_id_type=MESH
            )

    for i in range(n_ex - 1):
        @pl.when((i < me_ex) & (i % 2 == home))
        def _():
            give(i).start()

    @pl.when(flank == 1)
    def _():
        for k in range(n_proj):
            pl.semaphore_signal(
                met, inc=1, device_id=(grp, mate, peer(k)), device_id_type=MESH
            )

    for q in range(n_proj - 1):
        @pl.when(q < me)
        def _():
            pl.semaphore_signal(near, inc=1, device_id=(grp, me_ex, q), device_id_type=MESH)

    flat[...] = jnp.zeros_like(flat)
    for copy in loads[:3]:
        copy.wait()
    m_in = dot(r_ref[0], ab[...]).astype(BF16)
    m_out = dot(r_ref[1], bb[...], NT).astype(BF16)
    loads[3].wait()
    part_in = dot(m_in, xb[...], NT)
    right_own[0] = part_in.astype(BF16)

    @pl.when(me < n_proj - 1)
    def _():
        pl.semaphore_wait(near, n_proj - 1 - me)

    def share_right(p):
        started = [
            swap(k, right_own.at[p], right_in.at[p], rs_sem.at[p], rr_sem.at[p]) for k in range(1, n_proj)
        ]
        for move in started:
            move.start()
        return started

    moves = [share_right(0)]
    def give_later(k):
        for i in range(k, n_ex):
            @pl.when((i == me_ex + k) & (i % 2 == home))
            def _():
                pl.semaphore_wait(ready.at[i], 1)
                give(i).start()

    @pl.when(flank == 1)
    def _():
        give_later(1)

    loads[4].wait()
    part_out = dot(m_out, cb[...], NT)
    right_own[1] = part_out.astype(BF16)
    moves.append(share_right(1))

    @pl.when(flank == 0)
    def _():
        give_later(1)

    for k in range(2, n_ex):
        give_later(k)
    loads[5].wait()
    left[0] = dot(cb[...], wb[...]).astype(BF16)
    left[1] = dot(xb[...], wb[...]).astype(BF16)

    loads[6].wait()
    position = lax.broadcasted_iota(jnp.int32, (k2, tokens), 1)
    live = []
    scale = []
    for e in range(ex_dev):
        count = len_ref[e]
        live.append((position >= e * seq) & (position < e * seq + count))
        scale.append(1.0 / jnp.full((k2, 128), count.astype(F32), F32))

    result = []
    for p, piece in enumerate((part_in, part_out)):
        for k, move in enumerate(moves[p]):
            move.wait_recv()
            piece = piece + right_in[p, k].astype(F32)
        piece = piece.astype(BF16).astype(F32)
        spread = jnp.concatenate([jnp.where(one, piece, 0.0) for one in live], axis=0).astype(BF16)
        result.append(dot(spread, left[p]))
    result = jnp.concatenate(result, axis=0)
    for p in range(2):
        for e in range(ex_dev):
            at = (p * ex_dev + e) * k2
            for q in range(n_proj):
                rows[at:at + k2, q * kc:(q + 1) * kc] = result[at:at + k2, q * kc:(q + 1) * kc] * scale[e]
    for q in range(n_proj):
        t_send[q] = rows[:, q * kc:(q + 1) * kc].astype(BF16)
    shares = [swap(k, t_send.at[peer(k)], t_in, ts_sem, tr_sem) for k in range(1, n_proj)]
    across = [pass_on(k, t_send.at[peer(k)], t_mate, us_sem, ur_sem) for k in range(n_proj)]

    @pl.when(flank == 1)
    def _():
        for share in (across[2], across[1], across[3], across[0]):
            share.start()

    for share in shares:
        share.start()

    @pl.when(flank == 0)
    def _():
        pl.semaphore_wait(met, n_proj)
        for share in across:
            share.start()

    l_at = lax.broadcasted_iota(jnp.int32, (128, kc), 0)
    k_at = lax.broadcasted_iota(jnp.int32, (128, kc), 1)
    keep = (k_at % reps) == (l_at // pd)
    b_at = lax.broadcasted_iota(jnp.int32, (picks, kc), 0)
    s_at = lax.broadcasted_iota(jnp.int32, (picks, kc), 1)
    pick = jnp.where((s_at // reps) == b_at, 1.0, 0.0).astype(BF16)

    for jj in range(per):
        @pl.when(flank * per + jj == me_ex)
        def _():
            own.wait()

        @pl.when(flank * per + jj != me_ex)
        def _():
            take(jj).wait_recv()
    acc = jnp.zeros((per * v_rows, 128), F32)
    for c in range(v_ref.shape[1] // 128):
        wide = held[:, c * 128:(c + 1) * 128].astype(F32)
        acc = acc + wide * wide
    val_sq = lax.dot_general(
        jnp.ones((ep, 128), F32), acc, NT, precision=lax.Precision.HIGHEST, preferred_element_type=F32
    )

    def score(w, block):
        block = block.astype(BF16).astype(F32)
        for e in range(ex_dev):
            one = [block[(p * ex_dev + e) * k2:(p * ex_dev + e + 1) * k2] for p in range(2)]
            tiled = jnp.where(keep, jnp.concatenate(one * reps, axis=0), 0.0)
            shuf[w, e * 128:(e + 1) * 128, :] = tiled.astype(BF16)
        spread = dot(pick, shuf[w], NT)
        for e in range(ex_dev):
            flat[w, pl.ds(e, picks, stride=ep), :] = spread[:, e * 128:(e + 1) * 128]
        tiles = [flat[w, b * ep:(b + 1) * ep, :] for b in range(picks)]
        train_sq = jnp.zeros((ep, 128), F32)
        for tile in tiles:
            train_sq = train_sq + tile * tile
        train_sq = jnp.sum(train_sq, axis=1, keepdims=True)
        train = jnp.concatenate(tiles, axis=1)
        dots = dot(train.astype(BF16), held[...], NT)
        for jj in range(per):
            span = slice(jj * v_rows, (jj + 1) * v_rows)
            f_send[w, jj] = jnp.concatenate(
                [dots[:, span], val_sq[:, span], jnp.broadcast_to(train_sq, (ep, 128 - 2 * v_rows))],
                axis=1,
            )
        return train

    def report(w, jj):
        return pltpu.make_async_remote_copy(
            src_ref=f_send.at[w, jj], dst_ref=f_recv.at[me], send_sem=fs_sem.at[w, jj], recv_sem=fr_sem.at[me],
            device_id=(grp, mate if w else me_ex, flank * per + jj), device_id_type=MESH,
        )

    def hear(q):
        return pltpu.make_async_remote_copy(
            src_ref=f_recv.at[q], dst_ref=f_recv.at[q], send_sem=fs_sem.at[0, 0], recv_sem=fr_sem.at[q],
            device_id=(grp, me_ex, me), device_id_type=MESH,
        )

    def own_stage():
        block = rows[:, pl.ds(pl.multiple_of(me * kc, 128), kc)]
        for k, share in enumerate(shares):
            share.wait_recv()
            block = block + t_in[k].astype(F32)
        train = score(0, block)
        for jj in range(per):
            @pl.when(me != flank * per + jj)
            def _():
                report(0, jj).start()

            @pl.when(me == flank * per + jj)
            def _():
                f_recv[me] = f_send[0, jj]
        tp_ref[...] = train

    def mate_stage():
        block = jnp.zeros((ex_dev * pd, kc), F32)
        for k, share in enumerate(across):
            share.wait_recv()
            block = block + t_mate[k].astype(F32)
        score(1, block)
        for jj in range(per):
            report(1, jj).start()

    @pl.when(flank == 0)
    def _():
        own_stage()
        mate_stage()

    @pl.when(flank == 1)
    def _():
        mate_stage()
        own_stage()

    for move in moves[0] + moves[1] + shares + across:
        move.wait_send()
    for i in range(n_ex):
        @pl.when((i != me_ex) & (i % 2 == home))
        def _():
            give(i).wait_send()
    for q in range(n_proj):
        @pl.when((me // per != flank) | (me != q))
        def _():
            hear(q).wait_recv()
    final = f_recv[0]
    for q in range(1, n_proj):
        final = final + f_recv[q]
    sc_ref[...] = final
    for jj in range(per):
        @pl.when(me != flank * per + jj)
        def _():
            report(0, jj).wait_send()

        report(1, jj).wait_send()


def paired_finish(pdim, train_ref, sums_ref, tp_ref, sc_ref):
    ex_dev, cs = sc_ref.shape
    tp_ref[...] = train_ref[:ex_dev, :].astype(BF16)
    final = sums_ref[:ex_dev, :]
    sc_ref[...] = (
        math.sqrt(pdim)
        * final[:, :cs]
        * lax.rsqrt(final[:, 2 * cs:3 * cs] + epsilon)
        * lax.rsqrt(final[:, cs:2 * cs] + epsilon)
    )


def finish(pdim, train_ref, sums_ref, tp_ref, sc_ref):
    ex_dev = tp_ref.shape[0]
    ep = train_ref.shape[0]
    tp_ref[...] = train_ref[:ex_dev, :].astype(BF16)
    final = sums_ref[...]
    scores = (
        math.sqrt(pdim)
        * final[:ep]
        * lax.rsqrt(final[ep + 8:] + epsilon)
        * lax.rsqrt(final[ep:ep + 1] + epsilon)
    )
    sc_ref[...] = scores[:ex_dev]


def shards(
    mesh, inputs, cotangents, lengths, adapter_down_matrix, adapter_up_matrix,
    width_side_sketch, rank_side_sketch, heldout_gradient_rows,
):
    n_ex, n_proj = mesh.shape["ex"], mesh.shape["proj"]
    ex_dev, seq, cols = inputs.shape
    tokens = ex_dev * seq
    rank = adapter_down_matrix.shape[0]
    k1 = width_side_sketch.shape[1]
    k2 = rank_side_sketch.shape[2]
    pd = 2 * k2
    kc = k1 // n_proj
    v_rows, v_cols = heldout_gradient_rows.shape
    nv = v_rows * n_ex
    cs = nv // n_proj
    ep = -(-ex_dev // 8) * 8
    pdim = pd * k1
    any_space = pl.BlockSpec(memory_space=pltpu.HBM)
    vmem = pl.BlockSpec(memory_space=pltpu.VMEM)
    dma = pltpu.SemaphoreType.DMA
    peers = n_proj - 1
    per = n_ex // 2
    paired = (
        n_ex == n_proj and n_ex % 2 == 0 and kc == 128 and 3 * v_rows <= 128 and v_rows % 16 == 0
        and k2 % 8 == 0 and v_cols == kc * pd
    )
    head = [
        pltpu.VMEM((tokens, cols), BF16),
        pltpu.VMEM((tokens, cols), BF16),
        pltpu.VMEM((rank, cols), BF16),
        pltpu.VMEM((cols, rank), BF16),
        pltpu.VMEM((cols, k1), BF16),
    ]
    if paired:
        body, end = paired_kernel, paired_finish
        sums_shape = (ep, 128)
        picks = kc * pd // 128
        firsts = [any_space] * 8
        scratch = head + [
            pltpu.VMEM((2, k2, rank), BF16),
            pltpu.SMEM((ex_dev,), jnp.int32),
            pltpu.VMEM((per * v_rows, v_cols), BF16),
            pltpu.VMEM((2, tokens, k1), BF16),
            pltpu.VMEM((ex_dev * pd, k1), F32),
            pltpu.VMEM((2, k2, tokens), BF16),
            pltpu.VMEM((2, peers, k2, tokens), BF16),
            pltpu.VMEM((n_proj, ex_dev * pd, kc), BF16),
            pltpu.VMEM((peers, ex_dev * pd, kc), BF16),
            pltpu.VMEM((n_proj, ex_dev * pd, kc), BF16),
            pltpu.VMEM((2, ex_dev * 128, kc), BF16),
            pltpu.VMEM((2, picks * ep, 128), F32),
            pltpu.VMEM((2, per, ep, 128), F32),
            pltpu.VMEM((n_proj, ep, 128), F32),
            dma((7,)),
            dma((2, peers)), dma((2, peers)),
            dma((peers,)), dma((peers,)),
            dma((n_proj,)), dma((n_proj,)),
            dma((n_ex,)), dma((per,)),
            dma((2, per)), dma((n_proj,)),
            dma,
            pltpu.SemaphoreType.REGULAR((n_ex,)),
            pltpu.SemaphoreType.REGULAR,
            pltpu.SemaphoreType.REGULAR,
        ]
    else:
        firsts = [pl.BlockSpec(memory_space=pltpu.SMEM)] + [any_space] * 5 + [vmem, any_space]
        chunks = 2 if v_rows % 32 == 0 else 1
        body, end = kernel, finish
        sums_shape = (2 * ep + 8, cs)
        scratch = head + [
            pltpu.VMEM((ex_dev * pd, k1), F32),
            pltpu.VMEM((2, tokens, k1), BF16),
            pltpu.VMEM((n_ex, v_rows, v_cols), BF16),
            pltpu.VMEM((pd, tokens), BF16),
            pltpu.VMEM((peers, pd, tokens), BF16),
            pltpu.VMEM((n_proj, ex_dev * pd, kc), BF16),
            pltpu.VMEM((peers, ex_dev * pd, kc), BF16),
            pltpu.VMEM((ex_dev * 128, kc), BF16),
            pltpu.VMEM((ep, v_cols), F32),
            pltpu.VMEM((nv, 128), F32),
            pltpu.VMEM((n_proj, 2 * ep + 8, cs), F32),
            pltpu.VMEM((peers, 2 * ep + 8, cs), F32),
            dma((5,)),
            dma((peers,)), dma((peers,)),
            dma((peers,)), dma((peers,)),
            dma((peers,)), dma((peers,)),
            dma((2, n_ex - 1, chunks)), dma((2, n_ex - 1, chunks)),
            dma,
        ]
    train, final = pl.pallas_call(
        functools.partial(body, (n_ex, n_proj, ex_dev, seq, pdim)),
        out_shape=(
            pltpu.VMEM((ep, v_cols), F32),
            pltpu.VMEM(sums_shape, F32),
        ),
        in_specs=firsts,
        out_specs=(vmem, vmem),
        scratch_shapes=scratch,
        compiler_params=pltpu.CompilerParams(
            collective_id=0, has_side_effects=True, vmem_limit_bytes=62 * 1024 * 1024
        ),
        name="project",
    )(
        lengths, inputs.reshape(tokens, cols), cotangents.reshape(tokens, cols),
        adapter_down_matrix, adapter_up_matrix, width_side_sketch,
        rank_side_sketch.swapaxes(1, 2), heldout_gradient_rows,
    )
    return pl.pallas_call(
        functools.partial(end, pdim),
        out_shape=(
            jax.ShapeDtypeStruct((ex_dev, v_cols), BF16),
            jax.ShapeDtypeStruct((ex_dev, cs), F32),
        ),
        in_specs=[vmem, vmem],
        out_specs=(vmem, vmem),
        compiler_params=pltpu.CompilerParams(vmem_limit_bytes=8 * 1024 * 1024),
        name="finish",
    )(train, final)


def solution(mesh):
    in_specs = (
        P(("grp", "ex"), None, "proj"),
        P(("grp", "ex"), None, "proj"),
        P(("grp", "ex")),
        P(None, "proj"),
        P("proj", None),
        P("proj", None),
        P(),
        P(("grp", "ex"), "proj"),
    )
    out_specs = (P(("grp", "ex"), "proj"), P(("grp", "ex"), "proj"))
    return jax.shard_map(
        functools.partial(shards, mesh), mesh=mesh, in_specs=in_specs, out_specs=out_specs, check_vma=False
    )
```
